32 devices in a mesh: gx: 2 (over x), gy: 4 (over y, core), gz: 4 (over z).
Axes of the slice: x: 2, y: 2, z: 4, core: 2. Of those that a mesh axis runs over, the one named last changes fastest.
Arguments:
- right_side: float32 [32, 64, 1024], P('gx', 'gy', 'gz'), may hold values from -5 to 5
- coefficients: float32 [4, 32, 64, 1024], P(None, 'gx', 'gy', 'gz'), may hold values from 0.1 to 32
- first_guess: float32 [32, 64, 1024], P('gx', 'gy', 'gz'), may hold values from -3 to 3
Outputs:
- solution_field: float32 [32, 64, 1024], P('gx', 'gy', 'gz')
The draws below stay inside these ranges and needn't reach their ends.
All inputs are finite; a program needn't handle non-finite values.
Results may differ from the reference program's by a relative error of at most 0.00002.
Values sent between devices are 32-bit elements; how exact they have to be, the bound alone decides.
A program may use at most 128 MiB of HBM per device.

```python
import jax
import jax.numpy as jnp
from jax import lax

CYCLES = 2
SWEEPS = 8
NX = 32
NY = 64
NZ = 1024


slab_width = 64


def draw_coefficients(key, part):
    first_pos = jnp.arange(NX, dtype=jnp.int32)[:, None, None]
    second_pos = jnp.arange(NY, dtype=jnp.int32)[None, :, None]
    third_pos = jnp.arange(NZ, dtype=jnp.int32)[None, None, :]
    slab_number = (first_pos + second_pos + third_pos) // slab_width % 3
    members = jnp.arange(3, dtype=jnp.int32)[:, None, None, None]
    strong = slab_number[None] == members
    diffusion_low = jnp.where(strong, jnp.float32(16.0), jnp.float32(0.15))
    diffusion_high = jnp.where(strong, jnp.float32(32.0), jnp.float32(0.3))
    reaction_low = jnp.full((1, NX, NY, NZ), 0.1, jnp.float32)
    reaction_high = jnp.full((1, NX, NY, NZ), 1.0, jnp.float32)
    lowest = jnp.concatenate([diffusion_low, reaction_low], 0)
    highest = jnp.concatenate([diffusion_high, reaction_high], 0)
    uniform_draw = jax.random.uniform(jax.random.fold_in(key, 11), (4, NX, NY, NZ), jnp.float32)
    return lowest * jnp.exp(uniform_draw * jnp.log(highest / lowest))


def draw_right_side(key, part):
    noise = jax.random.normal(jax.random.fold_in(key, 23), (NX, NY, NZ), jnp.float32)
    return jnp.clip(noise, -5.0, 5.0)


def steps_of(key, extent, shards, low, top_value):
    factor_of, own = 1.0, jax.random.fold_in(key, 6)
    for position, shards_of in shards:
        draws = jnp.exp(jax.random.uniform(jax.random.fold_in(own, position), (shards_of,), jnp.float32, low / len(shards), top_value / len(shards)))
        factor_of = factor_of * jnp.repeat(draws, extent[position] // shards_of).reshape([-1 if axis == position else 1 for axis in range(len(extent))])
    return factor_of


def scatter_about(stream_key, dims, width, reach, pieces=(), held_as=jnp.bfloat16):
    values = jax.random.normal(stream_key, dims, jnp.float32) * width
    if len(pieces) > 0:
        values = steps_of(stream_key, dims, pieces, -0.22, 0.18) * values
    return jnp.clip(values, min=-reach, max=reach).astype(held_as)


def setup_inputs(seed: int = 0) -> dict:
    streams_of = jax.random.split(jax.random.key(seed), 4)
    right_side = draw_right_side(jax.random.fold_in(streams_of[3], 71), 0)
    coefficients = draw_coefficients(jax.random.fold_in(streams_of[3], 71), 0)
    first_guess = scatter_about(streams_of[2], (NX, NY, NZ), 0.5, 3.0, ((0, 2), (1, 4), (2, 4)), jnp.float32)
    return {"right_side": right_side, "coefficients": coefficients, "first_guess": first_guess}


relaxation = 0.8
blending = 0.4


def pad_along(values, direction):
    widths = [(0, 0)] * values.ndim
    widths[direction] = (1, 1)
    return jnp.pad(values, widths)


def neighbours(values, direction):
    length = values.shape[direction]
    padded = pad_along(values, direction)
    upper_cells = lax.slice_in_dim(padded, 2, length + 2, axis=direction)
    lower_cells = lax.slice_in_dim(padded, 0, length, axis=direction)
    return upper_cells, lower_cells


def face_weights(fields):
    diagonal = fields[3]
    weights = []
    for direction in range(3):
        upper_cells, lower_cells = neighbours(fields[direction], direction)
        weight_high = 0.5 * (fields[direction] + upper_cells)
        weight_low = 0.5 * (fields[direction] + lower_cells)
        weights.append((weight_high, weight_low))
        diagonal = diagonal + weight_high + weight_low
    return weights, diagonal


def operate(values, reaction, weights):
    result = reaction * values
    for direction in range(3):
        weight_high, weight_low = weights[direction]
        upper_cells, lower_cells = neighbours(values, direction)
        result = result + (weight_high * (values - upper_cells) + weight_low * (values - lower_cells))
    return result


def pair_mean(values, direction):
    shape = values.shape
    split_shape = shape[:direction] + (shape[direction] // 2, 2) + shape[direction + 1:]
    paired = values.reshape(split_shape)
    even_cells = lax.index_in_dim(paired, 0, direction + 1, keepdims=False)
    odd_cells = lax.index_in_dim(paired, 1, direction + 1, keepdims=False)
    return 0.5 * (even_cells + odd_cells)


def coarse_fields(fields, direction):
    averaged = pair_mean(fields, direction + 1)
    factors = [1.0, 1.0, 1.0, 1.0]
    factors[direction] = 0.25
    return jnp.stack([averaged[member] * factors[member] for member in range(4)])


def prolong_padded(padded, direction):
    length = padded.shape[direction] - 2
    middle = lax.slice_in_dim(padded, 1, length + 1, axis=direction)
    upper_cells = lax.slice_in_dim(padded, 2, length + 2, axis=direction)
    lower_cells = lax.slice_in_dim(padded, 0, length, axis=direction)
    even_cells = 0.75 * middle + 0.25 * lower_cells
    odd_cells = 0.75 * middle + 0.25 * upper_cells
    joined = jnp.stack([even_cells, odd_cells], direction + 1)
    new_shape = list(middle.shape)
    new_shape[direction] = 2 * length
    return joined.reshape(new_shape)


def reference(right_side, coefficients, first_guess):
    weights, diagonal = face_weights(coefficients)
    branches = []
    for direction in range(3):
        coarse = coarse_fields(coefficients, direction)
        coarse_weights, coarse_diagonal = face_weights(coarse)
        branches.append((coarse[3], coarse_weights, coarse_diagonal))
    solution_field = first_guess
    for cycle_index in range(CYCLES):
        residual = right_side - operate(solution_field, coefficients[3], weights)
        update = None
        for direction in range(3):
            coarse_reaction, coarse_weights, coarse_diagonal = branches[direction]
            coarse_residual = pair_mean(residual, direction)
            errors = jnp.zeros_like(coarse_residual)
            for repeat in range(SWEEPS):
                errors = errors + relaxation * (coarse_residual - operate(errors, coarse_reaction, coarse_weights)) / coarse_diagonal
            correction = prolong_padded(pad_along(errors, direction), direction)
            update = correction if update is None else update + correction
        solution_field = solution_field + blending * update
    return solution_field
```

```python
import functools

import jax
import jax.numpy as jnp
from jax import lax
from jax.experimental import pallas as pl
from jax.experimental.pallas import tpu as pltpu
from jax.sharding import PartitionSpec as P

CYCLES = 2
SWEEPS = 8
REACH = 2 * (SWEEPS + 1)
STEP = 20
LANES = 128
CHUNK = 1

relaxation = 0.8
blending = 0.4
MESH = pl.DeviceIdType.MESH


def iota(shape, dim):
    return lax.broadcasted_iota(jnp.int32, shape, dim)


def spread(a, b):
    total = None
    for _ in range(3):
        part = a.astype(jnp.bfloat16)
        a = a - part.astype(jnp.float32)
        term = jnp.dot(part, b, preferred_element_type=jnp.float32)
        total = term if total is None else total + term
    return total


def kernel(sizes, names, b_ref, k_ref, g_ref, out_ref, *scratch):
    (fields, cells, tiles, es, yss, yrs, ms, fs, kxr, kys, kyr, zs, zr, us, ur,
     send, recv, ksend, krecv, zsend, zrecv) = scratch
    nx, ny, nz = sizes
    wide = nz + LANES
    shapes = ((nx // 2, ny, wide), (nx, ny // 2, wide), (nx, ny, nz // 2 + LANES), (nx, ny, wide))
    place = [lax.axis_index(n) for n in names]
    counts = [lax.axis_size(n) for n in names]
    has_low = [p > 0 for p in place]
    has_high = [p < c - 1 for p, c in zip(place, counts)]
    ways = []
    for axis in range(3):
        ways.append((axis, -1, has_low[axis], has_high[axis]))
        ways.append((axis, 1, has_high[axis], has_low[axis]))

    def target(way):
        axis, step = ways[way][:2]
        return {names[axis]: place[axis] + step}

    def copy(src, dst, ssem, rsem, way):
        return pltpu.make_async_remote_copy(
            src_ref=src, dst_ref=dst, send_sem=ssem, recv_sem=rsem,
            device_id=target(way), device_id_type=MESH,
        )

    def start(copies):
        for way, c in copies:
            @pl.when(ways[way][2])
            def _():
                c.start()

    def finish(copies):
        for way, c in copies:
            @pl.when(ways[way][3])
            def _():
                c.wait_recv()
        for way, c in copies:
            @pl.when(ways[way][2])
            def _():
                c.wait_send()

    def faces(g, slot, keep=(0, 1, 2, 3)):
        x = shapes[g][0]
        e, ys, yr = es[g], yss[g], yrs[g]
        ends = (
            (e.at[slot, 1], e.at[slot, x + 1]),
            (e.at[slot, x], e.at[slot, 0]),
            (ys.at[slot, 0], yr.at[slot, 1]),
            (ys.at[slot, 1], yr.at[slot, 0]),
        )
        return [
            (way, copy(*ends[way], send.at[g, way, slot], recv.at[g, way, slot], way)) for way in keep
        ]

    for g in range(4):
        x = shapes[g][0]
        for slot in range(2):
            zero = jnp.zeros(shapes[g][1:], jnp.float32)
            es[g][slot, 0] = zero
            es[g][slot, x + 1] = zero
        yrs[g][...] = jnp.zeros(yrs[g].shape, jnp.float32)
    kxr[...] = jnp.zeros(kxr.shape, jnp.float32)
    kyr[...] = jnp.zeros(kyr.shape, jnp.float32)
    zr[...] = jnp.zeros(zr.shape, jnp.float32)
    ur[...] = jnp.zeros(ur.shape, jnp.float32)

    barrier = pltpu.get_barrier_semaphore()
    for way in range(6):
        @pl.when(ways[way][2])
        def _():
            pl.semaphore_signal(barrier, inc=1, device_id=target(way), device_id_type=MESH)
    peers = sum(jnp.where(has, 1, 0) for has in has_low + has_high)
    pl.semaphore_wait(barrier, peers)

    lane = iota((nx, ny, LANES), 2)
    low = jnp.zeros((nx, ny, LANES), jnp.float32)
    high = low
    for j in range(6):
        if j < 4:
            first, last = k_ref[j, :, :, :LANES], k_ref[j, :, :, nz - LANES:]
        elif j == 4:
            first, last = g_ref[:, :, :LANES], g_ref[:, :, nz - LANES:]
        else:
            first, last = b_ref[:, :, :LANES], b_ref[:, :, nz - LANES:]
        here = (lane >= STEP * j) & (lane < STEP * j + REACH)
        low = jnp.where(here, pltpu.roll(first, STEP * j, 2) if j else first, low)
        high = jnp.where(here, pltpu.roll(last, (STEP * j + REACH) % LANES, 2), high)
    zs[0] = low
    zs[1] = high
    deep = [
        (4, copy(zs.at[0], zr.at[1], zsend.at[0], zrecv.at[0], 4)),
        (5, copy(zs.at[1], zr.at[0], zsend.at[1], zrecv.at[1], 5)),
    ]
    start(deep)
    for j in range(4):
        fields[j, :, :, :nz] = k_ref[j]
    fields[4, :, :, :nz] = b_ref[...]
    es[3][0, 1:nx + 1, :, :nz] = g_ref[...]
    finish(deep)
    above, below = zr[1], zr[0]

    def beside(j):
        up = pltpu.roll(above, (LANES - STEP * j) % LANES, 2) if j else above
        down = pltpu.roll(below, (2 * LANES - REACH - STEP * j) % LANES, 2)
        return jnp.where(lane < REACH, up, jnp.where(lane >= LANES - REACH, down, 0.0))

    for j in range(4):
        fields[j, :, :, nz:] = beside(j)
    es[3][0, 1:nx + 1, :, nz:] = beside(4)
    fields[4, :, :, nz:] = beside(5)

    def send_guess(slot):
        u = es[3][slot, 1:nx + 1]
        yss[3][slot, 0] = u[:, 0:1, :]
        yss[3][slot, 1] = u[:, ny - 1:ny, :]
        start(faces(3, slot))

    ky = fields[1]
    for row in range(2):
        kys[0, row] = ky[:, row:row + 1, :]
        kys[1, row] = ky[:, ny - 2 + row:ny - 1 + row, :]
    edges = [
        (0, copy(fields.at[0, pl.ds(0, 2)], kxr.at[1], ksend.at[0], krecv.at[0], 0)),
        (1, copy(fields.at[0, pl.ds(nx - 2, 2)], kxr.at[0], ksend.at[1], krecv.at[1], 1)),
        (2, copy(kys.at[0], kyr.at[1], ksend.at[2], krecv.at[2], 2)),
        (3, copy(kys.at[1], kyr.at[0], ksend.at[3], krecv.at[3], 3)),
    ]
    start(edges)
    send_guess(0)

    half = nz // 2
    r, c = iota((wide, half + LANES), 0), iota((wide, half + LANES), 1)
    home = jnp.where(
        r < nz, r // 2,
        jnp.where(r < nz + LANES // 2, half + (r - nz) // 2, half + LANES // 2 + (r - nz) // 2),
    )
    z_mean = jnp.where(home == c, 0.5, 0.0).astype(jnp.bfloat16)
    rows = nx * ny
    r, c = iota((half + LANES, nz), 0), iota((half + LANES, nz), 1)
    main = c // 2
    total = half + LANES
    side = jnp.where(c % 2 == 1, main + 1, jnp.where(main == 0, total - 1, main - 1))
    z_spread = (jnp.where(r == main, 0.75, 0.0) + jnp.where(r == side, 0.25, 0.0)).astype(jnp.bfloat16)

    count = wide // LANES
    even_rows, odd_rows = pl.ds(0, ny // 2, stride=2), pl.ds(1, ny // 2, stride=2)

    def put_tiles(planes, values):
        for t in range(values.shape[2] // LANES):
            tiles[t, planes] = values[:, :, LANES * t:LANES * (t + 1)]

    def get_tiles(planes, tiles_of=count):
        return jnp.concatenate([tiles[t, planes] for t in range(tiles_of)], 2)

    def y_mean(planes):
        return jnp.concatenate(
            [0.5 * (tiles[t, planes, even_rows] + tiles[t, planes, odd_rows]) for t in range(count)], 2)

    def chunks(x, step=CHUNK):
        return [slice(x0, x0 + step) for x0 in range(0, x, step)]

    def below_of(ref, planes, halo):
        if planes.start > 0:
            return ref[planes.start - 1:planes.stop - 1]
        return halo if planes.stop == 1 else jnp.concatenate([halo, ref[0:planes.stop - 1]], 0)

    def above_of(ref, planes, halo):
        if planes.stop < ref.shape[0]:
            return ref[planes.start + 1:planes.stop + 1]
        if planes.stop == planes.start + 1:
            return halo
        return jnp.concatenate([ref[planes.start + 1:planes.stop], halo], 0)

    def y_shift(values, halo_low, halo_high):
        y = values.shape[1]
        row = iota(values.shape, 1)
        lower = jnp.where(row == 0, halo_low, pltpu.roll(values, 1, 1))
        upper = jnp.where(row == y - 1, halo_high, pltpu.roll(values, y - 1, 1))
        return lower, upper

    def z_shift(values):
        return pltpu.roll(values, 1, 2), pltpu.roll(values, values.shape[2] - 1, 2)

    def face_weights(k, planes, near_x, near_y):
        k0, k1, k2 = k.at[0], k.at[1], k.at[2]
        m1, m2 = k1[planes], k2[planes]
        groups = (
            (k0[planes], (below_of(k0, planes, near_x[0]), above_of(k0, planes, near_x[1]))),
            (m1, y_shift(m1, near_y[0](planes), near_y[1](planes))),
            (m2, z_shift(m2)),
        )
        found = []
        total = k[3, planes]
        for middle, pair in groups:
            for other in pair:
                found.append(0.5 * (middle + other))
                total = total + found[-1]
        return found, total

    for j in range(4):
        for d in range(2):
            factor = 0.25 if j == d else 1.0
            if d == 0:
                for i in range(nx // 2):
                    cells[0][j, i] = (0.5 * factor) * (fields[j, 2 * i] + fields[j, 2 * i + 1])
            else:
                for planes in chunks(nx):
                    put_tiles(planes, fields[j, planes])
                for planes in chunks(nx):
                    cells[1][j, planes] = y_mean(planes) * factor
    for j in range(4):
        factor = 0.25 if j == 2 else 1.0
        for planes in chunks(nx, nx // 2):
            flat = fields[j, planes].reshape((rows // 2, wide))
            cells[2][j, planes] = (spread(flat, z_mean) * factor).reshape((nx // 2,) + shapes[2][1:])
    finish(edges)
    near_rows = [kxr[0, 1], kxr[1, 0]] + [kyr[0, 1].reshape((nx, wide)), kyr[1, 0].reshape((nx, wide))]
    edge = spread(jnp.concatenate(near_rows, 0), z_mean)
    edge_x = [edge[0:ny][None], edge[ny:2 * ny][None]]
    edge_y = [edge[2 * ny + nx * side:2 * ny + nx * (side + 1)].reshape((nx, 1, half + LANES)) for side in range(2)]
    put_tiles(slice(0, 2), jnp.stack([kxr[0, 1], kxr[1, 0]]))
    pair = y_mean(slice(0, 2))

    near_xs = (
        [0.125 * (kxr[side, 0:1] + kxr[side, 1:2]) for side in range(2)],
        [pair[0:1], pair[1:2]],
        edge_x,
    )

    def y_face(d, side):
        nearest = kyr.at[side, 1 - side]
        if d == 0:
            return lambda planes: jnp.concatenate(
                [0.5 * (nearest[2 * i:2 * i + 1] + nearest[2 * i + 1:2 * i + 2])
                 for i in range(planes.start, planes.stop)], 0)
        if d == 1:
            return lambda planes: 0.125 * (kyr[side, 0, planes] + kyr[side, 1, planes])
        if d == 2:
            return lambda planes: edge_y[side][planes]
        return lambda planes: nearest[planes]

    for d in range(3):
        for planes in chunks(shapes[d][0]):
            w, total_coarse = face_weights(
                cells[d], planes, near_xs[d], (y_face(d, 0), y_face(d, 1)))
            inside = cells[d][3, planes] > 0.0
            scale = jnp.where(inside, relaxation / jnp.where(inside, total_coarse, 1.0), 0.0)
            ms[d][6, planes] = scale
            for j in range(6):
                ms[d][j, planes] = w[j] * scale

    def sweep(g, slot, new_slot, keep=(0, 1, 2, 3)):
        e, yr, ys, m, f = es[g], yrs[g], yss[g], ms[g], fs[g]
        x, y, z = shapes[g]
        order = list(range(0, x, CHUNK))
        order = order[:1] + order[-1:] + order[1:-1]
        for x0 in order:
            planes = slice(x0, x0 + CHUNK)
            middle = e[slot, x0 + 1:x0 + 1 + CHUNK]
            y_low, y_high = y_shift(middle, yr[slot, 0, planes], yr[slot, 1, planes])
            z_low, z_high = z_shift(middle)
            new = (1.0 - relaxation) * middle + f[planes]
            new = new + m[0, planes] * e[slot, x0:x0 + CHUNK]
            new = new + m[1, planes] * e[slot, x0 + 2:x0 + 2 + CHUNK]
            new = new + m[2, planes] * y_low
            new = new + m[3, planes] * y_high
            new = new + m[4, planes] * z_low
            new = new + m[5, planes] * z_high
            e[new_slot, x0 + 1:x0 + 1 + CHUNK] = new
            ys[new_slot, 0, planes] = new[:, 0:1]
            ys[new_slot, 1, planes] = new[:, y - 1:y]
            if x0 == order[1] and 0 in keep:
                start(faces(g, new_slot, (0, 1)))
        if 2 in keep:
            start(faces(g, new_slot, (2, 3)))

    for cycle in range(CYCLES):
        slot = cycle % 2
        finish(faces(3, slot))
        u = es[3]
        for planes in chunks(nx):
            x0, x1 = planes.start, planes.stop
            middle = u[slot, x0 + 1:x1 + 1]
            y_low, y_high = y_shift(middle, yrs[3][slot, 0, planes], yrs[3][slot, 1, planes])
            z_low, z_high = z_shift(middle)
            w, total_fine = face_weights(
                fields, planes, (kxr[0, 1:2], kxr[1, 0:1]), (y_face(3, 0), y_face(3, 1)))
            residual = fields[4, planes] - total_fine * middle
            around = (u[slot, x0:x1], u[slot, x0 + 2:x1 + 2], y_low, y_high, z_low, z_high)
            for j in range(6):
                residual = residual + w[j] * around[j]
            put_tiles(planes, residual)
        for g in range(3):
            x, y, z = shapes[g]
            if g == 2:
                flat = get_tiles(slice(0, nx)).reshape((rows, wide))
                whole = spread(flat, z_mean).reshape(shapes[2])
            for planes in chunks(x):
                if g == 0:
                    pairs = [get_tiles(slice(2 * i, 2 * i + 2)) for i in range(planes.start, planes.stop)]
                    first = jnp.concatenate([0.5 * (p[0:1] + p[1:2]) for p in pairs], 0)
                elif g == 1:
                    first = y_mean(planes)
                else:
                    first = whole[planes]
                first = ms[g][6, planes] * first
                fs[g][planes] = first
                es[g][1, planes.start + 1:planes.stop + 1] = first
                yss[g][1, 0, planes] = first[:, 0:1]
                yss[g][1, 1, planes] = first[:, y - 1:y]
            start(faces(g, 1))

        @pl.loop(1, SWEEPS - 1)
        def _(repeat):
            old = lax.rem(repeat, 2)
            for g in range(3):
                finish(faces(g, old))
                sweep(g, old, 1 - old)

        last = SWEEPS % 2
        needed = ((0, 1), (2, 3), ())
        for g in range(3):
            finish(faces(g, 1 - last))
            sweep(g, 1 - last, last, needed[g])
        e = es[2][last, 1:nx + 1].reshape((rows, half + LANES))
        from_z = spread(e, z_spread).reshape((nx, ny, nz))
        finish(faces(1, last, needed[1]))
        for planes in chunks(nx):
            e = es[1][last, planes.start + 1:planes.stop + 1, :, :nz]
            y_low, y_high = y_shift(
                e, yrs[1][last, 0, planes, :, :nz], yrs[1][last, 1, planes, :, :nz])
            even = 0.75 * e + 0.25 * y_low
            odd = 0.75 * e + 0.25 * y_high
            for t in range(nz // LANES):
                tiles[t, planes, even_rows] = even[:, :, LANES * t:LANES * (t + 1)]
                tiles[t, planes, odd_rows] = odd[:, :, LANES * t:LANES * (t + 1)]
        finish(faces(0, last, needed[0]))
        for i in range(nx // 2):
            planes = slice(2 * i, 2 * i + 2)
            e = es[0][last, i:i + 3, :, :nz]
            even = 0.75 * e[1:2] + 0.25 * e[0:1]
            odd = 0.75 * e[1:2] + 0.25 * e[2:3]
            update = (jnp.concatenate([even, odd], 0) + get_tiles(planes, nz // LANES)) + from_z[planes]
            final = es[3][slot, 2 * i + 1:2 * i + 3, :, :nz] + blending * update
            if cycle == CYCLES - 1:
                out_ref[planes] = final
            else:
                es[3][1 - slot, 2 * i + 1:2 * i + 3, :, :nz] = final
        if cycle == CYCLES - 1:
            continue
        result = es[3].at[1 - slot, 1:nx + 1]
        per = LANES // STEP
        plane_lane = iota((ny, LANES), 1)
        groups = us.shape[1]
        for q in range(groups):
            low = jnp.zeros((ny, LANES), jnp.float32)
            high = low
            for p in range(min(per, nx - q * per)):
                here = (plane_lane >= STEP * p) & (plane_lane < STEP * p + REACH)
                first = result[q * per + p, :, :LANES]
                low = jnp.where(here, pltpu.roll(first, STEP * p, 1) if p else first, low)
                high = jnp.where(
                    here, pltpu.roll(result[q * per + p, :, nz - LANES:nz], (STEP * p + REACH) % LANES, 1), high)
            us[0, q] = low
            us[1, q] = high
        again = [
            (4, copy(us.at[0], ur.at[1], zsend.at[2], zrecv.at[2], 4)),
            (5, copy(us.at[1], ur.at[0], zsend.at[3], zrecv.at[3], 5)),
        ]
        start(again)
        finish(again)
        for i in range(nx):
            q, p = i // per, i % per
            up = pltpu.roll(ur[1, q], (LANES - STEP * p) % LANES, 1) if p else ur[1, q]
            down = pltpu.roll(ur[0, q], (2 * LANES - REACH - STEP * p) % LANES, 1)
            es[3][1 - slot, i + 1, :, nz:] = jnp.where(
                plane_lane < REACH, up, jnp.where(plane_lane >= LANES - REACH, down, 0.0))
        send_guess(1 - slot)


def body(names, right_side, coefficients, first_guess):
    nx, ny, nz = right_side.shape
    wide = nz + LANES
    shapes = ((nx // 2, ny, wide), (nx, ny // 2, wide), (nx, ny, nz // 2 + LANES), (nx, ny, wide))
    f32 = jnp.float32
    vmem = lambda *shape: pltpu.VMEM(shape, f32)
    dma = pltpu.SemaphoreType.DMA
    groups = -(-nx // (LANES // STEP))
    scratch = [
        vmem(5, nx, ny, wide),
        tuple(vmem(4, x, y, z) for x, y, z in shapes[:3]),
        vmem(wide // LANES, nx, ny, LANES),
        tuple(vmem(2, x + 2, y, z) for x, y, z in shapes),
        tuple(vmem(2, 2, x, 1, z) for x, y, z in shapes),
        tuple(vmem(2, 2, x, 1, z) for x, y, z in shapes),
        tuple(vmem(7, x, y, z) for x, y, z in shapes[:3]),
        tuple(vmem(x, y, z) for x, y, z in shapes[:3]),
        vmem(2, 2, ny, wide),
        vmem(2, 2, nx, 1, wide),
        vmem(2, 2, nx, 1, wide),
        vmem(2, nx, ny, LANES),
        vmem(2, nx, ny, LANES),
        vmem(2, groups, ny, LANES),
        vmem(2, groups, ny, LANES),
        dma((4, 4, 2)), dma((4, 4, 2)), dma((4,)), dma((4,)), dma((4,)), dma((4,)),
    ]
    spec = pl.BlockSpec(memory_space=pltpu.VMEM)
    return pl.pallas_call(
        functools.partial(kernel, (nx, ny, nz), names),
        out_shape=jax.ShapeDtypeStruct(right_side.shape, f32),
        in_specs=[spec] * 3,
        out_specs=spec,
        scratch_shapes=scratch,
        compiler_params=pltpu.CompilerParams(
            collective_id=0, has_side_effects=True, vmem_limit_bytes=60 * 1024 * 1024),
    )(right_side, coefficients, first_guess)


def slab_kernel(sizes, mesh_counts, names, b_hbm, k_hbm, g_hbm, out_ref, *scratch):
    (stage, sb, rb, field, ub, bb, rr, fw, cells, ms, fs, es, tmp, so, ro,
     in_sem, send, recv, zsend, zrecv, gsend, grecv, osend, orecv) = scratch
    nx, ny, nz = sizes
    cx, cy, cz = mesh_counts
    group = cx * cy
    slab = nz // group
    pieces = LANES // slab
    rows_of = nx // pieces
    deep = 2 * SWEEPS
    near = SWEEPS
    span = LANES // cx
    gx, gy, gz = (lax.axis_index(n) for n in names)
    me = gx * cy + gy

    def slab_of(x, y, z):
        p = x * cy + y + lax.rem(x, 2) * (cy - 1 - 2 * y)
        return p + lax.rem(z, 2) * (group - 1 - 2 * p)

    def device_of(s, z):
        p = s + lax.rem(z, 2) * (group - 1 - 2 * s)
        x, t = p // cy, lax.rem(p, cy)
        return x, t + lax.rem(x, 2) * (cy - 1 - 2 * t)

    mine = slab_of(gx, gy, gz)
    chain = gz * group + mine
    has_prev, has_next = chain > 0, chain < cz * group - 1

    def neighbour(step):
        c = chain + step
        c = jnp.clip(c, 0, cz * group - 1)
        z, s = c // group, lax.rem(c, group)
        x, y = device_of(s, z)
        return {names[0]: x, names[1]: y, names[2]: z}

    prev_id, next_id = neighbour(-1), neighbour(1)
    across_prev = has_prev & (mine == 0)
    across_next = has_next & (mine == group - 1)

    loads = [pltpu.make_async_copy(k_hbm.at[j], stage.at[j], in_sem.at[j]) for j in range(4)]
    loads.append(pltpu.make_async_copy(g_hbm, stage.at[4], in_sem.at[4]))
    loads.append(pltpu.make_async_copy(b_hbm, stage.at[5], in_sem.at[5]))
    for c in loads:
        c.start()

    def peer(rel):
        return lax.rem(gx + rel // cy, cx), lax.rem(gy + rel % cy, cy)

    barrier = pltpu.get_barrier_semaphore()
    for rel in range(1, group):
        x, y = peer(rel)
        pl.semaphore_signal(barrier, inc=1, device_id={names[0]: x, names[1]: y}, device_id_type=MESH)

    @pl.when(across_prev)
    def _():
        pl.semaphore_signal(barrier, inc=1, device_id=prev_id, device_id_type=MESH)

    @pl.when(across_next)
    def _():
        pl.semaphore_signal(barrier, inc=1, device_id=next_id, device_id_type=MESH)

    @pl.when(jnp.logical_not(has_prev))
    def _():
        field[:, :, 0:deep] = jnp.zeros((4, nx, deep, LANES), jnp.float32)
        ub[:, 0:near] = jnp.zeros((nx, near, LANES), jnp.float32)
        for g in range(3):
            x = fs[g].shape[1]
            fs[g][:, :, 0:near] = jnp.zeros((CYCLES, x, near, LANES), jnp.float32)

    @pl.when(jnp.logical_not(has_next))
    def _():
        field[:, :, slab + deep:] = jnp.zeros((4, nx, deep, LANES), jnp.float32)
        ub[:, slab + near:] = jnp.zeros((nx, near, LANES), jnp.float32)
        for g in range(3):
            x, rows = fs[g].shape[1:3]
            fs[g][:, :, rows - near:] = jnp.zeros((CYCLES, x, near, LANES), jnp.float32)

    def lane_of(shape):
        return iota(shape, len(shape) - 1)

    tile_lane = lane_of((ny, LANES))

    def regroup(values):
        values = list(values)
        step = pieces // 2
        while step:
            width = slab * step
            low = lax.rem(tile_lane // width, 2) == 0
            for i in range(pieces):
                if i & step == 0:
                    a, c = values[i], values[i + step]
                    values[i] = jnp.where(low, a, pltpu.roll(c, width, 1))
                    values[i + step] = jnp.where(low, pltpu.roll(a, LANES - width, 1), c)
            step //= 2
        return values

    def pack(f):
        for xi in range(rows_of):
            for t in range(nz // LANES):
                parts = regroup(
                    [stage[f, q * rows_of + xi, :, LANES * t:LANES * (t + 1)] for q in range(pieces)])
                for q in range(pieces):
                    sb[f, t * pieces + q, xi] = parts[q]

    def spread_copies(f):
        copies = []
        for rel in range(1, group):
            x, y = peer(rel)
            copies.append(pltpu.make_async_remote_copy(
                src_ref=sb.at[f, slab_of(x, y, gz)], dst_ref=rb.at[f, :, me],
                send_sem=send.at[f, rel], recv_sem=recv.at[f, rel],
                device_id={names[0]: x, names[1]: y}, device_id_type=MESH))
        return copies

    def z_copies(ref, own_low, own, halo, ssem, rsem):
        up = pltpu.make_async_remote_copy(
            src_ref=ref.at[:, pl.ds(own_low + own - halo, halo)], dst_ref=ref.at[:, pl.ds(own_low - halo, halo)],
            send_sem=ssem.at[0], recv_sem=rsem.at[0], device_id=next_id, device_id_type=MESH)
        down = pltpu.make_async_remote_copy(
            src_ref=ref.at[:, pl.ds(own_low, halo)], dst_ref=ref.at[:, pl.ds(own_low + own, halo)],
            send_sem=ssem.at[1], recv_sem=rsem.at[1], device_id=prev_id, device_id_type=MESH)
        return up, down

    def z_start(copies):
        up, down = copies

        @pl.when(has_next)
        def _():
            up.start()

        @pl.when(has_prev)
        def _():
            down.start()

    def z_finish(copies):
        up, down = copies

        @pl.when(has_prev)
        def _():
            up.wait_recv()

        @pl.when(has_next)
        def _():
            down.wait_recv()

        @pl.when(has_next)
        def _():
            up.wait_send()

        @pl.when(has_prev)
        def _():
            down.wait_send()

    every = []
    for f in range(6):
        loads[f].wait()
        pack(f)
        if f == 0:
            pl.semaphore_wait(
                barrier, group - 1 + jnp.where(across_prev, 1, 0) + jnp.where(across_next, 1, 0))
        copies = spread_copies(f)
        for c in copies:
            c.start()
        every.append(copies)
        rb[f, :, me] = sb[f, mine]

    def arrive(f):
        for c in every[f]:
            c.wait_recv()
        for xi in range(rows_of):
            turned = rb[f, xi].reshape((LANES, LANES)).T
            for q in range(pieces):
                part = turned[q * slab:(q + 1) * slab]
                x = q * rows_of + xi
                if f < 4:
                    field[f, x, deep:deep + slab] = part
                elif f == 4:
                    ub[x, near:near + slab] = part
                else:
                    bb[x] = part

    halos = []
    for f in range(5):
        arrive(f)
        if f < 4:
            halos.append(z_copies(field.at[f], deep, slab, deep, zsend.at[f], zrecv.at[f]))
        else:
            halos.append(z_copies(ub, near, slab, near, zsend.at[f], zrecv.at[f]))
        z_start(halos[-1])

    wide_rows = slab + 2 * near
    first_row, last_row = deep - near, deep + slab + near
    half = span // 2
    r, c = iota((2 * LANES, LANES), 0), iota((2 * LANES, LANES), 1)
    lane = lax.rem(r, LANES)
    y_mean = jnp.where(
        (r // LANES == lax.rem(c, span) // half) & (lane // span == c // span)
        & (lax.rem(lane, span) // 2 == lax.rem(c, half)), 0.5, 0.0).astype(jnp.bfloat16)
    r, c = iota((LANES, 2 * LANES), 0), iota((LANES, 2 * LANES), 1)
    lane = lax.rem(c, LANES)
    here = (c // LANES == lax.rem(r, span) // half) & (lane // span == r // span)
    fine_y = lax.rem(lane, span)
    main = fine_y // 2
    side = jnp.where(lax.rem(fine_y, 2) == 1, main + 1, main - 1)
    coarse_y = lax.rem(r, half)
    y_spread = jnp.where(
        here & (coarse_y == main), 0.75, jnp.where(here & (coarse_y == side), 0.25, 0.0)).astype(jnp.bfloat16)
    folds = nx // 2

    def fold_y(rows_low, rows_high):
        n = rows_low.shape[0] * rows_low.shape[1]
        both = jnp.concatenate([rows_low.reshape((n, LANES)), rows_high.reshape((n, LANES))], 1)
        return spread(both, y_mean).reshape(rows_low.shape)

    for f in range(4):
        z_finish(halos[f])
        factors = [0.25 if f == d else 1.0 for d in range(3)]
        for i in range(nx // 2):
            cells[0][f, i] = (0.5 * factors[0]) * (
                field[f, 2 * i, first_row:last_row] + field[f, 2 * i + 1, first_row:last_row])
        cells[1][f] = fold_y(
            field[f, 0:folds, first_row:last_row], field[f, folds:nx, first_row:last_row]) * factors[1]
        coarse_rows = slab // 2 + 2 * near
        for x in range(nx):
            cells[2][f, x] = (0.5 * factors[2]) * (
                field[f, x, pl.ds(0, coarse_rows, stride=2)] + field[f, x, pl.ds(1, coarse_rows, stride=2)])

    def masks(shape, width):
        lanes = lane_of(shape)
        y = lax.rem(lanes, width)
        return y != 0, y != width - 1, lanes >= width, lanes < LANES - width

    def x_pair(get, i, count, width):
        below = get(i - 1) if i > 0 else pltpu.roll(get(count - 1), width, 1)
        above = get(i + 1) if i < count - 1 else pltpu.roll(get(0), LANES - width, 1)
        return below, above

    def weights(k, i, count, width, z_pair):
        y_low, y_high, x_low, x_high = masks(k(3, i).shape, width)
        k0, k1, k2 = k(0, i), k(1, i), k(2, i)
        below, above = x_pair(lambda p: k(0, p), i, count, width)
        if i == 0:
            below = jnp.where(x_low, below, 0.0)
        if i == count - 1:
            above = jnp.where(x_high, above, 0.0)
        around = [
            (k0, below, x_low if i == 0 else None), (k0, above, x_high if i == count - 1 else None),
            (k1, jnp.where(y_low, pltpu.roll(k1, 1, 1), 0.0), y_low),
            (k1, jnp.where(y_high, pltpu.roll(k1, LANES - 1, 1), 0.0), y_high),
        ]
        around += [(k2, other, None) for other in z_pair]
        total = k(3, i)
        found = []
        for middle, other, keep in around:
            w = 0.5 * (middle + other)
            total = total + w
            found.append(w if keep is None else jnp.where(keep, w, 0.0))
        return found, total

    widths = (span, half, span)
    for g in range(3):
        count, rows = cells[g].shape[1:3]
        for i in range(count):
            k2 = cells[g][2, i]
            z_pair = (pltpu.roll(k2, 1, 0), pltpu.roll(k2, rows - 1, 0))
            w, total = weights(lambda j, p: cells[g][j, p], i, count, widths[g], z_pair)
            inside = cells[g][3, i] > 0.0
            scale = jnp.where(inside, relaxation / jnp.where(inside, total, 1.0), 0.0)
            ms[g][6, i] = scale
            for j in range(6):
                ms[g][j, i] = w[j] * scale
    own = slice(deep, deep + slab)
    for i in range(nx):
        z_pair = (field[2, i, deep - 1:deep + slab - 1], field[2, i, deep + 1:deep + slab + 1])
        w, total = weights(lambda j, p: field[j, p, own], i, nx, span, z_pair)
        for j in range(6):
            fw[j, i] = w[j]
        fw[6, i] = total

    z_finish(halos[4])
    arrive(5)

    def sweep(g, src, dst):
        count, rows = src.shape[0:2]
        m, f = ms[g], fs[g]
        for i in range(count):
            middle = src[i]
            below, above = x_pair(lambda p: src[p], i, count, widths[g])
            new = (1.0 - relaxation) * middle + f[cycle, i]
            new = new + m[0, i] * below
            new = new + m[1, i] * above
            new = new + m[2, i] * pltpu.roll(middle, 1, 1)
            new = new + m[3, i] * pltpu.roll(middle, LANES - 1, 1)
            new = new + m[4, i] * pltpu.roll(middle, 1, 0)
            new = new + m[5, i] * pltpu.roll(middle, rows - 1, 0)
            dst[i] = new

    for cycle in range(CYCLES):
        for i in range(nx):
            u = ub[i, near:near + slab]
            below, above = x_pair(lambda p: ub[p, near:near + slab], i, nx, span)
            residual = bb[i] - fw[6, i] * u
            residual = residual + fw[0, i] * below
            residual = residual + fw[1, i] * above
            residual = residual + fw[2, i] * pltpu.roll(u, 1, 1)
            residual = residual + fw[3, i] * pltpu.roll(u, LANES - 1, 1)
            residual = residual + fw[4, i] * ub[i, near - 1:near + slab - 1]
            residual = residual + fw[5, i] * ub[i, near + 1:near + slab + 1]
            rr[i] = residual
        for x in range(nx):
            first = 0.5 * (rr[x, pl.ds(0, slab // 2, stride=2)] + rr[x, pl.ds(1, slab // 2, stride=2)])
            fs[2][cycle, x, near:near + slab // 2] = ms[2][6, x, near:near + slab // 2] * first
        for i in range(nx // 2):
            first = 0.5 * (rr[2 * i] + rr[2 * i + 1])
            fs[0][cycle, i, near:near + slab] = ms[0][6, i, near:near + slab] * first
        first = fold_y(rr[0:folds], rr[folds:nx])
        fs[1][cycle, :, near:near + slab] = ms[1][6, :, near:near + slab] * first
        moves = []
        for g in range(3):
            rows = fs[g].shape[2]
            moves.append(z_copies(
                fs[g].at[cycle], near, rows - 2 * near, near, gsend.at[cycle, g], grecv.at[cycle, g]))
            z_start(moves[-1])
        for g in range(3):
            z_finish(moves[g])
            sweep(g, fs[g].at[cycle], es[g].at[0])

        @pl.loop(0, SWEEPS - 2)
        def _(repeat):
            old = lax.rem(repeat, 2)
            for g in range(3):
                sweep(g, es[g].at[old], es[g].at[1 - old])

        last = (SWEEPS - 2) % 2
        keep = wide_rows if cycle < CYCLES - 1 else slab
        low = 0 if cycle < CYCLES - 1 else near
        taken = slice(low, low + keep)
        lanes = lane_of((keep, LANES))
        e = es[1][last, :, taken].reshape((folds * keep, LANES))
        from_y = spread(e, y_spread)
        coarse_low = near - (near - low) // 2
        count = keep // 2
        for x in range(nx):
            middle = es[2][last, x, coarse_low:coarse_low + count]
            lower = es[2][last, x, coarse_low - 1:coarse_low + count - 1]
            upper = es[2][last, x, coarse_low + 1:coarse_low + count + 1]
            tmp[x, pl.ds(0, count, stride=2)] = 0.75 * middle + 0.25 * lower
            tmp[x, pl.ds(1, count, stride=2)] = 0.75 * middle + 0.25 * upper
        for i in range(nx // 2):
            middle = es[0][last, i, taken]
            below, above = x_pair(lambda p: es[0][last, p, taken], i, nx // 2, span)
            if i == 0:
                below = jnp.where(lanes >= span, below, 0.0)
            if i == nx // 2 - 1:
                above = jnp.where(lanes < LANES - span, above, 0.0)
            for odd, other in ((0, below), (1, above)):
                x = 2 * i + odd
                from_x = 0.75 * middle + 0.25 * other
                fold, xi = x // folds, x % folds
                mid_y = from_y[xi * keep:(xi + 1) * keep, LANES * fold:LANES * (fold + 1)]
                update = (from_x + mid_y) + tmp[x, 0:keep]
                ub[x, taken] = ub[x, taken] + blending * update
        if cycle < CYCLES - 1:
            @pl.when(jnp.logical_not(has_prev))
            def _():
                ub[:, 0:near] = jnp.zeros((nx, near, LANES), jnp.float32)

            @pl.when(jnp.logical_not(has_next))
            def _():
                ub[:, slab + near:] = jnp.zeros((nx, near, LANES), jnp.float32)

    backs = []
    for xi in range(rows_of):
        block = jnp.concatenate([ub[q * rows_of + xi, near:near + slab] for q in range(pieces)], 0)
        turned = block.T
        for j in range(group):
            so[j, xi] = turned[j * ny:(j + 1) * ny]
    for rel in range(1, group):
        x, y = peer(rel)
        backs.append(pltpu.make_async_remote_copy(
            src_ref=so.at[x * cy + y], dst_ref=ro.at[mine], send_sem=osend.at[rel], recv_sem=orecv.at[rel],
            device_id={names[0]: x, names[1]: y}, device_id_type=MESH))
    for c in backs:
        c.start()
    ro[mine] = so[me]
    for c in backs:
        c.wait_recv()
    for xi in range(rows_of):
        for t in range(nz // LANES):
            parts = regroup([ro[t * pieces + q, xi] for q in range(pieces)])
            for q in range(pieces):
                out_ref[q * rows_of + xi, :, LANES * t:LANES * (t + 1)] = parts[q]
    for copies in every + [backs]:
        for c in copies:
            c.wait_send()


def slab_fits(shape, counts):
    nx, ny, nz = shape
    cx, cy, _ = counts
    group = cx * cy
    if nz % group or ny * group != LANES or LANES % (2 * cx):
        return False
    slab = nz // group
    pieces = LANES // slab
    return (
        slab * pieces == LANES and pieces & (pieces - 1) == 0 and nx % (2 * pieces) == 0
        and slab % 16 == 0 and slab >= 2 * SWEEPS and nz % LANES == 0)


def slab_body(names, counts, right_side, coefficients, first_guess):
    nx, ny, nz = right_side.shape
    f32 = jnp.float32
    vmem = lambda *shape: pltpu.VMEM(shape, f32)
    dma = pltpu.SemaphoreType.DMA
    group = counts[0] * counts[1]
    slab = nz // group
    rows_of = nx // (LANES // slab)
    near, deep = SWEEPS, 2 * SWEEPS
    wide = slab + 2 * near
    shapes = ((nx // 2, wide), (nx // 2, wide), (nx, slab // 2 + 2 * near))
    blocks = (group, rows_of, ny, LANES)
    scratch = [
        vmem(6, nx, ny, nz),
        vmem(6, *blocks),
        vmem(6, rows_of, group, ny, LANES),
        vmem(4, nx, slab + 2 * deep, LANES),
        vmem(nx, wide, LANES),
        vmem(nx, slab, LANES),
        vmem(nx, slab, LANES),
        vmem(7, nx, slab, LANES),
        tuple(vmem(4, x, z, LANES) for x, z in shapes),
        tuple(vmem(7, x, z, LANES) for x, z in shapes),
        tuple(vmem(CYCLES, x, z, LANES) for x, z in shapes),
        tuple(vmem(2, x, z, LANES) for x, z in shapes),
        vmem(nx, wide, LANES),
        vmem(*blocks),
        vmem(*blocks),
        dma((6,)), dma((6, group)), dma((6, group)), dma((5, 2)), dma((5, 2)),
        dma((CYCLES, 3, 2)), dma((CYCLES, 3, 2)), dma((group,)), dma((group,)),
    ]
    hbm = pl.BlockSpec(memory_space=pl.ANY)
    return pl.pallas_call(
        functools.partial(slab_kernel, (nx, ny, nz), counts, names),
        out_shape=jax.ShapeDtypeStruct(right_side.shape, f32),
        in_specs=[hbm] * 3,
        out_specs=pl.BlockSpec(memory_space=pltpu.VMEM),
        scratch_shapes=scratch,
        compiler_params=pltpu.CompilerParams(
            collective_id=0, has_side_effects=True, vmem_limit_bytes=60 * 1024 * 1024),
    )(right_side, coefficients, first_guess)


def solution(mesh):
    names = tuple(mesh.axis_names)
    counts = tuple(mesh.shape[n] for n in names)
    in_specs = (P(*names), P(None, *names), P(*names))

    def local(right_side, coefficients, first_guess):
        if slab_fits(right_side.shape, counts):
            return slab_body(names, counts, right_side, coefficients, first_guess)
        return body(names, right_side, coefficients, first_guess)

    return jax.shard_map(
        local, mesh=mesh, in_specs=in_specs, out_specs=P(*names), check_vma=False)
```

```python
import functools

import jax
import jax.numpy as jnp
from jax import lax
from jax.experimental import pallas as pl
from jax.experimental.pallas import tpu as pltpu
from jax.sharding import PartitionSpec as P

CYCLES = 2
SWEEPS = 8
REACH = 2 * (SWEEPS + 1)
STEP = 20
LANES = 128
CHUNK = 1

relaxation = 0.8
blending = 0.4
MESH = pl.DeviceIdType.MESH


def iota(shape, dim):
    return lax.broadcasted_iota(jnp.int32, shape, dim)


def spread(a, b):
    total = None
    for _ in range(3):
        part = a.astype(jnp.bfloat16)
        a = a - part.astype(jnp.float32)
        term = jnp.dot(part, b, preferred_element_type=jnp.float32)
        total = term if total is None else total + term
    return total


def kernel(sizes, names, b_ref, k_ref, g_ref, out_ref, *scratch):
    (fields, cells, tiles, es, yss, yrs, ms, fs, kxr, kys, kyr, zs, zr, us, ur,
     send, recv, ksend, krecv, zsend, zrecv) = scratch
    nx, ny, nz = sizes
    wide = nz + LANES
    shapes = ((nx // 2, ny, wide), (nx, ny // 2, wide), (nx, ny, nz // 2 + LANES), (nx, ny, wide))
    place = [lax.axis_index(n) for n in names]
    counts = [lax.axis_size(n) for n in names]
    has_low = [p > 0 for p in place]
    has_high = [p < c - 1 for p, c in zip(place, counts)]
    ways = []
    for axis in range(3):
        ways.append((axis, -1, has_low[axis], has_high[axis]))
        ways.append((axis, 1, has_high[axis], has_low[axis]))

    def target(way):
        axis, step = ways[way][:2]
        return {names[axis]: place[axis] + step}

    def copy(src, dst, ssem, rsem, way):
        return pltpu.make_async_remote_copy(
            src_ref=src, dst_ref=dst, send_sem=ssem, recv_sem=rsem,
            device_id=target(way), device_id_type=MESH,
        )

    def start(copies):
        for way, c in copies:
            @pl.when(ways[way][2])
            def _():
                c.start()

    def finish(copies):
        for way, c in copies:
            @pl.when(ways[way][3])
            def _():
                c.wait_recv()
        for way, c in copies:
            @pl.when(ways[way][2])
            def _():
                c.wait_send()

    def faces(g, slot, keep=(0, 1, 2, 3)):
        x = shapes[g][0]
        e, ys, yr = es[g], yss[g], yrs[g]
        ends = (
            (e.at[slot, 1], e.at[slot, x + 1]),
            (e.at[slot, x], e.at[slot, 0]),
            (ys.at[slot, 0], yr.at[slot, 1]),
            (ys.at[slot, 1], yr.at[slot, 0]),
        )
        return [
            (way, copy(*ends[way], send.at[g, way, slot], recv.at[g, way, slot], way)) for way in keep
        ]

    for g in range(4):
        x = shapes[g][0]
        for slot in range(2):
            zero = jnp.zeros(shapes[g][1:], jnp.float32)
            es[g][slot, 0] = zero
            es[g][slot, x + 1] = zero
        yrs[g][...] = jnp.zeros(yrs[g].shape, jnp.float32)
    kxr[...] = jnp.zeros(kxr.shape, jnp.float32)
    kyr[...] = jnp.zeros(kyr.shape, jnp.float32)
    zr[...] = jnp.zeros(zr.shape, jnp.float32)
    ur[...] = jnp.zeros(ur.shape, jnp.float32)

    barrier = pltpu.get_barrier_semaphore()
    for way in range(6):
        @pl.when(ways[way][2])
        def _():
            pl.semaphore_signal(barrier, inc=1, device_id=target(way), device_id_type=MESH)
    peers = sum(jnp.where(has, 1, 0) for has in has_low + has_high)
    pl.semaphore_wait(barrier, peers)

    lane = iota((nx, ny, LANES), 2)
    low = jnp.zeros((nx, ny, LANES), jnp.float32)
    high = low
    for j in range(6):
        if j < 4:
            first, last = k_ref[j, :, :, :LANES], k_ref[j, :, :, nz - LANES:]
        elif j == 4:
            first, last = g_ref[:, :, :LANES], g_ref[:, :, nz - LANES:]
        else:
            first, last = b_ref[:, :, :LANES], b_ref[:, :, nz - LANES:]
        here = (lane >= STEP * j) & (lane < STEP * j + REACH)
        low = jnp.where(here, pltpu.roll(first, STEP * j, 2) if j else first, low)
        high = jnp.where(here, pltpu.roll(last, (STEP * j + REACH) % LANES, 2), high)
    zs[0] = low
    zs[1] = high
    deep = [
        (4, copy(zs.at[0], zr.at[1], zsend.at[0], zrecv.at[0], 4)),
        (5, copy(zs.at[1], zr.at[0], zsend.at[1], zrecv.at[1], 5)),
    ]
    start(deep)
    for j in range(4):
        fields[j, :, :, :nz] = k_ref[j]
    fields[4, :, :, :nz] = b_ref[...]
    es[3][0, 1:nx + 1, :, :nz] = g_ref[...]
    finish(deep)
    above, below = zr[1], zr[0]

    def beside(j):
        up = pltpu.roll(above, (LANES - STEP * j) % LANES, 2) if j else above
        down = pltpu.roll(below, (2 * LANES - REACH - STEP * j) % LANES, 2)
        return jnp.where(lane < REACH, up, jnp.where(lane >= LANES - REACH, down, 0.0))

    for j in range(4):
        fields[j, :, :, nz:] = beside(j)
    es[3][0, 1:nx + 1, :, nz:] = beside(4)
    fields[4, :, :, nz:] = beside(5)

    def send_guess(slot):
        u = es[3][slot, 1:nx + 1]
        yss[3][slot, 0] = u[:, 0:1, :]
        yss[3][slot, 1] = u[:, ny - 1:ny, :]
        start(faces(3, slot))

    ky = fields[1]
    for row in range(2):
        kys[0, row] = ky[:, row:row + 1, :]
        kys[1, row] = ky[:, ny - 2 + row:ny - 1 + row, :]
    edges = [
        (0, copy(fields.at[0, pl.ds(0, 2)], kxr.at[1], ksend.at[0], krecv.at[0], 0)),
        (1, copy(fields.at[0, pl.ds(nx - 2, 2)], kxr.at[0], ksend.at[1], krecv.at[1], 1)),
        (2, copy(kys.at[0], kyr.at[1], ksend.at[2], krecv.at[2], 2)),
        (3, copy(kys.at[1], kyr.at[0], ksend.at[3], krecv.at[3], 3)),
    ]
    start(edges)
    send_guess(0)

    half = nz // 2
    r, c = iota((wide, half + LANES), 0), iota((wide, half + LANES), 1)
    home = jnp.where(
        r < nz, r // 2,
        jnp.where(r < nz + LANES // 2, half + (r - nz) // 2, half + LANES // 2 + (r - nz) // 2),
    )
    z_mean = jnp.where(home == c, 0.5, 0.0).astype(jnp.bfloat16)
    rows = nx * ny
    r, c = iota((half + LANES, nz), 0), iota((half + LANES, nz), 1)
    main = c // 2
    total = half + LANES
    side = jnp.where(c % 2 == 1, main + 1, jnp.where(main == 0, total - 1, main - 1))
    z_spread = (jnp.where(r == main, 0.75, 0.0) + jnp.where(r == side, 0.25, 0.0)).astype(jnp.bfloat16)

    count = wide // LANES
    even_rows, odd_rows = pl.ds(0, ny // 2, stride=2), pl.ds(1, ny // 2, stride=2)

    def put_tiles(planes, values):
        for t in range(values.shape[2] // LANES):
            tiles[t, planes] = values[:, :, LANES * t:LANES * (t + 1)]

    def get_tiles(planes, tiles_of=count):
        return jnp.concatenate([tiles[t, planes] for t in range(tiles_of)], 2)

    def y_mean(planes):
        return jnp.concatenate(
            [0.5 * (tiles[t, planes, even_rows] + tiles[t, planes, odd_rows]) for t in range(count)], 2)

    def chunks(x, step=CHUNK):
        return [slice(x0, x0 + step) for x0 in range(0, x, step)]

    def below_of(ref, planes, halo):
        if planes.start > 0:
            return ref[planes.start - 1:planes.stop - 1]
        return halo if planes.stop == 1 else jnp.concatenate([halo, ref[0:planes.stop - 1]], 0)

    def above_of(ref, planes, halo):
        if planes.stop < ref.shape[0]:
            return ref[planes.start + 1:planes.stop + 1]
        if planes.stop == planes.start + 1:
            return halo
        return jnp.concatenate([ref[planes.start + 1:planes.stop], halo], 0)

    def y_shift(values, halo_low, halo_high):
        y = values.shape[1]
        row = iota(values.shape, 1)
        lower = jnp.where(row == 0, halo_low, pltpu.roll(values, 1, 1))
        upper = jnp.where(row == y - 1, halo_high, pltpu.roll(values, y - 1, 1))
        return lower, upper

    def z_shift(values):
        return pltpu.roll(values, 1, 2), pltpu.roll(values, values.shape[2] - 1, 2)

    def face_weights(k, planes, near_x, near_y):
        k0, k1, k2 = k.at[0], k.at[1], k.at[2]
        m1, m2 = k1[planes], k2[planes]
        groups = (
            (k0[planes], (below_of(k0, planes, near_x[0]), above_of(k0, planes, near_x[1]))),
            (m1, y_shift(m1, near_y[0](planes), near_y[1](planes))),
            (m2, z_shift(m2)),
        )
        found = []
        total = k[3, planes]
        for middle, pair in groups:
            for other in pair:
                found.append(0.5 * (middle + other))
                total = total + found[-1]
        return found, total

    for j in range(4):
        for d in range(2):
            factor = 0.25 if j == d else 1.0
            if d == 0:
                for i in range(nx // 2):
                    cells[0][j, i] = (0.5 * factor) * (fields[j, 2 * i] + fields[j, 2 * i + 1])
            else:
                for planes in chunks(nx):
                    put_tiles(planes, fields[j, planes])
                for planes in chunks(nx):
                    cells[1][j, planes] = y_mean(planes) * factor
    for j in range(4):
        factor = 0.25 if j == 2 else 1.0
        for planes in chunks(nx, nx // 2):
            flat = fields[j, planes].reshape((rows // 2, wide))
            cells[2][j, planes] = (spread(flat, z_mean) * factor).reshape((nx // 2,) + shapes[2][1:])
    finish(edges)
    near_rows = [kxr[0, 1], kxr[1, 0]] + [kyr[0, 1].reshape((nx, wide)), kyr[1, 0].reshape((nx, wide))]
    edge = spread(jnp.concatenate(near_rows, 0), z_mean)
    edge_x = [edge[0:ny][None], edge[ny:2 * ny][None]]
    edge_y = [edge[2 * ny + nx * side:2 * ny + nx * (side + 1)].reshape((nx, 1, half + LANES)) for side in range(2)]
    put_tiles(slice(0, 2), jnp.stack([kxr[0, 1], kxr[1, 0]]))
    pair = y_mean(slice(0, 2))

    near_xs = (
        [0.125 * (kxr[side, 0:1] + kxr[side, 1:2]) for side in range(2)],
        [pair[0:1], pair[1:2]],
        edge_x,
    )

    def y_face(d, side):
        nearest = kyr.at[side, 1 - side]
        if d == 0:
            return lambda planes: jnp.concatenate(
                [0.5 * (nearest[2 * i:2 * i + 1] + nearest[2 * i + 1:2 * i + 2])
                 for i in range(planes.start, planes.stop)], 0)
        if d == 1:
            return lambda planes: 0.125 * (kyr[side, 0, planes] + kyr[side, 1, planes])
        if d == 2:
            return lambda planes: edge_y[side][planes]
        return lambda planes: nearest[planes]

    for d in range(3):
        for planes in chunks(shapes[d][0]):
            w, total_coarse = face_weights(
                cells[d], planes, near_xs[d], (y_face(d, 0), y_face(d, 1)))
            inside = cells[d][3, planes] > 0.0
            scale = jnp.where(inside, relaxation / jnp.where(inside, total_coarse, 1.0), 0.0)
            ms[d][6, planes] = scale
            for j in range(6):
                ms[d][j, planes] = w[j] * scale

    def sweep(g, slot, new_slot, keep=(0, 1, 2, 3)):
        e, yr, ys, m, f = es[g], yrs[g], yss[g], ms[g], fs[g]
        x, y, z = shapes[g]
        order = list(range(0, x, CHUNK))
        order = order[:1] + order[-1:] + order[1:-1]
        for x0 in order:
            planes = slice(x0, x0 + CHUNK)
            middle = e[slot, x0 + 1:x0 + 1 + CHUNK]
            y_low, y_high = y_shift(middle, yr[slot, 0, planes], yr[slot, 1, planes])
            z_low, z_high = z_shift(middle)
            new = (1.0 - relaxation) * middle + f[planes]
            new = new + m[0, planes] * e[slot, x0:x0 + CHUNK]
            new = new + m[1, planes] * e[slot, x0 + 2:x0 + 2 + CHUNK]
            new = new + m[2, planes] * y_low
            new = new + m[3, planes] * y_high
            new = new + m[4, planes] * z_low
            new = new + m[5, planes] * z_high
            e[new_slot, x0 + 1:x0 + 1 + CHUNK] = new
            ys[new_slot, 0, planes] = new[:, 0:1]
            ys[new_slot, 1, planes] = new[:, y - 1:y]
            if x0 == order[1] and 0 in keep:
                start(faces(g, new_slot, (0, 1)))
        if 2 in keep:
            start(faces(g, new_slot, (2, 3)))

    for cycle in range(CYCLES):
        slot = cycle % 2
        finish(faces(3, slot))
        u = es[3]
        for planes in chunks(nx):
            x0, x1 = planes.start, planes.stop
            middle = u[slot, x0 + 1:x1 + 1]
            y_low, y_high = y_shift(middle, yrs[3][slot, 0, planes], yrs[3][slot, 1, planes])
            z_low, z_high = z_shift(middle)
            w, total_fine = face_weights(
                fields, planes, (kxr[0, 1:2], kxr[1, 0:1]), (y_face(3, 0), y_face(3, 1)))
            residual = fields[4, planes] - total_fine * middle
            around = (u[slot, x0:x1], u[slot, x0 + 2:x1 + 2], y_low, y_high, z_low, z_high)
            for j in range(6):
                residual = residual + w[j] * around[j]
            put_tiles(planes, residual)
        for g in range(3):
            x, y, z = shapes[g]
            if g == 2:
                flat = get_tiles(slice(0, nx)).reshape((rows, wide))
                whole = spread(flat, z_mean).reshape(shapes[2])
            for planes in chunks(x):
                if g == 0:
                    pairs = [get_tiles(slice(2 * i, 2 * i + 2)) for i in range(planes.start, planes.stop)]
                    first = jnp.concatenate([0.5 * (p[0:1] + p[1:2]) for p in pairs], 0)
                elif g == 1:
                    first = y_mean(planes)
                else:
                    first = whole[planes]
                first = ms[g][6, planes] * first
                fs[g][planes] = first
                es[g][1, planes.start + 1:planes.stop + 1] = first
                yss[g][1, 0, planes] = first[:, 0:1]
                yss[g][1, 1, planes] = first[:, y - 1:y]
            start(faces(g, 1))

        @pl.loop(1, SWEEPS - 1)
        def _(repeat):
            old = lax.rem(repeat, 2)
            for g in range(3):
                finish(faces(g, old))
                sweep(g, old, 1 - old)

        last = SWEEPS % 2
        needed = ((0, 1), (2, 3), ())
        for g in range(3):
            finish(faces(g, 1 - last))
            sweep(g, 1 - last, last, needed[g])
        e = es[2][last, 1:nx + 1].reshape((rows, half + LANES))
        from_z = spread(e, z_spread).reshape((nx, ny, nz))
        finish(faces(1, last, needed[1]))
        for planes in chunks(nx):
            e = es[1][last, planes.start + 1:planes.stop + 1, :, :nz]
            y_low, y_high = y_shift(
                e, yrs[1][last, 0, planes, :, :nz], yrs[1][last, 1, planes, :, :nz])
            even = 0.75 * e + 0.25 * y_low
            odd = 0.75 * e + 0.25 * y_high
            for t in range(nz // LANES):
                tiles[t, planes, even_rows] = even[:, :, LANES * t:LANES * (t + 1)]
                tiles[t, planes, odd_rows] = odd[:, :, LANES * t:LANES * (t + 1)]
        finish(faces(0, last, needed[0]))
        for i in range(nx // 2):
            planes = slice(2 * i, 2 * i + 2)
            e = es[0][last, i:i + 3, :, :nz]
            even = 0.75 * e[1:2] + 0.25 * e[0:1]
            odd = 0.75 * e[1:2] + 0.25 * e[2:3]
            update = (jnp.concatenate([even, odd], 0) + get_tiles(planes, nz // LANES)) + from_z[planes]
            final = es[3][slot, 2 * i + 1:2 * i + 3, :, :nz] + blending * update
            if cycle == CYCLES - 1:
                out_ref[planes] = final
            else:
                es[3][1 - slot, 2 * i + 1:2 * i + 3, :, :nz] = final
        if cycle == CYCLES - 1:
            continue
        result = es[3].at[1 - slot, 1:nx + 1]
        per = LANES // STEP
        plane_lane = iota((ny, LANES), 1)
        groups = us.shape[1]
        for q in range(groups):
            low = jnp.zeros((ny, LANES), jnp.float32)
            high = low
            for p in range(min(per, nx - q * per)):
                here = (plane_lane >= STEP * p) & (plane_lane < STEP * p + REACH)
                first = result[q * per + p, :, :LANES]
                low = jnp.where(here, pltpu.roll(first, STEP * p, 1) if p else first, low)
                high = jnp.where(
                    here, pltpu.roll(result[q * per + p, :, nz - LANES:nz], (STEP * p + REACH) % LANES, 1), high)
            us[0, q] = low
            us[1, q] = high
        again = [
            (4, copy(us.at[0], ur.at[1], zsend.at[2], zrecv.at[2], 4)),
            (5, copy(us.at[1], ur.at[0], zsend.at[3], zrecv.at[3], 5)),
        ]
        start(again)
        finish(again)
        for i in range(nx):
            q, p = i // per, i % per
            up = pltpu.roll(ur[1, q], (LANES - STEP * p) % LANES, 1) if p else ur[1, q]
            down = pltpu.roll(ur[0, q], (2 * LANES - REACH - STEP * p) % LANES, 1)
            es[3][1 - slot, i + 1, :, nz:] = jnp.where(
                plane_lane < REACH, up, jnp.where(plane_lane >= LANES - REACH, down, 0.0))
        send_guess(1 - slot)


def body(names, right_side, coefficients, first_guess):
    nx, ny, nz = right_side.shape
    wide = nz + LANES
    shapes = ((nx // 2, ny, wide), (nx, ny // 2, wide), (nx, ny, nz // 2 + LANES), (nx, ny, wide))
    f32 = jnp.float32
    vmem = lambda *shape: pltpu.VMEM(shape, f32)
    dma = pltpu.SemaphoreType.DMA
    groups = -(-nx // (LANES // STEP))
    scratch = [
        vmem(5, nx, ny, wide),
        tuple(vmem(4, x, y, z) for x, y, z in shapes[:3]),
        vmem(wide // LANES, nx, ny, LANES),
        tuple(vmem(2, x + 2, y, z) for x, y, z in shapes),
        tuple(vmem(2, 2, x, 1, z) for x, y, z in shapes),
        tuple(vmem(2, 2, x, 1, z) for x, y, z in shapes),
        tuple(vmem(7, x, y, z) for x, y, z in shapes[:3]),
        tuple(vmem(x, y, z) for x, y, z in shapes[:3]),
        vmem(2, 2, ny, wide),
        vmem(2, 2, nx, 1, wide),
        vmem(2, 2, nx, 1, wide),
        vmem(2, nx, ny, LANES),
        vmem(2, nx, ny, LANES),
        vmem(2, groups, ny, LANES),
        vmem(2, groups, ny, LANES),
        dma((4, 4, 2)), dma((4, 4, 2)), dma((4,)), dma((4,)), dma((4,)), dma((4,)),
    ]
    spec = pl.BlockSpec(memory_space=pltpu.VMEM)
    return pl.pallas_call(
        functools.partial(kernel, (nx, ny, nz), names),
        out_shape=jax.ShapeDtypeStruct(right_side.shape, f32),
        in_specs=[spec] * 3,
        out_specs=spec,
        scratch_shapes=scratch,
        compiler_params=pltpu.CompilerParams(
            collective_id=0, has_side_effects=True, vmem_limit_bytes=60 * 1024 * 1024),
    )(right_side, coefficients, first_guess)


def slab_kernel(sizes, mesh_counts, names, b_hbm, k_hbm, g_hbm, out_ref, *scratch):
    (stage, sb, rb, field, ub, bb, rr, fw, cells, ms, fs, es, tmp, so, ro, hx, hys, hyr, hzs, hz, ex,
     in_sem, send, recv, zsend, zrecv, gsend, grecv, osend, orecv, hsend, hrecv, esend, erecv) = scratch
    nx, ny, nz = sizes
    cx, cy, cz = mesh_counts
    group = cx * cy
    slab = nz // group
    pieces = LANES // slab
    rows_of = nx // pieces
    near = SWEEPS
    nears = (near, near, near // 2)
    span = LANES // cx
    gx, gy, gz = (lax.axis_index(n) for n in names)
    me = gx * cy + gy

    def slab_of(x, y, z):
        p = x * cy + y + lax.rem(x, 2) * (cy - 1 - 2 * y)
        return p + lax.rem(z, 2) * (group - 1 - 2 * p)

    def device_of(s, z):
        p = s + lax.rem(z, 2) * (group - 1 - 2 * s)
        x, t = p // cy, lax.rem(p, cy)
        return x, t + lax.rem(x, 2) * (cy - 1 - 2 * t)

    mine = slab_of(gx, gy, gz)
    chain = gz * group + mine
    has_prev, has_next = chain > 0, chain < cz * group - 1

    def neighbour(step):
        c = chain + step
        c = jnp.clip(c, 0, cz * group - 1)
        z, s = c // group, lax.rem(c, group)
        x, y = device_of(s, z)
        return {names[0]: x, names[1]: y, names[2]: z}

    prev_id, next_id = neighbour(-1), neighbour(1)
    place, counts = (gx, gy, gz), (cx, cy, cz)
    has_low = [q > 0 for q in place]
    has_high = [q < c - 1 for q, c in zip(place, counts)]

    loads = [pltpu.make_async_copy(k_hbm.at[j], stage.at[j], in_sem.at[j]) for j in range(4)]
    loads.append(pltpu.make_async_copy(g_hbm, stage.at[4], in_sem.at[4]))
    loads.append(pltpu.make_async_copy(b_hbm, stage.at[5], in_sem.at[5]))
    for c in loads:
        c.start()

    def peer(rel):
        return lax.rem(gx + rel // cy, cx), lax.rem(gy + rel % cy, cy)

    barrier = pltpu.get_barrier_semaphore()
    for rel in range(1, group):
        x, y = peer(rel)
        pl.semaphore_signal(barrier, inc=1, device_id={names[0]: x, names[1]: y}, device_id_type=MESH)

    @pl.when(has_low[2])
    def _():
        pl.semaphore_signal(barrier, inc=1, device_id={names[2]: gz - 1}, device_id_type=MESH)

    @pl.when(has_high[2])
    def _():
        pl.semaphore_signal(barrier, inc=1, device_id={names[2]: gz + 1}, device_id_type=MESH)

    @pl.when(jnp.logical_not(has_prev))
    def _():
        field[:, :, 0:near] = jnp.zeros((4, nx, near, LANES), jnp.float32)
        for g in range(3):
            x = fs[g].shape[1]
            fs[g][:, :, 0:nears[g]] = jnp.zeros((CYCLES, x, nears[g], LANES), jnp.float32)
        ex[:, :, 0:nears[2]] = jnp.zeros((CYCLES, nx, nears[2], LANES), jnp.float32)

    @pl.when(jnp.logical_not(has_next))
    def _():
        field[:, :, slab + near:] = jnp.zeros((4, nx, near, LANES), jnp.float32)
        for g in range(3):
            x, rows = fs[g].shape[1:3]
            fs[g][:, :, rows - nears[g]:] = jnp.zeros((CYCLES, x, nears[g], LANES), jnp.float32)
        ex[:, :, slab // 2 + nears[2]:] = jnp.zeros((CYCLES, nx, nears[2], LANES), jnp.float32)

    def lane_of(shape):
        return iota(shape, len(shape) - 1)

    tile_lane = lane_of((ny, LANES))

    def regroup(values):
        values = list(values)
        step = pieces // 2
        while step:
            width = slab * step
            low = lax.rem(tile_lane // width, 2) == 0
            for i in range(pieces):
                if i & step == 0:
                    a, c = values[i], values[i + step]
                    values[i] = jnp.where(low, a, pltpu.roll(c, width, 1))
                    values[i + step] = jnp.where(low, pltpu.roll(a, LANES - width, 1), c)
            step //= 2
        return values

    def pack(f):
        for xi in range(rows_of):
            for t in range(nz // LANES):
                parts = regroup(
                    [stage[5 if f == 4 else f, q * rows_of + xi, :, LANES * t:LANES * (t + 1)] for q in range(pieces)])
                for q in range(pieces):
                    sb[f, t * pieces + q, xi] = parts[q]

    def spread_copies(f):
        copies = []
        for rel in range(1, group):
            x, y = peer(rel)
            copies.append(pltpu.make_async_remote_copy(
                src_ref=sb.at[f, slab_of(x, y, gz)], dst_ref=rb.at[f, :, me],
                send_sem=send.at[f, rel], recv_sem=recv.at[f, rel],
                device_id={names[0]: x, names[1]: y}, device_id_type=MESH))
        return copies

    def z_copies(ref, own_low, own, halo, ssem, rsem):
        up = pltpu.make_async_remote_copy(
            src_ref=ref.at[:, pl.ds(own_low + own - halo, halo)], dst_ref=ref.at[:, pl.ds(own_low - halo, halo)],
            send_sem=ssem.at[0], recv_sem=rsem.at[0], device_id=next_id, device_id_type=MESH)
        down = pltpu.make_async_remote_copy(
            src_ref=ref.at[:, pl.ds(own_low, halo)], dst_ref=ref.at[:, pl.ds(own_low + own, halo)],
            send_sem=ssem.at[1], recv_sem=rsem.at[1], device_id=prev_id, device_id_type=MESH)
        return up, down

    def z_start(copies):
        up, down = copies

        @pl.when(has_next)
        def _():
            up.start()

        @pl.when(has_prev)
        def _():
            down.start()

    def z_finish(copies):
        up, down = copies

        @pl.when(has_prev)
        def _():
            up.wait_recv()

        @pl.when(has_next)
        def _():
            down.wait_recv()

        @pl.when(has_next)
        def _():
            up.wait_send()

        @pl.when(has_prev)
        def _():
            down.wait_send()

    for side in range(2):
        absent = [jnp.logical_not((has_low, has_high)[side][axis]) for axis in range(3)]

        @pl.when(absent[0])
        def _():
            hx[:, side] = jnp.zeros((2, ny, nz), jnp.float32)

        @pl.when(absent[1])
        def _():
            hyr[:, side] = jnp.zeros((2, nx, 1, nz), jnp.float32)

        @pl.when(absent[2])
        def _():
            hz[side] = jnp.zeros((ny, LANES), jnp.float32)

    faces = []
    for a in range(2):
        for axis in range(3 if a == 0 else 2):
            v = 4 if a == 0 else axis
            for side in range(2):
                src = (stage.at[v, (0, nx - 1)[side]], hys.at[a, side], hzs.at[side])[axis]
                dst = (hx.at[a, 1 - side], hyr.at[a, 1 - side], hz.at[1 - side])[axis]
                faces.append((
                    pltpu.make_async_remote_copy(
                        src_ref=src, dst_ref=dst, send_sem=hsend.at[a, axis, side], recv_sem=hrecv.at[a, axis, side],
                        device_id={names[axis]: place[axis] + (-1, 1)[side]}, device_id_type=MESH),
                    (has_low, has_high)[side][axis], (has_high, has_low)[side][axis]))

    for f in (4, 0, 1, 2):
        loads[f].wait()
    for a in range(2):
        for side in range(2):
            row = (0, ny - 1)[side]
            hys[a, side] = stage[4 if a == 0 else 1, :, row:row + 1, :]
    for side in range(2):
        edge = jnp.zeros((ny, LANES), jnp.float32)
        for a in range(2):
            for i in range(nx):
                v, to = 4 if a == 0 else 2, a * nx + i
                if side == 0:
                    rolled = pltpu.roll(stage[v, i, :, 0:LANES], to, 1) if to else stage[v, i, :, 0:LANES]
                else:
                    rolled = pltpu.roll(stage[v, i, :, nz - LANES:nz], to + 1, 1)
                edge = jnp.where(tile_lane == to, rolled, edge)
        hzs[side] = edge
    pl.semaphore_wait(barrier, group - 1 + jnp.where(has_low[2], 1, 0) + jnp.where(has_high[2], 1, 0))
    for c, goes, _ in faces:
        @pl.when(goes)
        def _():
            c.start()

    every = []

    def send_out(f):
        pack(f)
        copies = spread_copies(f)
        for c in copies:
            c.start()
        every.append(copies)
        rb[f, :, me] = sb[f, mine]

    for f in range(4):
        if f == 3:
            loads[3].wait()
        send_out(f)
    loads[5].wait()
    for c, goes, comes in faces:
        @pl.when(comes)
        def _():
            c.wait_recv()

    tile_row = iota((ny, LANES), 0)
    count_t = nz // LANES

    def home_shifts(f, a, i, axis):
        tiles_of = [stage[f, i, :, LANES * t:LANES * (t + 1)] for t in range(count_t)]
        if axis == 0:
            low = stage[f, i - 1] if i > 0 else hx[a, 0]
            high = stage[f, i + 1] if i < nx - 1 else hx[a, 1]
            cut = lambda v: [v[:, LANES * t:LANES * (t + 1)] for t in range(count_t)]
            return list(zip(cut(low), cut(high)))
        if axis == 1:
            found = []
            for t in range(count_t):
                at = slice(LANES * t, LANES * (t + 1))
                found.append((
                    jnp.where(tile_row == 0, hyr[a, 0, i, :, at], pltpu.roll(tiles_of[t], 1, 0)),
                    jnp.where(tile_row == ny - 1, hyr[a, 1, i, :, at], pltpu.roll(tiles_of[t], ny - 1, 0))))
            return found
        to = a * nx + i
        ups = [pltpu.roll(hz[0], LANES - to, 1) if to else hz[0]] + [pltpu.roll(v, 1, 1) for v in tiles_of]
        downs = [pltpu.roll(v, LANES - 1, 1) for v in tiles_of] + [pltpu.roll(hz[1], LANES - 1 - to, 1)]
        return [
            (jnp.where(tile_lane == 0, ups[t], ups[t + 1]),
             jnp.where(tile_lane == LANES - 1, downs[t + 1], downs[t])) for t in range(count_t)]

    for i in range(nx):
        around = [(home_shifts(4, 0, i, axis), home_shifts(axis, 1, i, axis)) for axis in range(3)]
        for t in range(count_t):
            at = slice(LANES * t, LANES * (t + 1))
            total = stage[3, i, :, at]
            pulled = stage[5, i, :, at]
            for axis in range(3):
                middle = stage[axis, i, :, at]
                for side in range(2):
                    w = 0.5 * (middle + around[axis][1][t][side])
                    total = total + w
                    pulled = pulled + w * around[axis][0][t][side]
            stage[5, i, :, at] = pulled - total * stage[4, i, :, at]

    def arrive(f):
        for c in every[f]:
            c.wait_recv()
        for xi in range(rows_of):
            turned = rb[f, xi].reshape((LANES, LANES)).T
            for q in range(pieces):
                part = turned[q * slab:(q + 1) * slab]
                x = q * rows_of + xi
                if f < 4:
                    field[f, x, near:near + slab] = part
                else:
                    bb[x] = part

    send_out(4)
    halos = []
    for f in range(4):
        arrive(f)
        halos.append(z_copies(field.at[f], near, slab, near, zsend.at[f], zrecv.at[f]))
        z_start(halos[-1])

    wide_rows = slab + 2 * near
    half = span // 2
    r, c = iota((2 * LANES, LANES), 0), iota((2 * LANES, LANES), 1)
    lane = lax.rem(r, LANES)
    y_mean = jnp.where(
        (r // LANES == lax.rem(c, span) // half) & (lane // span == c // span)
        & (lax.rem(lane, span) // 2 == lax.rem(c, half)), 0.5, 0.0).astype(jnp.bfloat16)
    r, c = iota((LANES, 2 * LANES), 0), iota((LANES, 2 * LANES), 1)
    lane = lax.rem(c, LANES)
    here = (c // LANES == lax.rem(r, span) // half) & (lane // span == r // span)
    fine_y = lax.rem(lane, span)
    main = fine_y // 2
    side = jnp.where(lax.rem(fine_y, 2) == 1, main + 1, main - 1)
    coarse_y = lax.rem(r, half)
    y_spread = jnp.where(
        here & (coarse_y == main), 0.75, jnp.where(here & (coarse_y == side), 0.25, 0.0)).astype(jnp.bfloat16)
    folds = nx // 2

    def fold_y(rows_low, rows_high):
        n = rows_low.shape[0] * rows_low.shape[1]
        both = jnp.concatenate([rows_low.reshape((n, LANES)), rows_high.reshape((n, LANES))], 1)
        return spread(both, y_mean).reshape(rows_low.shape)

    for f in range(4):
        z_finish(halos[f])
        factors = [0.25 if f == d else 1.0 for d in range(3)]
        for i in range(nx // 2):
            cells[0][f, i] = (0.5 * factors[0]) * (
                field[f, 2 * i] + field[f, 2 * i + 1])
        cells[1][f] = fold_y(
            field[f, 0:folds], field[f, folds:nx]) * factors[1]
        coarse_rows = slab // 2 + 2 * nears[2]
        for x in range(nx):
            cells[2][f, x] = (0.5 * factors[2]) * (
                field[f, x, pl.ds(0, coarse_rows, stride=2)] + field[f, x, pl.ds(1, coarse_rows, stride=2)])

    def masks(shape, width):
        lanes = lane_of(shape)
        y = lax.rem(lanes, width)
        return y != 0, y != width - 1, lanes >= width, lanes < LANES - width

    def x_pair(get, i, count, width):
        below = get(i - 1) if i > 0 else pltpu.roll(get(count - 1), width, 1)
        above = get(i + 1) if i < count - 1 else pltpu.roll(get(0), LANES - width, 1)
        return below, above

    def weights(k, i, count, width, z_pair):
        y_low, y_high, x_low, x_high = masks(k(3, i).shape, width)
        k0, k1, k2 = k(0, i), k(1, i), k(2, i)
        below, above = x_pair(lambda p: k(0, p), i, count, width)
        if i == 0:
            below = jnp.where(x_low, below, 0.0)
        if i == count - 1:
            above = jnp.where(x_high, above, 0.0)
        around = [
            (k0, below, x_low if i == 0 else None), (k0, above, x_high if i == count - 1 else None),
            (k1, jnp.where(y_low, pltpu.roll(k1, 1, 1), 0.0), y_low),
            (k1, jnp.where(y_high, pltpu.roll(k1, LANES - 1, 1), 0.0), y_high),
        ]
        around += [(k2, other, None) for other in z_pair]
        total = k(3, i)
        found = []
        for middle, other, keep in around:
            w = 0.5 * (middle + other)
            total = total + w
            found.append(w if keep is None else jnp.where(keep, w, 0.0))
        return found, total

    widths = (span, half, span)
    for g in range(3):
        count, rows = cells[g].shape[1:3]
        for i in range(count):
            k2 = cells[g][2, i]
            z_pair = (pltpu.roll(k2, 1, 0), pltpu.roll(k2, rows - 1, 0))
            w, total = weights(lambda j, p: cells[g][j, p], i, count, widths[g], z_pair)
            inside = cells[g][3, i] > 0.0
            scale = jnp.where(inside, relaxation / jnp.where(inside, total, 1.0), 0.0)
            ms[g][6, i] = scale
            for j in range(6):
                ms[g][j, i] = w[j] * scale
    own = slice(near, near + slab)
    for i in range(nx):
        z_pair = (field[2, i, near - 1:near + slab - 1], field[2, i, near + 1:near + slab + 1])
        w, total = weights(lambda j, p: field[j, p, own], i, nx, span, z_pair)
        for j in range(6):
            fw[j, i] = w[j]
        fw[6, i] = total

    arrive(4)

    pad = 8

    def plane(src, i, rows, shift=0):
        if len(src.shape) == 2:
            at = pad + i * rows + shift
            return src[at:at + rows]
        return pltpu.roll(src[i], -shift % rows, 0) if shift else src[i]

    for g in range(3):
        rows = es[g].shape[1]
        es[g][:, 0:pad] = jnp.zeros((2, pad, LANES), jnp.float32)
        es[g][:, rows - pad:] = jnp.zeros((2, pad, LANES), jnp.float32)

    def sweep(g, src, dst, inner=False):
        count, rows = fs[g].shape[1:3]
        m, f = ms[g], fs[g]
        for i in range(count):
            middle = plane(src, i, rows)
            below, above = x_pair(lambda p: plane(src, p, rows), i, count, widths[g])
            new = (1.0 - relaxation) * middle + f[cycle, i]
            new = new + m[0, i] * below
            new = new + m[1, i] * above
            new = new + m[2, i] * pltpu.roll(middle, 1, 1)
            new = new + m[3, i] * pltpu.roll(middle, LANES - 1, 1)
            new = new + m[4, i] * plane(src, i, rows, -1)
            new = new + m[5, i] * plane(src, i, rows, 1)
            if inner:
                dst[i, nears[g]:rows - nears[g]] = new[nears[g]:rows - nears[g]]
            else:
                dst[pad + i * rows:pad + (i + 1) * rows] = new

    for cycle in range(CYCLES):
        left = rr if cycle else bb
        for i in range(nx if cycle else 0):
            u = ub[i, near:near + slab]
            below, above = x_pair(lambda p: ub[p, near:near + slab], i, nx, span)
            residual = bb[i] - fw[6, i] * u
            residual = residual + fw[0, i] * below
            residual = residual + fw[1, i] * above
            residual = residual + fw[2, i] * pltpu.roll(u, 1, 1)
            residual = residual + fw[3, i] * pltpu.roll(u, LANES - 1, 1)
            residual = residual + fw[4, i] * ub[i, near - 1:near + slab - 1]
            residual = residual + fw[5, i] * ub[i, near + 1:near + slab + 1]
            rr[i] = residual
        moves = {}

        def send_first(g):
            rows = fs[g].shape[2]
            moves[g] = z_copies(
                fs[g].at[cycle], nears[g], rows - 2 * nears[g], nears[g], gsend.at[cycle, g], grecv.at[cycle, g])
            z_start(moves[g])

        low2, high2 = nears[2], nears[2] + slab // 2
        for x in range(nx):
            first = 0.5 * (left[x, pl.ds(0, slab // 2, stride=2)] + left[x, pl.ds(1, slab // 2, stride=2)])
            fs[2][cycle, x, low2:high2] = ms[2][6, x, low2:high2] * first
        send_first(2)
        for i in range(nx // 2):
            first = 0.5 * (left[2 * i] + left[2 * i + 1])
            fs[0][cycle, i, near:near + slab] = ms[0][6, i, near:near + slab] * first
        send_first(0)
        first = fold_y(left[0:folds], left[folds:nx])
        fs[1][cycle, :, near:near + slab] = ms[1][6, :, near:near + slab] * first
        send_first(1)

        z_finish(moves[2])
        src = fs[2].at[cycle]
        for repeat in range(nears[2] - 1):
            sweep(2, src, es[2].at[repeat % 2])
            src = es[2].at[repeat % 2]
        sweep(2, src, ex.at[cycle], True)
        middle_move = z_copies(ex.at[cycle], low2, slab // 2, low2, esend.at[cycle], erecv.at[cycle])
        z_start(middle_move)
        for g in range(2):
            z_finish(moves[g])
            sweep(g, fs[g].at[cycle], es[g].at[0])

        @pl.loop(0, SWEEPS - 2)
        def _(repeat):
            old = lax.rem(repeat, 2)
            for g in range(2):
                sweep(g, es[g].at[old], es[g].at[1 - old])

        last = (SWEEPS - 2) % 2
        z_finish(middle_move)
        src = ex.at[cycle]
        for repeat in range(SWEEPS - 1 - nears[2]):
            slot = (last + SWEEPS - nears[2] - repeat) % 2
            sweep(2, src, es[2].at[slot])
            src = es[2].at[slot]
        keep = wide_rows if cycle < CYCLES - 1 else slab
        low = 0 if cycle < CYCLES - 1 else near
        taken = slice(low, low + keep)
        lanes = lane_of((keep, LANES))
        e_of = [functools.partial(plane, es[g].at[last], rows=fs[g].shape[2]) for g in range(3)]
        e = jnp.concatenate([e_of[1](i)[taken] for i in range(folds)], 0)
        from_y = spread(e, y_spread)
        count = keep // 2
        for x in range(nx):
            middle, lower, upper = (e_of[2](x, shift=step)[low // 2:low // 2 + count] for step in (0, -1, 1))
            tmp[x, pl.ds(0, count, stride=2)] = 0.75 * middle + 0.25 * lower
            tmp[x, pl.ds(1, count, stride=2)] = 0.75 * middle + 0.25 * upper
        for i in range(nx // 2):
            middle = e_of[0](i)[taken]
            below, above = x_pair(lambda p: e_of[0](p)[taken], i, nx // 2, span)
            if i == 0:
                below = jnp.where(lanes >= span, below, 0.0)
            if i == nx // 2 - 1:
                above = jnp.where(lanes < LANES - span, above, 0.0)
            for odd, other in ((0, below), (1, above)):
                x = 2 * i + odd
                from_x = 0.75 * middle + 0.25 * other
                fold, xi = x // folds, x % folds
                mid_y = from_y[xi * keep:(xi + 1) * keep, LANES * fold:LANES * (fold + 1)]
                update = (from_x + mid_y) + tmp[x, 0:keep]
                ub[x, taken] = ub[x, taken] + blending * update if cycle else blending * update
        if cycle < CYCLES - 1:
            @pl.when(jnp.logical_not(has_prev))
            def _():
                ub[:, 0:near] = jnp.zeros((nx, near, LANES), jnp.float32)

            @pl.when(jnp.logical_not(has_next))
            def _():
                ub[:, slab + near:] = jnp.zeros((nx, near, LANES), jnp.float32)

    backs = []
    for xi in range(rows_of):
        block = jnp.concatenate([ub[q * rows_of + xi, near:near + slab] for q in range(pieces)], 0)
        turned = block.T
        for j in range(group):
            so[j, xi] = turned[j * ny:(j + 1) * ny]
    for rel in range(1, group):
        x, y = peer(rel)
        backs.append(pltpu.make_async_remote_copy(
            src_ref=so.at[x * cy + y], dst_ref=ro.at[mine], send_sem=osend.at[rel], recv_sem=orecv.at[rel],
            device_id={names[0]: x, names[1]: y}, device_id_type=MESH))
    for c in backs:
        c.start()
    ro[mine] = so[me]
    for c in backs:
        c.wait_recv()
    for xi in range(rows_of):
        for t in range(nz // LANES):
            parts = regroup([ro[t * pieces + q, xi] for q in range(pieces)])
            for q in range(pieces):
                x, at = q * rows_of + xi, slice(LANES * t, LANES * (t + 1))
                out_ref[x, :, at] = stage[4, x, :, at] + parts[q]
    for copies in every + [backs]:
        for c in copies:
            c.wait_send()
    for c, goes, _ in faces:
        @pl.when(goes)
        def _():
            c.wait_send()


def slab_fits(shape, counts):
    nx, ny, nz = shape
    cx, cy, _ = counts
    group = cx * cy
    if nz % group or ny * group != LANES or LANES % (2 * cx):
        return False
    slab = nz // group
    pieces = LANES // slab
    return (
        slab * pieces == LANES and pieces & (pieces - 1) == 0 and nx % (2 * pieces) == 0
        and slab % 16 == 0 and slab >= 2 * SWEEPS and nz % LANES == 0 and 2 * nx <= LANES)


def slab_body(names, counts, right_side, coefficients, first_guess):
    nx, ny, nz = right_side.shape
    f32 = jnp.float32
    vmem = lambda *shape: pltpu.VMEM(shape, f32)
    dma = pltpu.SemaphoreType.DMA
    group = counts[0] * counts[1]
    slab = nz // group
    rows_of = nx // (LANES // slab)
    near = SWEEPS
    wide = slab + 2 * near
    shapes = ((nx // 2, wide), (nx // 2, wide), (nx, slab // 2 + near))
    blocks = (group, rows_of, ny, LANES)
    scratch = [
        vmem(6, nx, ny, nz),
        vmem(5, *blocks),
        vmem(5, rows_of, group, ny, LANES),
        vmem(4, nx, wide, LANES),
        vmem(nx, wide, LANES),
        vmem(nx, slab, LANES),
        vmem(nx, slab, LANES),
        vmem(7, nx, slab, LANES),
        tuple(vmem(4, x, z, LANES) for x, z in shapes),
        tuple(vmem(7, x, z, LANES) for x, z in shapes),
        tuple(vmem(CYCLES, x, z, LANES) for x, z in shapes),
        tuple(vmem(2, x * z + 16, LANES) for x, z in shapes),
        vmem(nx, wide, LANES),
        vmem(*blocks),
        vmem(*blocks),
        vmem(2, 2, ny, nz), vmem(2, 2, nx, 1, nz), vmem(2, 2, nx, 1, nz), vmem(2, ny, LANES),
        vmem(2, ny, LANES), vmem(CYCLES, *shapes[2], LANES),
        dma((6,)), dma((5, group)), dma((5, group)), dma((4, 2)), dma((4, 2)),
        dma((CYCLES, 3, 2)), dma((CYCLES, 3, 2)), dma((group,)), dma((group,)),
        dma((2, 3, 2)), dma((2, 3, 2)), dma((CYCLES, 2)), dma((CYCLES, 2)),
    ]
    hbm = pl.BlockSpec(memory_space=pl.ANY)
    return pl.pallas_call(
        functools.partial(slab_kernel, (nx, ny, nz), counts, names),
        out_shape=jax.ShapeDtypeStruct(right_side.shape, f32),
        in_specs=[hbm] * 3,
        out_specs=pl.BlockSpec(memory_space=pltpu.VMEM),
        scratch_shapes=scratch,
        compiler_params=pltpu.CompilerParams(
            collective_id=0, has_side_effects=True, vmem_limit_bytes=60 * 1024 * 1024),
    )(right_side, coefficients, first_guess)


def solution(mesh):
    names = tuple(mesh.axis_names)
    counts = tuple(mesh.shape[n] for n in names)
    in_specs = (P(*names), P(None, *names), P(*names))

    def local(right_side, coefficients, first_guess):
        if slab_fits(right_side.shape, counts):
            return slab_body(names, counts, right_side, coefficients, first_guess)
        return body(names, right_side, coefficients, first_guess)

    return jax.shard_map(
        local, mesh=mesh, in_specs=in_specs, out_specs=P(*names), check_vma=False)
```

```python
import functools

import jax
import jax.numpy as jnp
from jax import lax
from jax.experimental import pallas as pl
from jax.experimental.pallas import tpu as pltpu
from jax.sharding import PartitionSpec as P

CYCLES = 2
SWEEPS = 8
REACH = 2 * (SWEEPS + 1)
STEP = 20
LANES = 128
CHUNK = 1

relaxation = 0.8
blending = 0.4
MESH = pl.DeviceIdType.MESH


def iota(shape, dim):
    return lax.broadcasted_iota(jnp.int32, shape, dim)


def spread(a, b):
    total = None
    for _ in range(3):
        part = a.astype(jnp.bfloat16)
        a = a - part.astype(jnp.float32)
        term = jnp.dot(part, b, preferred_element_type=jnp.float32)
        total = term if total is None else total + term
    return total


def kernel(sizes, names, b_ref, k_ref, g_ref, out_ref, *scratch):
    (fields, cells, tiles, es, yss, yrs, ms, fs, kxr, kys, kyr, zs, zr, us, ur,
     send, recv, ksend, krecv, zsend, zrecv) = scratch
    nx, ny, nz = sizes
    wide = nz + LANES
    shapes = ((nx // 2, ny, wide), (nx, ny // 2, wide), (nx, ny, nz // 2 + LANES), (nx, ny, wide))
    place = [lax.axis_index(n) for n in names]
    counts = [lax.axis_size(n) for n in names]
    has_low = [p > 0 for p in place]
    has_high = [p < c - 1 for p, c in zip(place, counts)]
    ways = []
    for axis in range(3):
        ways.append((axis, -1, has_low[axis], has_high[axis]))
        ways.append((axis, 1, has_high[axis], has_low[axis]))

    def target(way):
        axis, step = ways[way][:2]
        return {names[axis]: place[axis] + step}

    def copy(src, dst, ssem, rsem, way):
        return pltpu.make_async_remote_copy(
            src_ref=src, dst_ref=dst, send_sem=ssem, recv_sem=rsem,
            device_id=target(way), device_id_type=MESH,
        )

    def start(copies):
        for way, c in copies:
            @pl.when(ways[way][2])
            def _():
                c.start()

    def finish(copies):
        for way, c in copies:
            @pl.when(ways[way][3])
            def _():
                c.wait_recv()
        for way, c in copies:
            @pl.when(ways[way][2])
            def _():
                c.wait_send()

    def faces(g, slot, keep=(0, 1, 2, 3)):
        x = shapes[g][0]
        e, ys, yr = es[g], yss[g], yrs[g]
        ends = (
            (e.at[slot, 1], e.at[slot, x + 1]),
            (e.at[slot, x], e.at[slot, 0]),
            (ys.at[slot, 0], yr.at[slot, 1]),
            (ys.at[slot, 1], yr.at[slot, 0]),
        )
        return [
            (way, copy(*ends[way], send.at[g, way, slot], recv.at[g, way, slot], way)) for way in keep
        ]

    for g in range(4):
        x = shapes[g][0]
        for slot in range(2):
            zero = jnp.zeros(shapes[g][1:], jnp.float32)
            es[g][slot, 0] = zero
            es[g][slot, x + 1] = zero
        yrs[g][...] = jnp.zeros(yrs[g].shape, jnp.float32)
    kxr[...] = jnp.zeros(kxr.shape, jnp.float32)
    kyr[...] = jnp.zeros(kyr.shape, jnp.float32)
    zr[...] = jnp.zeros(zr.shape, jnp.float32)
    ur[...] = jnp.zeros(ur.shape, jnp.float32)

    barrier = pltpu.get_barrier_semaphore()
    for way in range(6):
        @pl.when(ways[way][2])
        def _():
            pl.semaphore_signal(barrier, inc=1, device_id=target(way), device_id_type=MESH)
    peers = sum(jnp.where(has, 1, 0) for has in has_low + has_high)
    pl.semaphore_wait(barrier, peers)

    lane = iota((nx, ny, LANES), 2)
    low = jnp.zeros((nx, ny, LANES), jnp.float32)
    high = low
    for j in range(6):
        if j < 4:
            first, last = k_ref[j, :, :, :LANES], k_ref[j, :, :, nz - LANES:]
        elif j == 4:
            first, last = g_ref[:, :, :LANES], g_ref[:, :, nz - LANES:]
        else:
            first, last = b_ref[:, :, :LANES], b_ref[:, :, nz - LANES:]
        here = (lane >= STEP * j) & (lane < STEP * j + REACH)
        low = jnp.where(here, pltpu.roll(first, STEP * j, 2) if j else first, low)
        high = jnp.where(here, pltpu.roll(last, (STEP * j + REACH) % LANES, 2), high)
    zs[0] = low
    zs[1] = high
    deep = [
        (4, copy(zs.at[0], zr.at[1], zsend.at[0], zrecv.at[0], 4)),
        (5, copy(zs.at[1], zr.at[0], zsend.at[1], zrecv.at[1], 5)),
    ]
    start(deep)
    for j in range(4):
        fields[j, :, :, :nz] = k_ref[j]
    fields[4, :, :, :nz] = b_ref[...]
    es[3][0, 1:nx + 1, :, :nz] = g_ref[...]
    finish(deep)
    above, below = zr[1], zr[0]

    def beside(j):
        up = pltpu.roll(above, (LANES - STEP * j) % LANES, 2) if j else above
        down = pltpu.roll(below, (2 * LANES - REACH - STEP * j) % LANES, 2)
        return jnp.where(lane < REACH, up, jnp.where(lane >= LANES - REACH, down, 0.0))

    for j in range(4):
        fields[j, :, :, nz:] = beside(j)
    es[3][0, 1:nx + 1, :, nz:] = beside(4)
    fields[4, :, :, nz:] = beside(5)

    def send_guess(slot):
        u = es[3][slot, 1:nx + 1]
        yss[3][slot, 0] = u[:, 0:1, :]
        yss[3][slot, 1] = u[:, ny - 1:ny, :]
        start(faces(3, slot))

    ky = fields[1]
    for row in range(2):
        kys[0, row] = ky[:, row:row + 1, :]
        kys[1, row] = ky[:, ny - 2 + row:ny - 1 + row, :]
    edges = [
        (0, copy(fields.at[0, pl.ds(0, 2)], kxr.at[1], ksend.at[0], krecv.at[0], 0)),
        (1, copy(fields.at[0, pl.ds(nx - 2, 2)], kxr.at[0], ksend.at[1], krecv.at[1], 1)),
        (2, copy(kys.at[0], kyr.at[1], ksend.at[2], krecv.at[2], 2)),
        (3, copy(kys.at[1], kyr.at[0], ksend.at[3], krecv.at[3], 3)),
    ]
    start(edges)
    send_guess(0)

    half = nz // 2
    r, c = iota((wide, half + LANES), 0), iota((wide, half + LANES), 1)
    home = jnp.where(
        r < nz, r // 2,
        jnp.where(r < nz + LANES // 2, half + (r - nz) // 2, half + LANES // 2 + (r - nz) // 2),
    )
    z_mean = jnp.where(home == c, 0.5, 0.0).astype(jnp.bfloat16)
    rows = nx * ny
    r, c = iota((half + LANES, nz), 0), iota((half + LANES, nz), 1)
    main = c // 2
    total = half + LANES
    side = jnp.where(c % 2 == 1, main + 1, jnp.where(main == 0, total - 1, main - 1))
    z_spread = (jnp.where(r == main, 0.75, 0.0) + jnp.where(r == side, 0.25, 0.0)).astype(jnp.bfloat16)

    count = wide // LANES
    even_rows, odd_rows = pl.ds(0, ny // 2, stride=2), pl.ds(1, ny // 2, stride=2)

    def put_tiles(planes, values):
        for t in range(values.shape[2] // LANES):
            tiles[t, planes] = values[:, :, LANES * t:LANES * (t + 1)]

    def get_tiles(planes, tiles_of=count):
        return jnp.concatenate([tiles[t, planes] for t in range(tiles_of)], 2)

    def y_mean(planes):
        return jnp.concatenate(
            [0.5 * (tiles[t, planes, even_rows] + tiles[t, planes, odd_rows]) for t in range(count)], 2)

    def chunks(x, step=CHUNK):
        return [slice(x0, x0 + step) for x0 in range(0, x, step)]

    def below_of(ref, planes, halo):
        if planes.start > 0:
            return ref[planes.start - 1:planes.stop - 1]
        return halo if planes.stop == 1 else jnp.concatenate([halo, ref[0:planes.stop - 1]], 0)

    def above_of(ref, planes, halo):
        if planes.stop < ref.shape[0]:
            return ref[planes.start + 1:planes.stop + 1]
        if planes.stop == planes.start + 1:
            return halo
        return jnp.concatenate([ref[planes.start + 1:planes.stop], halo], 0)

    def y_shift(values, halo_low, halo_high):
        y = values.shape[1]
        row = iota(values.shape, 1)
        lower = jnp.where(row == 0, halo_low, pltpu.roll(values, 1, 1))
        upper = jnp.where(row == y - 1, halo_high, pltpu.roll(values, y - 1, 1))
        return lower, upper

    def z_shift(values):
        return pltpu.roll(values, 1, 2), pltpu.roll(values, values.shape[2] - 1, 2)

    def face_weights(k, planes, near_x, near_y):
        k0, k1, k2 = k.at[0], k.at[1], k.at[2]
        m1, m2 = k1[planes], k2[planes]
        groups = (
            (k0[planes], (below_of(k0, planes, near_x[0]), above_of(k0, planes, near_x[1]))),
            (m1, y_shift(m1, near_y[0](planes), near_y[1](planes))),
            (m2, z_shift(m2)),
        )
        found = []
        total = k[3, planes]
        for middle, pair in groups:
            for other in pair:
                found.append(0.5 * (middle + other))
                total = total + found[-1]
        return found, total

    for j in range(4):
        for d in range(2):
            factor = 0.25 if j == d else 1.0
            if d == 0:
                for i in range(nx // 2):
                    cells[0][j, i] = (0.5 * factor) * (fields[j, 2 * i] + fields[j, 2 * i + 1])
            else:
                for planes in chunks(nx):
                    put_tiles(planes, fields[j, planes])
                for planes in chunks(nx):
                    cells[1][j, planes] = y_mean(planes) * factor
    for j in range(4):
        factor = 0.25 if j == 2 else 1.0
        for planes in chunks(nx, nx // 2):
            flat = fields[j, planes].reshape((rows // 2, wide))
            cells[2][j, planes] = (spread(flat, z_mean) * factor).reshape((nx // 2,) + shapes[2][1:])
    finish(edges)
    near_rows = [kxr[0, 1], kxr[1, 0]] + [kyr[0, 1].reshape((nx, wide)), kyr[1, 0].reshape((nx, wide))]
    edge = spread(jnp.concatenate(near_rows, 0), z_mean)
    edge_x = [edge[0:ny][None], edge[ny:2 * ny][None]]
    edge_y = [edge[2 * ny + nx * side:2 * ny + nx * (side + 1)].reshape((nx, 1, half + LANES)) for side in range(2)]
    put_tiles(slice(0, 2), jnp.stack([kxr[0, 1], kxr[1, 0]]))
    pair = y_mean(slice(0, 2))

    near_xs = (
        [0.125 * (kxr[side, 0:1] + kxr[side, 1:2]) for side in range(2)],
        [pair[0:1], pair[1:2]],
        edge_x,
    )

    def y_face(d, side):
        nearest = kyr.at[side, 1 - side]
        if d == 0:
            return lambda planes: jnp.concatenate(
                [0.5 * (nearest[2 * i:2 * i + 1] + nearest[2 * i + 1:2 * i + 2])
                 for i in range(planes.start, planes.stop)], 0)
        if d == 1:
            return lambda planes: 0.125 * (kyr[side, 0, planes] + kyr[side, 1, planes])
        if d == 2:
            return lambda planes: edge_y[side][planes]
        return lambda planes: nearest[planes]

    for d in range(3):
        for planes in chunks(shapes[d][0]):
            w, total_coarse = face_weights(
                cells[d], planes, near_xs[d], (y_face(d, 0), y_face(d, 1)))
            inside = cells[d][3, planes] > 0.0
            scale = jnp.where(inside, relaxation / jnp.where(inside, total_coarse, 1.0), 0.0)
            ms[d][6, planes] = scale
            for j in range(6):
                ms[d][j, planes] = w[j] * scale

    def sweep(g, slot, new_slot, keep=(0, 1, 2, 3)):
        e, yr, ys, m, f = es[g], yrs[g], yss[g], ms[g], fs[g]
        x, y, z = shapes[g]
        order = list(range(0, x, CHUNK))
        order = order[:1] + order[-1:] + order[1:-1]
        for x0 in order:
            planes = slice(x0, x0 + CHUNK)
            middle = e[slot, x0 + 1:x0 + 1 + CHUNK]
            y_low, y_high = y_shift(middle, yr[slot, 0, planes], yr[slot, 1, planes])
            z_low, z_high = z_shift(middle)
            new = (1.0 - relaxation) * middle + f[planes]
            new = new + m[0, planes] * e[slot, x0:x0 + CHUNK]
            new = new + m[1, planes] * e[slot, x0 + 2:x0 + 2 + CHUNK]
            new = new + m[2, planes] * y_low
            new = new + m[3, planes] * y_high
            new = new + m[4, planes] * z_low
            new = new + m[5, planes] * z_high
            e[new_slot, x0 + 1:x0 + 1 + CHUNK] = new
            ys[new_slot, 0, planes] = new[:, 0:1]
            ys[new_slot, 1, planes] = new[:, y - 1:y]
            if x0 == order[1] and 0 in keep:
                start(faces(g, new_slot, (0, 1)))
        if 2 in keep:
            start(faces(g, new_slot, (2, 3)))

    for cycle in range(CYCLES):
        slot = cycle % 2
        finish(faces(3, slot))
        u = es[3]
        for planes in chunks(nx):
            x0, x1 = planes.start, planes.stop
            middle = u[slot, x0 + 1:x1 + 1]
            y_low, y_high = y_shift(middle, yrs[3][slot, 0, planes], yrs[3][slot, 1, planes])
            z_low, z_high = z_shift(middle)
            w, total_fine = face_weights(
                fields, planes, (kxr[0, 1:2], kxr[1, 0:1]), (y_face(3, 0), y_face(3, 1)))
            residual = fields[4, planes] - total_fine * middle
            around = (u[slot, x0:x1], u[slot, x0 + 2:x1 + 2], y_low, y_high, z_low, z_high)
            for j in range(6):
                residual = residual + w[j] * around[j]
            put_tiles(planes, residual)
        for g in range(3):
            x, y, z = shapes[g]
            if g == 2:
                flat = get_tiles(slice(0, nx)).reshape((rows, wide))
                whole = spread(flat, z_mean).reshape(shapes[2])
            for planes in chunks(x):
                if g == 0:
                    pairs = [get_tiles(slice(2 * i, 2 * i + 2)) for i in range(planes.start, planes.stop)]
                    first = jnp.concatenate([0.5 * (p[0:1] + p[1:2]) for p in pairs], 0)
                elif g == 1:
                    first = y_mean(planes)
                else:
                    first = whole[planes]
                first = ms[g][6, planes] * first
                fs[g][planes] = first
                es[g][1, planes.start + 1:planes.stop + 1] = first
                yss[g][1, 0, planes] = first[:, 0:1]
                yss[g][1, 1, planes] = first[:, y - 1:y]
            start(faces(g, 1))

        @pl.loop(1, SWEEPS - 1)
        def _(repeat):
            old = lax.rem(repeat, 2)
            for g in range(3):
                finish(faces(g, old))
                sweep(g, old, 1 - old)

        last = SWEEPS % 2
        needed = ((0, 1), (2, 3), ())
        for g in range(3):
            finish(faces(g, 1 - last))
            sweep(g, 1 - last, last, needed[g])
        e = es[2][last, 1:nx + 1].reshape((rows, half + LANES))
        from_z = spread(e, z_spread).reshape((nx, ny, nz))
        finish(faces(1, last, needed[1]))
        for planes in chunks(nx):
            e = es[1][last, planes.start + 1:planes.stop + 1, :, :nz]
            y_low, y_high = y_shift(
                e, yrs[1][last, 0, planes, :, :nz], yrs[1][last, 1, planes, :, :nz])
            even = 0.75 * e + 0.25 * y_low
            odd = 0.75 * e + 0.25 * y_high
            for t in range(nz // LANES):
                tiles[t, planes, even_rows] = even[:, :, LANES * t:LANES * (t + 1)]
                tiles[t, planes, odd_rows] = odd[:, :, LANES * t:LANES * (t + 1)]
        finish(faces(0, last, needed[0]))
        for i in range(nx // 2):
            planes = slice(2 * i, 2 * i + 2)
            e = es[0][last, i:i + 3, :, :nz]
            even = 0.75 * e[1:2] + 0.25 * e[0:1]
            odd = 0.75 * e[1:2] + 0.25 * e[2:3]
            update = (jnp.concatenate([even, odd], 0) + get_tiles(planes, nz // LANES)) + from_z[planes]
            final = es[3][slot, 2 * i + 1:2 * i + 3, :, :nz] + blending * update
            if cycle == CYCLES - 1:
                out_ref[planes] = final
            else:
                es[3][1 - slot, 2 * i + 1:2 * i + 3, :, :nz] = final
        if cycle == CYCLES - 1:
            continue
        result = es[3].at[1 - slot, 1:nx + 1]
        per = LANES // STEP
        plane_lane = iota((ny, LANES), 1)
        groups = us.shape[1]
        for q in range(groups):
            low = jnp.zeros((ny, LANES), jnp.float32)
            high = low
            for p in range(min(per, nx - q * per)):
                here = (plane_lane >= STEP * p) & (plane_lane < STEP * p + REACH)
                first = result[q * per + p, :, :LANES]
                low = jnp.where(here, pltpu.roll(first, STEP * p, 1) if p else first, low)
                high = jnp.where(
                    here, pltpu.roll(result[q * per + p, :, nz - LANES:nz], (STEP * p + REACH) % LANES, 1), high)
            us[0, q] = low
            us[1, q] = high
        again = [
            (4, copy(us.at[0], ur.at[1], zsend.at[2], zrecv.at[2], 4)),
            (5, copy(us.at[1], ur.at[0], zsend.at[3], zrecv.at[3], 5)),
        ]
        start(again)
        finish(again)
        for i in range(nx):
            q, p = i // per, i % per
            up = pltpu.roll(ur[1, q], (LANES - STEP * p) % LANES, 1) if p else ur[1, q]
            down = pltpu.roll(ur[0, q], (2 * LANES - REACH - STEP * p) % LANES, 1)
            es[3][1 - slot, i + 1, :, nz:] = jnp.where(
                plane_lane < REACH, up, jnp.where(plane_lane >= LANES - REACH, down, 0.0))
        send_guess(1 - slot)


def body(names, right_side, coefficients, first_guess):
    nx, ny, nz = right_side.shape
    wide = nz + LANES
    shapes = ((nx // 2, ny, wide), (nx, ny // 2, wide), (nx, ny, nz // 2 + LANES), (nx, ny, wide))
    f32 = jnp.float32
    vmem = lambda *shape: pltpu.VMEM(shape, f32)
    dma = pltpu.SemaphoreType.DMA
    groups = -(-nx // (LANES // STEP))
    scratch = [
        vmem(5, nx, ny, wide),
        tuple(vmem(4, x, y, z) for x, y, z in shapes[:3]),
        vmem(wide // LANES, nx, ny, LANES),
        tuple(vmem(2, x + 2, y, z) for x, y, z in shapes),
        tuple(vmem(2, 2, x, 1, z) for x, y, z in shapes),
        tuple(vmem(2, 2, x, 1, z) for x, y, z in shapes),
        tuple(vmem(7, x, y, z) for x, y, z in shapes[:3]),
        tuple(vmem(x, y, z) for x, y, z in shapes[:3]),
        vmem(2, 2, ny, wide),
        vmem(2, 2, nx, 1, wide),
        vmem(2, 2, nx, 1, wide),
        vmem(2, nx, ny, LANES),
        vmem(2, nx, ny, LANES),
        vmem(2, groups, ny, LANES),
        vmem(2, groups, ny, LANES),
        dma((4, 4, 2)), dma((4, 4, 2)), dma((4,)), dma((4,)), dma((4,)), dma((4,)),
    ]
    spec = pl.BlockSpec(memory_space=pltpu.VMEM)
    return pl.pallas_call(
        functools.partial(kernel, (nx, ny, nz), names),
        out_shape=jax.ShapeDtypeStruct(right_side.shape, f32),
        in_specs=[spec] * 3,
        out_specs=spec,
        scratch_shapes=scratch,
        compiler_params=pltpu.CompilerParams(
            collective_id=0, has_side_effects=True, vmem_limit_bytes=60 * 1024 * 1024),
    )(right_side, coefficients, first_guess)


def slab_kernel(sizes, mesh_counts, names, b_hbm, k_hbm, g_hbm, out_ref, *scratch):
    (stage, sb, rb, field, ub, bb, rr, fw, cells, ms, fs, es, tmp, so, ro, hx, hys, hyr, hzs, hz, ex,
     in_sem, send, recv, zsend, zrecv, gsend, grecv, osend, orecv, hsend, hrecv, esend, erecv) = scratch
    nx, ny, nz = sizes
    cx, cy, cz = mesh_counts
    group = cx * cy
    slab = nz // group
    pieces = LANES // slab
    rows_of = nx // pieces
    near = SWEEPS
    nears = (near, near, near // 2)
    span = LANES // cx
    gx, gy, gz = (lax.axis_index(n) for n in names)
    me = gx * cy + gy

    def slab_of(x, y, z):
        p = x * cy + y + lax.rem(x, 2) * (cy - 1 - 2 * y)
        return p + lax.rem(z, 2) * (group - 1 - 2 * p)

    def device_of(s, z):
        p = s + lax.rem(z, 2) * (group - 1 - 2 * s)
        x, t = p // cy, lax.rem(p, cy)
        return x, t + lax.rem(x, 2) * (cy - 1 - 2 * t)

    mine = slab_of(gx, gy, gz)
    chain = gz * group + mine
    has_prev, has_next = chain > 0, chain < cz * group - 1

    def neighbour(step):
        c = chain + step
        c = jnp.clip(c, 0, cz * group - 1)
        z, s = c // group, lax.rem(c, group)
        x, y = device_of(s, z)
        return {names[0]: x, names[1]: y, names[2]: z}

    prev_id, next_id = neighbour(-1), neighbour(1)
    place, counts = (gx, gy, gz), (cx, cy, cz)
    has_low = [q > 0 for q in place]
    has_high = [q < c - 1 for q, c in zip(place, counts)]

    loads = [pltpu.make_async_copy(k_hbm.at[j], stage.at[j], in_sem.at[j]) for j in range(4)]
    loads.append(pltpu.make_async_copy(g_hbm, stage.at[4], in_sem.at[4]))
    loads.append(pltpu.make_async_copy(b_hbm, stage.at[5], in_sem.at[5]))
    order = (2, 0, 1, 3)
    for f in order + (4, 5):
        loads[f].start()

    def peer(rel):
        return lax.rem(gx + rel // cy, cx), lax.rem(gy + rel % cy, cy)

    barrier = pltpu.get_barrier_semaphore()
    for rel in range(1, group):
        x, y = peer(rel)
        pl.semaphore_signal(barrier, inc=1, device_id={names[0]: x, names[1]: y}, device_id_type=MESH)

    @pl.when(has_low[2])
    def _():
        pl.semaphore_signal(barrier, inc=1, device_id={names[2]: gz - 1}, device_id_type=MESH)

    @pl.when(has_high[2])
    def _():
        pl.semaphore_signal(barrier, inc=1, device_id={names[2]: gz + 1}, device_id_type=MESH)

    def lane_of(shape):
        return iota(shape, len(shape) - 1)

    tile_lane = lane_of((ny, LANES))

    def regroup(values):
        values = list(values)
        step = pieces // 2
        while step:
            width = slab * step
            low = lax.rem(tile_lane // width, 2) == 0
            for i in range(pieces):
                if i & step == 0:
                    a, c = values[i], values[i + step]
                    values[i] = jnp.where(low, a, pltpu.roll(c, width, 1))
                    values[i + step] = jnp.where(low, pltpu.roll(a, LANES - width, 1), c)
            step //= 2
        return values

    def pack(f):
        for xi in range(rows_of):
            for t in range(nz // LANES):
                parts = regroup(
                    [stage[5 if f == 4 else f, q * rows_of + xi, :, LANES * t:LANES * (t + 1)] for q in range(pieces)])
                for q in range(pieces):
                    sb[f, t * pieces + q, xi] = parts[q]

    def spread_copies(f):
        copies = []
        for rel in range(1, group):
            x, y = peer(rel)
            copies.append(pltpu.make_async_remote_copy(
                src_ref=sb.at[f, slab_of(x, y, gz)], dst_ref=rb.at[f, :, me],
                send_sem=send.at[f, rel], recv_sem=recv.at[f, rel],
                device_id={names[0]: x, names[1]: y}, device_id_type=MESH))
        return copies

    def z_copies(ref, own_low, own, halo, ssem, rsem):
        up = pltpu.make_async_remote_copy(
            src_ref=ref.at[:, pl.ds(own_low + own - halo, halo)], dst_ref=ref.at[:, pl.ds(own_low - halo, halo)],
            send_sem=ssem.at[0], recv_sem=rsem.at[0], device_id=next_id, device_id_type=MESH)
        down = pltpu.make_async_remote_copy(
            src_ref=ref.at[:, pl.ds(own_low, halo)], dst_ref=ref.at[:, pl.ds(own_low + own, halo)],
            send_sem=ssem.at[1], recv_sem=rsem.at[1], device_id=prev_id, device_id_type=MESH)
        return up, down

    def z_start(copies):
        up, down = copies

        @pl.when(has_next)
        def _():
            up.start()

        @pl.when(has_prev)
        def _():
            down.start()

    def z_finish(copies):
        up, down = copies

        @pl.when(has_prev)
        def _():
            up.wait_recv()

        @pl.when(has_next)
        def _():
            down.wait_recv()

        @pl.when(has_next)
        def _():
            up.wait_send()

        @pl.when(has_prev)
        def _():
            down.wait_send()

    faces = []
    for a in range(2):
        for axis in range(3 if a == 0 else 2):
            v = 4 if a == 0 else axis
            for side in range(2):
                src = (stage.at[v, (0, nx - 1)[side]], hys.at[a, side], hzs.at[side])[axis]
                dst = (hx.at[a, 1 - side], hyr.at[a, 1 - side], hz.at[1 - side])[axis]
                faces.append((
                    pltpu.make_async_remote_copy(
                        src_ref=src, dst_ref=dst, send_sem=hsend.at[a, axis, side], recv_sem=hrecv.at[a, axis, side],
                        device_id={names[axis]: place[axis] + (-1, 1)[side]}, device_id_type=MESH),
                    (has_low, has_high)[side][axis], (has_high, has_low)[side][axis]))

    every = {}

    def send_out(f):
        every[f] = spread_copies(f)
        for c in every[f]:
            c.start()
        rb[f, :, me] = sb[f, mine]

    loads[2].wait()
    pack(2)
    pl.semaphore_wait(barrier, group - 1 + jnp.where(has_low[2], 1, 0) + jnp.where(has_high[2], 1, 0))
    send_out(2)
    loads[0].wait()
    pack(0)
    send_out(0)
    loads[1].wait()
    loads[4].wait()
    for a in range(2):
        for side in range(2):
            row = (0, ny - 1)[side]
            hys[a, side] = stage[4 if a == 0 else 1, :, row:row + 1, :]
    for side in range(2):
        edge = jnp.zeros((ny, LANES), jnp.float32)
        for a in range(2):
            for i in range(nx):
                v, to = 4 if a == 0 else 2, a * nx + i
                if side == 0:
                    rolled = pltpu.roll(stage[v, i, :, 0:LANES], to, 1) if to else stage[v, i, :, 0:LANES]
                else:
                    rolled = pltpu.roll(stage[v, i, :, nz - LANES:nz], to + 1, 1)
                edge = jnp.where(tile_lane == to, rolled, edge)
        hzs[side] = edge
    for c, goes, _ in faces:
        @pl.when(goes)
        def _():
            c.start()

    pack(1)
    send_out(1)
    loads[3].wait()
    pack(3)
    send_out(3)
    loads[5].wait()

    for side in range(2):
        absent = [jnp.logical_not((has_low, has_high)[side][axis]) for axis in range(3)]

        @pl.when(absent[0])
        def _():
            hx[:, side] = jnp.zeros((2, ny, nz), jnp.float32)

        @pl.when(absent[1])
        def _():
            hyr[:, side] = jnp.zeros((2, nx, 1, nz), jnp.float32)

        @pl.when(absent[2])
        def _():
            hz[side] = jnp.zeros((ny, LANES), jnp.float32)

    @pl.when(jnp.logical_not(has_prev))
    def _():
        field[:, :, 0:near] = jnp.zeros((4, nx, near, LANES), jnp.float32)
        for g in range(3):
            x = fs[g].shape[1]
            fs[g][:, :, 0:nears[g]] = jnp.zeros((CYCLES, x, nears[g], LANES), jnp.float32)
        ex[:, :, 0:nears[2]] = jnp.zeros((CYCLES, nx, nears[2], LANES), jnp.float32)

    @pl.when(jnp.logical_not(has_next))
    def _():
        field[:, :, slab + near:] = jnp.zeros((4, nx, near, LANES), jnp.float32)
        for g in range(3):
            x, rows = fs[g].shape[1:3]
            fs[g][:, :, rows - nears[g]:] = jnp.zeros((CYCLES, x, nears[g], LANES), jnp.float32)
        ex[:, :, slab // 2 + nears[2]:] = jnp.zeros((CYCLES, nx, nears[2], LANES), jnp.float32)

    tile_row = iota((ny, LANES), 0)
    count_t = nz // LANES

    def home_shifts(f, a, i, axis):
        tiles_of = [stage[f, i, :, LANES * t:LANES * (t + 1)] for t in range(count_t)]
        if axis == 0:
            low = stage[f, i - 1] if i > 0 else hx[a, 0]
            high = stage[f, i + 1] if i < nx - 1 else hx[a, 1]
            cut = lambda v: [v[:, LANES * t:LANES * (t + 1)] for t in range(count_t)]
            return list(zip(cut(low), cut(high)))
        if axis == 1:
            found = []
            for t in range(count_t):
                at = slice(LANES * t, LANES * (t + 1))
                found.append((
                    jnp.where(tile_row == 0, hyr[a, 0, i, :, at], pltpu.roll(tiles_of[t], 1, 0)),
                    jnp.where(tile_row == ny - 1, hyr[a, 1, i, :, at], pltpu.roll(tiles_of[t], ny - 1, 0))))
            return found
        to = a * nx + i
        ups = [pltpu.roll(hz[0], LANES - to, 1) if to else hz[0]] + [pltpu.roll(v, 1, 1) for v in tiles_of]
        downs = [pltpu.roll(v, LANES - 1, 1) for v in tiles_of] + [pltpu.roll(hz[1], LANES - 1 - to, 1)]
        return [
            (jnp.where(tile_lane == 0, ups[t], ups[t + 1]),
             jnp.where(tile_lane == LANES - 1, downs[t + 1], downs[t])) for t in range(count_t)]

    def arrive(f):
        for c in every[f]:
            c.wait_recv()
        for xi in range(rows_of):
            turned = rb[f, xi].reshape((LANES, LANES)).T
            for q in range(pieces):
                part = turned[q * slab:(q + 1) * slab]
                x = q * rows_of + xi
                if f < 4:
                    field[f, x, near:near + slab] = part
                else:
                    bb[x] = part

    halos = {}

    def take(f):
        arrive(f)
        halos[f] = z_copies(field.at[f], near, slab, near, zsend.at[f], zrecv.at[f])
        z_start(halos[f])

    take(2)
    for c, goes, comes in faces:
        @pl.when(comes)
        def _():
            c.wait_recv()
    for i in range(nx):
        around = [(home_shifts(4, 0, i, axis), home_shifts(axis, 1, i, axis)) for axis in range(3)]
        for t in range(count_t):
            at = slice(LANES * t, LANES * (t + 1))
            total = stage[3, i, :, at]
            pulled = stage[5, i, :, at]
            for axis in range(3):
                middle = stage[axis, i, :, at]
                for side in range(2):
                    w = 0.5 * (middle + around[axis][1][t][side])
                    total = total + w
                    pulled = pulled + w * around[axis][0][t][side]
            stage[5, i, :, at] = pulled - total * stage[4, i, :, at]

    pack(4)
    send_out(4)

    wide_rows = slab + 2 * near
    half = span // 2
    r, c = iota((2 * LANES, LANES), 0), iota((2 * LANES, LANES), 1)
    lane = lax.rem(r, LANES)
    y_mean = jnp.where(
        (r // LANES == lax.rem(c, span) // half) & (lane // span == c // span)
        & (lax.rem(lane, span) // 2 == lax.rem(c, half)), 0.5, 0.0).astype(jnp.bfloat16)
    r, c = iota((LANES, 2 * LANES), 0), iota((LANES, 2 * LANES), 1)
    lane = lax.rem(c, LANES)
    here = (c // LANES == lax.rem(r, span) // half) & (lane // span == r // span)
    fine_y = lax.rem(lane, span)
    main = fine_y // 2
    side = jnp.where(lax.rem(fine_y, 2) == 1, main + 1, main - 1)
    coarse_y = lax.rem(r, half)
    y_spread = jnp.where(
        here & (coarse_y == main), 0.75, jnp.where(here & (coarse_y == side), 0.25, 0.0)).astype(jnp.bfloat16)
    folds = nx // 2

    def fold_y(rows_low, rows_high):
        n = rows_low.shape[0] * rows_low.shape[1]
        both = jnp.concatenate([rows_low.reshape((n, LANES)), rows_high.reshape((n, LANES))], 1)
        return spread(both, y_mean).reshape(rows_low.shape)

    def coarsen(f, low, high):
        factors = [0.25 if f == d else 1.0 for d in range(3)]
        for i in range(nx // 2):
            cells[0][f, i, low:high] = (0.5 * factors[0]) * (field[f, 2 * i, low:high] + field[f, 2 * i + 1, low:high])
        cells[1][f, :, low:high] = fold_y(field[f, 0:folds, low:high], field[f, folds:nx, low:high]) * factors[1]
        n = (high - low) // 2
        for x in range(nx):
            cells[2][f, x, low // 2:high // 2] = (0.5 * factors[2]) * (
                field[f, x, pl.ds(low, n, stride=2)] + field[f, x, pl.ds(low + 1, n, stride=2)])

    def take_halo(f):
        z_finish(halos[f])
        coarsen(f, 0, near)
        coarsen(f, near + slab, wide_rows)

    coarsen(2, near, near + slab)
    for f in order[1:]:
        take(f)
        coarsen(f, near, near + slab)
    take_halo(2)

    def masks(shape, width):
        lanes = lane_of(shape)
        y = lax.rem(lanes, width)
        return y != 0, y != width - 1, lanes >= width, lanes < LANES - width

    def x_pair(get, i, count, width):
        below = get(i - 1) if i > 0 else pltpu.roll(get(count - 1), width, 1)
        above = get(i + 1) if i < count - 1 else pltpu.roll(get(0), LANES - width, 1)
        return below, above

    def weights(k, i, count, width, z_pair):
        y_low, y_high, x_low, x_high = masks(k(3, i).shape, width)
        k0, k1, k2 = k(0, i), k(1, i), k(2, i)
        below, above = x_pair(lambda p: k(0, p), i, count, width)
        if i == 0:
            below = jnp.where(x_low, below, 0.0)
        if i == count - 1:
            above = jnp.where(x_high, above, 0.0)
        around = [
            (k0, below, x_low if i == 0 else None), (k0, above, x_high if i == count - 1 else None),
            (k1, jnp.where(y_low, pltpu.roll(k1, 1, 1), 0.0), y_low),
            (k1, jnp.where(y_high, pltpu.roll(k1, LANES - 1, 1), 0.0), y_high),
        ]
        around += [(k2, other, None) for other in z_pair]
        total = k(3, i)
        found = []
        for middle, other, keep in around:
            w = 0.5 * (middle + other)
            total = total + w
            found.append(w if keep is None else jnp.where(keep, w, 0.0))
        return found, total

    widths = (span, half, span)
    for g in range(3):
        count, rows = cells[g].shape[1:3]
        at = slice(nears[g], rows - nears[g])
        for i in range(count):
            z_pair = [cells[g][2, i, at.start + step:at.stop + step] for step in (-1, 1)]
            _, total = weights(lambda j, p: cells[g][j, p, at], i, count, widths[g], z_pair)
            ms[g][6, i, at] = relaxation / total
    own = slice(near, near + slab)
    for i in range(nx):
        z_pair = (field[2, i, near - 1:near + slab - 1], field[2, i, near + 1:near + slab + 1])
        w, total = weights(lambda j, p: field[j, p, own], i, nx, span, z_pair)
        for j in range(6):
            fw[j, i] = w[j]
        fw[6, i] = total

    def restrict(cycle, left):
        moves = {}

        def send_first(g):
            rows = fs[g].shape[2]
            moves[g] = z_copies(
                fs[g].at[cycle], nears[g], rows - 2 * nears[g], nears[g], gsend.at[cycle, g], grecv.at[cycle, g])
            z_start(moves[g])

        low2, high2 = nears[2], nears[2] + slab // 2
        for x in range(nx):
            first = 0.5 * (left[x, pl.ds(0, slab // 2, stride=2)] + left[x, pl.ds(1, slab // 2, stride=2)])
            fs[2][cycle, x, low2:high2] = ms[2][6, x, low2:high2] * first
        send_first(2)
        for i in range(nx // 2):
            first = 0.5 * (left[2 * i] + left[2 * i + 1])
            fs[0][cycle, i, near:near + slab] = ms[0][6, i, near:near + slab] * first
        send_first(0)
        first = fold_y(left[0:folds], left[folds:nx])
        fs[1][cycle, :, near:near + slab] = ms[1][6, :, near:near + slab] * first
        send_first(1)
        return moves

    take_halo(0)
    take_halo(1)
    arrive(4)
    first_moves = restrict(0, bb)
    take_halo(3)
    for g in range(3):
        count, rows = cells[g].shape[1:3]
        for i in range(count):
            k2 = cells[g][2, i]
            z_pair = (pltpu.roll(k2, 1, 0), pltpu.roll(k2, rows - 1, 0))
            w, total = weights(lambda j, p: cells[g][j, p], i, count, widths[g], z_pair)
            inside = cells[g][3, i] > 0.0
            scale = jnp.where(inside, relaxation / jnp.where(inside, total, 1.0), 0.0)
            ms[g][6, i] = scale
            for j in range(6):
                ms[g][j, i] = w[j] * scale
    low2 = nears[2]
    pad = 8

    def plane(src, i, rows, shift=0):
        if len(src.shape) == 2:
            at = pad + i * rows + shift
            return src[at:at + rows]
        return pltpu.roll(src[i], -shift % rows, 0) if shift else src[i]

    for g in range(3):
        rows = es[g].shape[1]
        es[g][:, 0:pad] = jnp.zeros((2, pad, LANES), jnp.float32)
        es[g][:, rows - pad:] = jnp.zeros((2, pad, LANES), jnp.float32)

    def sweep(g, src, dst, inner=False):
        count, rows = fs[g].shape[1:3]
        m, f = ms[g], fs[g]
        for i in range(count):
            middle = plane(src, i, rows)
            below, above = x_pair(lambda p: plane(src, p, rows), i, count, widths[g])
            new = (1.0 - relaxation) * middle + f[cycle, i]
            new = new + m[0, i] * below
            new = new + m[1, i] * above
            new = new + m[2, i] * pltpu.roll(middle, 1, 1)
            new = new + m[3, i] * pltpu.roll(middle, LANES - 1, 1)
            new = new + m[4, i] * plane(src, i, rows, -1)
            new = new + m[5, i] * plane(src, i, rows, 1)
            if inner:
                dst[i, nears[g]:rows - nears[g]] = new[nears[g]:rows - nears[g]]
            else:
                dst[pad + i * rows:pad + (i + 1) * rows] = new

    backs = []

    def give_back(xi):
        block = jnp.concatenate([ub[q * rows_of + xi, near:near + slab] for q in range(pieces)], 0)
        turned = block.T
        for j in range(group):
            so[j, xi] = turned[j * ny:(j + 1) * ny]
        copies = []
        for rel in range(1, group):
            x, y = peer(rel)
            copies.append(pltpu.make_async_remote_copy(
                src_ref=so.at[x * cy + y, xi], dst_ref=ro.at[mine, xi], send_sem=osend.at[rel, xi],
                recv_sem=orecv.at[rel, xi], device_id={names[0]: x, names[1]: y}, device_id_type=MESH))
        for c in copies:
            c.start()
        backs.append(copies)
        ro[mine, xi] = so[me, xi]

    for cycle in range(CYCLES):
        for i in range(nx if cycle else 0):
            u = ub[i, near:near + slab]
            below, above = x_pair(lambda p: ub[p, near:near + slab], i, nx, span)
            residual = bb[i] - fw[6, i] * u
            residual = residual + fw[0, i] * below
            residual = residual + fw[1, i] * above
            residual = residual + fw[2, i] * pltpu.roll(u, 1, 1)
            residual = residual + fw[3, i] * pltpu.roll(u, LANES - 1, 1)
            residual = residual + fw[4, i] * ub[i, near - 1:near + slab - 1]
            residual = residual + fw[5, i] * ub[i, near + 1:near + slab + 1]
            rr[i] = residual
        moves = first_moves if cycle == 0 else restrict(cycle, rr)
        z_finish(moves[2])
        src = fs[2].at[cycle]
        for repeat in range(nears[2] - 1):
            sweep(2, src, es[2].at[repeat % 2])
            src = es[2].at[repeat % 2]
        sweep(2, src, ex.at[cycle], True)
        middle_move = z_copies(ex.at[cycle], low2, slab // 2, low2, esend.at[cycle], erecv.at[cycle])
        z_start(middle_move)
        for g in range(2):
            z_finish(moves[g])
            sweep(g, fs[g].at[cycle], es[g].at[0])

        @pl.loop(0, SWEEPS - 2)
        def _(repeat):
            old = lax.rem(repeat, 2)
            for g in range(2):
                sweep(g, es[g].at[old], es[g].at[1 - old])

        last = (SWEEPS - 2) % 2
        z_finish(middle_move)
        src = ex.at[cycle]
        for repeat in range(SWEEPS - 1 - nears[2]):
            slot = (last + SWEEPS - nears[2] - repeat) % 2
            sweep(2, src, es[2].at[slot])
            src = es[2].at[slot]
        keep = wide_rows if cycle < CYCLES - 1 else slab
        low = 0 if cycle < CYCLES - 1 else near
        taken = slice(low, low + keep)
        lanes = lane_of((keep, LANES))
        e_of = [functools.partial(plane, es[g].at[last], rows=fs[g].shape[2]) for g in range(3)]
        e = jnp.concatenate([e_of[1](i)[taken] for i in range(folds)], 0)
        from_y = spread(e, y_spread)
        count = keep // 2
        for x in range(nx):
            middle, lower, upper = (e_of[2](x, shift=step)[low // 2:low // 2 + count] for step in (0, -1, 1))
            tmp[x, pl.ds(0, count, stride=2)] = 0.75 * middle + 0.25 * lower
            tmp[x, pl.ds(1, count, stride=2)] = 0.75 * middle + 0.25 * upper
        for x in range(nx) if cycle < CYCLES - 1 else [q * rows_of + xi for xi in range(rows_of) for q in range(pieces)]:
            i, odd = x // 2, x % 2
            middle = e_of[0](i)[taken]
            other = x_pair(lambda p: e_of[0](p)[taken], i, nx // 2, span)[odd]
            if x == 0:
                other = jnp.where(lanes >= span, other, 0.0)
            if x == nx - 1:
                other = jnp.where(lanes < LANES - span, other, 0.0)
            from_x = 0.75 * middle + 0.25 * other
            fold, xi = x // folds, x % folds
            mid_y = from_y[xi * keep:(xi + 1) * keep, LANES * fold:LANES * (fold + 1)]
            update = blending * ((from_x + mid_y) + tmp[x, 0:keep])
            ub[x, taken] = ub[x, taken] + update if cycle else update
            if cycle == CYCLES - 1 and x // rows_of == pieces - 1:
                give_back(x % rows_of)
        if cycle < CYCLES - 1:
            @pl.when(jnp.logical_not(has_prev))
            def _():
                ub[:, 0:near] = jnp.zeros((nx, near, LANES), jnp.float32)

            @pl.when(jnp.logical_not(has_next))
            def _():
                ub[:, slab + near:] = jnp.zeros((nx, near, LANES), jnp.float32)

    for xi in range(rows_of):
        for c in backs[xi]:
            c.wait_recv()
        for t in range(nz // LANES):
            parts = regroup([ro[t * pieces + q, xi] for q in range(pieces)])
            for q in range(pieces):
                x, at = q * rows_of + xi, slice(LANES * t, LANES * (t + 1))
                out_ref[x, :, at] = stage[4, x, :, at] + parts[q]
    for copies in list(every.values()) + backs:
        for c in copies:
            c.wait_send()
    for c, goes, _ in faces:
        @pl.when(goes)
        def _():
            c.wait_send()


def slab_fits(shape, counts):
    nx, ny, nz = shape
    cx, cy, _ = counts
    group = cx * cy
    if nz % group or ny * group != LANES or LANES % (2 * cx):
        return False
    slab = nz // group
    pieces = LANES // slab
    return (
        slab * pieces == LANES and pieces & (pieces - 1) == 0 and nx % (2 * pieces) == 0
        and slab % 16 == 0 and slab >= 2 * SWEEPS and nz % LANES == 0 and 2 * nx <= LANES)


def slab_body(names, counts, right_side, coefficients, first_guess):
    nx, ny, nz = right_side.shape
    f32 = jnp.float32
    vmem = lambda *shape: pltpu.VMEM(shape, f32)
    dma = pltpu.SemaphoreType.DMA
    group = counts[0] * counts[1]
    slab = nz // group
    rows_of = nx // (LANES // slab)
    near = SWEEPS
    wide = slab + 2 * near
    shapes = ((nx // 2, wide), (nx // 2, wide), (nx, slab // 2 + near))
    blocks = (group, rows_of, ny, LANES)
    scratch = [
        vmem(6, nx, ny, nz),
        vmem(5, *blocks),
        vmem(5, rows_of, group, ny, LANES),
        vmem(4, nx, wide, LANES),
        vmem(nx, wide, LANES),
        vmem(nx, slab, LANES),
        vmem(nx, slab, LANES),
        vmem(7, nx, slab, LANES),
        tuple(vmem(4, x, z, LANES) for x, z in shapes),
        tuple(vmem(7, x, z, LANES) for x, z in shapes),
        tuple(vmem(CYCLES, x, z, LANES) for x, z in shapes),
        tuple(vmem(2, x * z + 16, LANES) for x, z in shapes),
        vmem(nx, wide, LANES),
        vmem(*blocks),
        vmem(*blocks),
        vmem(2, 2, ny, nz), vmem(2, 2, nx, 1, nz), vmem(2, 2, nx, 1, nz), vmem(2, ny, LANES),
        vmem(2, ny, LANES), vmem(CYCLES, *shapes[2], LANES),
        dma((6,)), dma((5, group)), dma((5, group)), dma((4, 2)), dma((4, 2)),
        dma((CYCLES, 3, 2)), dma((CYCLES, 3, 2)), dma((group, rows_of)), dma((group, rows_of)),
        dma((2, 3, 2)), dma((2, 3, 2)), dma((CYCLES, 2)), dma((CYCLES, 2)),
    ]
    hbm = pl.BlockSpec(memory_space=pl.ANY)
    return pl.pallas_call(
        functools.partial(slab_kernel, (nx, ny, nz), counts, names),
        out_shape=jax.ShapeDtypeStruct(right_side.shape, f32),
        in_specs=[hbm] * 3,
        out_specs=pl.BlockSpec(memory_space=pltpu.VMEM),
        scratch_shapes=scratch,
        compiler_params=pltpu.CompilerParams(
            collective_id=0, has_side_effects=True, vmem_limit_bytes=60 * 1024 * 1024),
    )(right_side, coefficients, first_guess)


def solution(mesh):
    names = tuple(mesh.axis_names)
    counts = tuple(mesh.shape[n] for n in names)
    in_specs = (P(*names), P(None, *names), P(*names))

    def local(right_side, coefficients, first_guess):
        if slab_fits(right_side.shape, counts):
            return slab_body(names, counts, right_side, coefficients, first_guess)
        return body(names, right_side, coefficients, first_guess)

    return jax.shard_map(
        local, mesh=mesh, in_specs=in_specs, out_specs=P(*names), check_vma=False)
```

```python
import functools

import jax
import jax.numpy as jnp
from jax import lax
from jax.experimental import pallas as pl
from jax.experimental.pallas import tpu as pltpu
from jax.sharding import PartitionSpec as P

CYCLES = 2
SWEEPS = 8
REACH = 2 * (SWEEPS + 1)
STEP = 20
LANES = 128
CHUNK = 1

relaxation = 0.8
blending = 0.4
MESH = pl.DeviceIdType.MESH


def iota(shape, dim):
    return lax.broadcasted_iota(jnp.int32, shape, dim)


def spread(a, b):
    total = None
    for _ in range(3):
        part = a.astype(jnp.bfloat16)
        a = a - part.astype(jnp.float32)
        term = jnp.dot(part, b, preferred_element_type=jnp.float32)
        total = term if total is None else total + term
    return total


def kernel(sizes, names, b_ref, k_ref, g_ref, out_ref, *scratch):
    (fields, cells, tiles, es, yss, yrs, ms, fs, kxr, kys, kyr, zs, zr, us, ur,
     send, recv, ksend, krecv, zsend, zrecv) = scratch
    nx, ny, nz = sizes
    wide = nz + LANES
    shapes = ((nx // 2, ny, wide), (nx, ny // 2, wide), (nx, ny, nz // 2 + LANES), (nx, ny, wide))
    place = [lax.axis_index(n) for n in names]
    counts = [lax.axis_size(n) for n in names]
    has_low = [p > 0 for p in place]
    has_high = [p < c - 1 for p, c in zip(place, counts)]
    ways = []
    for axis in range(3):
        ways.append((axis, -1, has_low[axis], has_high[axis]))
        ways.append((axis, 1, has_high[axis], has_low[axis]))

    def target(way):
        axis, step = ways[way][:2]
        return {names[axis]: place[axis] + step}

    def copy(src, dst, ssem, rsem, way):
        return pltpu.make_async_remote_copy(
            src_ref=src, dst_ref=dst, send_sem=ssem, recv_sem=rsem,
            device_id=target(way), device_id_type=MESH,
        )

    def start(copies):
        for way, c in copies:
            @pl.when(ways[way][2])
            def _():
                c.start()

    def finish(copies):
        for way, c in copies:
            @pl.when(ways[way][3])
            def _():
                c.wait_recv()
        for way, c in copies:
            @pl.when(ways[way][2])
            def _():
                c.wait_send()

    def faces(g, slot, keep=(0, 1, 2, 3)):
        x = shapes[g][0]
        e, ys, yr = es[g], yss[g], yrs[g]
        ends = (
            (e.at[slot, 1], e.at[slot, x + 1]),
            (e.at[slot, x], e.at[slot, 0]),
            (ys.at[slot, 0], yr.at[slot, 1]),
            (ys.at[slot, 1], yr.at[slot, 0]),
        )
        return [
            (way, copy(*ends[way], send.at[g, way, slot], recv.at[g, way, slot], way)) for way in keep
        ]

    for g in range(4):
        x = shapes[g][0]
        for slot in range(2):
            zero = jnp.zeros(shapes[g][1:], jnp.float32)
            es[g][slot, 0] = zero
            es[g][slot, x + 1] = zero
        yrs[g][...] = jnp.zeros(yrs[g].shape, jnp.float32)
    kxr[...] = jnp.zeros(kxr.shape, jnp.float32)
    kyr[...] = jnp.zeros(kyr.shape, jnp.float32)
    zr[...] = jnp.zeros(zr.shape, jnp.float32)
    ur[...] = jnp.zeros(ur.shape, jnp.float32)

    barrier = pltpu.get_barrier_semaphore()
    for way in range(6):
        @pl.when(ways[way][2])
        def _():
            pl.semaphore_signal(barrier, inc=1, device_id=target(way), device_id_type=MESH)
    peers = sum(jnp.where(has, 1, 0) for has in has_low + has_high)
    pl.semaphore_wait(barrier, peers)

    lane = iota((nx, ny, LANES), 2)
    low = jnp.zeros((nx, ny, LANES), jnp.float32)
    high = low
    for j in range(6):
        if j < 4:
            first, last = k_ref[j, :, :, :LANES], k_ref[j, :, :, nz - LANES:]
        elif j == 4:
            first, last = g_ref[:, :, :LANES], g_ref[:, :, nz - LANES:]
        else:
            first, last = b_ref[:, :, :LANES], b_ref[:, :, nz - LANES:]
        here = (lane >= STEP * j) & (lane < STEP * j + REACH)
        low = jnp.where(here, pltpu.roll(first, STEP * j, 2) if j else first, low)
        high = jnp.where(here, pltpu.roll(last, (STEP * j + REACH) % LANES, 2), high)
    zs[0] = low
    zs[1] = high
    deep = [
        (4, copy(zs.at[0], zr.at[1], zsend.at[0], zrecv.at[0], 4)),
        (5, copy(zs.at[1], zr.at[0], zsend.at[1], zrecv.at[1], 5)),
    ]
    start(deep)
    for j in range(4):
        fields[j, :, :, :nz] = k_ref[j]
    fields[4, :, :, :nz] = b_ref[...]
    es[3][0, 1:nx + 1, :, :nz] = g_ref[...]
    finish(deep)
    above, below = zr[1], zr[0]

    def beside(j):
        up = pltpu.roll(above, (LANES - STEP * j) % LANES, 2) if j else above
        down = pltpu.roll(below, (2 * LANES - REACH - STEP * j) % LANES, 2)
        return jnp.where(lane < REACH, up, jnp.where(lane >= LANES - REACH, down, 0.0))

    for j in range(4):
        fields[j, :, :, nz:] = beside(j)
    es[3][0, 1:nx + 1, :, nz:] = beside(4)
    fields[4, :, :, nz:] = beside(5)

    def send_guess(slot):
        u = es[3][slot, 1:nx + 1]
        yss[3][slot, 0] = u[:, 0:1, :]
        yss[3][slot, 1] = u[:, ny - 1:ny, :]
        start(faces(3, slot))

    ky = fields[1]
    for row in range(2):
        kys[0, row] = ky[:, row:row + 1, :]
        kys[1, row] = ky[:, ny - 2 + row:ny - 1 + row, :]
    edges = [
        (0, copy(fields.at[0, pl.ds(0, 2)], kxr.at[1], ksend.at[0], krecv.at[0], 0)),
        (1, copy(fields.at[0, pl.ds(nx - 2, 2)], kxr.at[0], ksend.at[1], krecv.at[1], 1)),
        (2, copy(kys.at[0], kyr.at[1], ksend.at[2], krecv.at[2], 2)),
        (3, copy(kys.at[1], kyr.at[0], ksend.at[3], krecv.at[3], 3)),
    ]
    start(edges)
    send_guess(0)

    half = nz // 2
    r, c = iota((wide, half + LANES), 0), iota((wide, half + LANES), 1)
    home = jnp.where(
        r < nz, r // 2,
        jnp.where(r < nz + LANES // 2, half + (r - nz) // 2, half + LANES // 2 + (r - nz) // 2),
    )
    z_mean = jnp.where(home == c, 0.5, 0.0).astype(jnp.bfloat16)
    rows = nx * ny
    r, c = iota((half + LANES, nz), 0), iota((half + LANES, nz), 1)
    main = c // 2
    total = half + LANES
    side = jnp.where(c % 2 == 1, main + 1, jnp.where(main == 0, total - 1, main - 1))
    z_spread = (jnp.where(r == main, 0.75, 0.0) + jnp.where(r == side, 0.25, 0.0)).astype(jnp.bfloat16)

    count = wide // LANES
    even_rows, odd_rows = pl.ds(0, ny // 2, stride=2), pl.ds(1, ny // 2, stride=2)

    def put_tiles(planes, values):
        for t in range(values.shape[2] // LANES):
            tiles[t, planes] = values[:, :, LANES * t:LANES * (t + 1)]

    def get_tiles(planes, tiles_of=count):
        return jnp.concatenate([tiles[t, planes] for t in range(tiles_of)], 2)

    def y_mean(planes):
        return jnp.concatenate(
            [0.5 * (tiles[t, planes, even_rows] + tiles[t, planes, odd_rows]) for t in range(count)], 2)

    def chunks(x, step=CHUNK):
        return [slice(x0, x0 + step) for x0 in range(0, x, step)]

    def below_of(ref, planes, halo):
        if planes.start > 0:
            return ref[planes.start - 1:planes.stop - 1]
        return halo if planes.stop == 1 else jnp.concatenate([halo, ref[0:planes.stop - 1]], 0)

    def above_of(ref, planes, halo):
        if planes.stop < ref.shape[0]:
            return ref[planes.start + 1:planes.stop + 1]
        if planes.stop == planes.start + 1:
            return halo
        return jnp.concatenate([ref[planes.start + 1:planes.stop], halo], 0)

    def y_shift(values, halo_low, halo_high):
        y = values.shape[1]
        row = iota(values.shape, 1)
        lower = jnp.where(row == 0, halo_low, pltpu.roll(values, 1, 1))
        upper = jnp.where(row == y - 1, halo_high, pltpu.roll(values, y - 1, 1))
        return lower, upper

    def z_shift(values):
        return pltpu.roll(values, 1, 2), pltpu.roll(values, values.shape[2] - 1, 2)

    def face_weights(k, planes, near_x, near_y):
        k0, k1, k2 = k.at[0], k.at[1], k.at[2]
        m1, m2 = k1[planes], k2[planes]
        groups = (
            (k0[planes], (below_of(k0, planes, near_x[0]), above_of(k0, planes, near_x[1]))),
            (m1, y_shift(m1, near_y[0](planes), near_y[1](planes))),
            (m2, z_shift(m2)),
        )
        found = []
        total = k[3, planes]
        for middle, pair in groups:
            for other in pair:
                found.append(0.5 * (middle + other))
                total = total + found[-1]
        return found, total

    for j in range(4):
        for d in range(2):
            factor = 0.25 if j == d else 1.0
            if d == 0:
                for i in range(nx // 2):
                    cells[0][j, i] = (0.5 * factor) * (fields[j, 2 * i] + fields[j, 2 * i + 1])
            else:
                for planes in chunks(nx):
                    put_tiles(planes, fields[j, planes])
                for planes in chunks(nx):
                    cells[1][j, planes] = y_mean(planes) * factor
    for j in range(4):
        factor = 0.25 if j == 2 else 1.0
        for planes in chunks(nx, nx // 2):
            flat = fields[j, planes].reshape((rows // 2, wide))
            cells[2][j, planes] = (spread(flat, z_mean) * factor).reshape((nx // 2,) + shapes[2][1:])
    finish(edges)
    near_rows = [kxr[0, 1], kxr[1, 0]] + [kyr[0, 1].reshape((nx, wide)), kyr[1, 0].reshape((nx, wide))]
    edge = spread(jnp.concatenate(near_rows, 0), z_mean)
    edge_x = [edge[0:ny][None], edge[ny:2 * ny][None]]
    edge_y = [edge[2 * ny + nx * side:2 * ny + nx * (side + 1)].reshape((nx, 1, half + LANES)) for side in range(2)]
    put_tiles(slice(0, 2), jnp.stack([kxr[0, 1], kxr[1, 0]]))
    pair = y_mean(slice(0, 2))

    near_xs = (
        [0.125 * (kxr[side, 0:1] + kxr[side, 1:2]) for side in range(2)],
        [pair[0:1], pair[1:2]],
        edge_x,
    )

    def y_face(d, side):
        nearest = kyr.at[side, 1 - side]
        if d == 0:
            return lambda planes: jnp.concatenate(
                [0.5 * (nearest[2 * i:2 * i + 1] + nearest[2 * i + 1:2 * i + 2])
                 for i in range(planes.start, planes.stop)], 0)
        if d == 1:
            return lambda planes: 0.125 * (kyr[side, 0, planes] + kyr[side, 1, planes])
        if d == 2:
            return lambda planes: edge_y[side][planes]
        return lambda planes: nearest[planes]

    for d in range(3):
        for planes in chunks(shapes[d][0]):
            w, total_coarse = face_weights(
                cells[d], planes, near_xs[d], (y_face(d, 0), y_face(d, 1)))
            inside = cells[d][3, planes] > 0.0
            scale = jnp.where(inside, relaxation / jnp.where(inside, total_coarse, 1.0), 0.0)
            ms[d][6, planes] = scale
            for j in range(6):
                ms[d][j, planes] = w[j] * scale

    def sweep(g, slot, new_slot, keep=(0, 1, 2, 3)):
        e, yr, ys, m, f = es[g], yrs[g], yss[g], ms[g], fs[g]
        x, y, z = shapes[g]
        order = list(range(0, x, CHUNK))
        order = order[:1] + order[-1:] + order[1:-1]
        for x0 in order:
            planes = slice(x0, x0 + CHUNK)
            middle = e[slot, x0 + 1:x0 + 1 + CHUNK]
            y_low, y_high = y_shift(middle, yr[slot, 0, planes], yr[slot, 1, planes])
            z_low, z_high = z_shift(middle)
            new = (1.0 - relaxation) * middle + f[planes]
            new = new + m[0, planes] * e[slot, x0:x0 + CHUNK]
            new = new + m[1, planes] * e[slot, x0 + 2:x0 + 2 + CHUNK]
            new = new + m[2, planes] * y_low
            new = new + m[3, planes] * y_high
            new = new + m[4, planes] * z_low
            new = new + m[5, planes] * z_high
            e[new_slot, x0 + 1:x0 + 1 + CHUNK] = new
            ys[new_slot, 0, planes] = new[:, 0:1]
            ys[new_slot, 1, planes] = new[:, y - 1:y]
            if x0 == order[1] and 0 in keep:
                start(faces(g, new_slot, (0, 1)))
        if 2 in keep:
            start(faces(g, new_slot, (2, 3)))

    for cycle in range(CYCLES):
        slot = cycle % 2
        finish(faces(3, slot))
        u = es[3]
        for planes in chunks(nx):
            x0, x1 = planes.start, planes.stop
            middle = u[slot, x0 + 1:x1 + 1]
            y_low, y_high = y_shift(middle, yrs[3][slot, 0, planes], yrs[3][slot, 1, planes])
            z_low, z_high = z_shift(middle)
            w, total_fine = face_weights(
                fields, planes, (kxr[0, 1:2], kxr[1, 0:1]), (y_face(3, 0), y_face(3, 1)))
            residual = fields[4, planes] - total_fine * middle
            around = (u[slot, x0:x1], u[slot, x0 + 2:x1 + 2], y_low, y_high, z_low, z_high)
            for j in range(6):
                residual = residual + w[j] * around[j]
            put_tiles(planes, residual)
        for g in range(3):
            x, y, z = shapes[g]
            if g == 2:
                flat = get_tiles(slice(0, nx)).reshape((rows, wide))
                whole = spread(flat, z_mean).reshape(shapes[2])
            for planes in chunks(x):
                if g == 0:
                    pairs = [get_tiles(slice(2 * i, 2 * i + 2)) for i in range(planes.start, planes.stop)]
                    first = jnp.concatenate([0.5 * (p[0:1] + p[1:2]) for p in pairs], 0)
                elif g == 1:
                    first = y_mean(planes)
                else:
                    first = whole[planes]
                first = ms[g][6, planes] * first
                fs[g][planes] = first
                es[g][1, planes.start + 1:planes.stop + 1] = first
                yss[g][1, 0, planes] = first[:, 0:1]
                yss[g][1, 1, planes] = first[:, y - 1:y]
            start(faces(g, 1))

        @pl.loop(1, SWEEPS - 1)
        def _(repeat):
            old = lax.rem(repeat, 2)
            for g in range(3):
                finish(faces(g, old))
                sweep(g, old, 1 - old)

        last = SWEEPS % 2
        needed = ((0, 1), (2, 3), ())
        for g in range(3):
            finish(faces(g, 1 - last))
            sweep(g, 1 - last, last, needed[g])
        e = es[2][last, 1:nx + 1].reshape((rows, half + LANES))
        from_z = spread(e, z_spread).reshape((nx, ny, nz))
        finish(faces(1, last, needed[1]))
        for planes in chunks(nx):
            e = es[1][last, planes.start + 1:planes.stop + 1, :, :nz]
            y_low, y_high = y_shift(
                e, yrs[1][last, 0, planes, :, :nz], yrs[1][last, 1, planes, :, :nz])
            even = 0.75 * e + 0.25 * y_low
            odd = 0.75 * e + 0.25 * y_high
            for t in range(nz // LANES):
                tiles[t, planes, even_rows] = even[:, :, LANES * t:LANES * (t + 1)]
                tiles[t, planes, odd_rows] = odd[:, :, LANES * t:LANES * (t + 1)]
        finish(faces(0, last, needed[0]))
        for i in range(nx // 2):
            planes = slice(2 * i, 2 * i + 2)
            e = es[0][last, i:i + 3, :, :nz]
            even = 0.75 * e[1:2] + 0.25 * e[0:1]
            odd = 0.75 * e[1:2] + 0.25 * e[2:3]
            update = (jnp.concatenate([even, odd], 0) + get_tiles(planes, nz // LANES)) + from_z[planes]
            final = es[3][slot, 2 * i + 1:2 * i + 3, :, :nz] + blending * update
            if cycle == CYCLES - 1:
                out_ref[planes] = final
            else:
                es[3][1 - slot, 2 * i + 1:2 * i + 3, :, :nz] = final
        if cycle == CYCLES - 1:
            continue
        result = es[3].at[1 - slot, 1:nx + 1]
        per = LANES // STEP
        plane_lane = iota((ny, LANES), 1)
        groups = us.shape[1]
        for q in range(groups):
            low = jnp.zeros((ny, LANES), jnp.float32)
            high = low
            for p in range(min(per, nx - q * per)):
                here = (plane_lane >= STEP * p) & (plane_lane < STEP * p + REACH)
                first = result[q * per + p, :, :LANES]
                low = jnp.where(here, pltpu.roll(first, STEP * p, 1) if p else first, low)
                high = jnp.where(
                    here, pltpu.roll(result[q * per + p, :, nz - LANES:nz], (STEP * p + REACH) % LANES, 1), high)
            us[0, q] = low
            us[1, q] = high
        again = [
            (4, copy(us.at[0], ur.at[1], zsend.at[2], zrecv.at[2], 4)),
            (5, copy(us.at[1], ur.at[0], zsend.at[3], zrecv.at[3], 5)),
        ]
        start(again)
        finish(again)
        for i in range(nx):
            q, p = i // per, i % per
            up = pltpu.roll(ur[1, q], (LANES - STEP * p) % LANES, 1) if p else ur[1, q]
            down = pltpu.roll(ur[0, q], (2 * LANES - REACH - STEP * p) % LANES, 1)
            es[3][1 - slot, i + 1, :, nz:] = jnp.where(
                plane_lane < REACH, up, jnp.where(plane_lane >= LANES - REACH, down, 0.0))
        send_guess(1 - slot)


def body(names, right_side, coefficients, first_guess):
    nx, ny, nz = right_side.shape
    wide = nz + LANES
    shapes = ((nx // 2, ny, wide), (nx, ny // 2, wide), (nx, ny, nz // 2 + LANES), (nx, ny, wide))
    f32 = jnp.float32
    vmem = lambda *shape: pltpu.VMEM(shape, f32)
    dma = pltpu.SemaphoreType.DMA
    groups = -(-nx // (LANES // STEP))
    scratch = [
        vmem(5, nx, ny, wide),
        tuple(vmem(4, x, y, z) for x, y, z in shapes[:3]),
        vmem(wide // LANES, nx, ny, LANES),
        tuple(vmem(2, x + 2, y, z) for x, y, z in shapes),
        tuple(vmem(2, 2, x, 1, z) for x, y, z in shapes),
        tuple(vmem(2, 2, x, 1, z) for x, y, z in shapes),
        tuple(vmem(7, x, y, z) for x, y, z in shapes[:3]),
        tuple(vmem(x, y, z) for x, y, z in shapes[:3]),
        vmem(2, 2, ny, wide),
        vmem(2, 2, nx, 1, wide),
        vmem(2, 2, nx, 1, wide),
        vmem(2, nx, ny, LANES),
        vmem(2, nx, ny, LANES),
        vmem(2, groups, ny, LANES),
        vmem(2, groups, ny, LANES),
        dma((4, 4, 2)), dma((4, 4, 2)), dma((4,)), dma((4,)), dma((4,)), dma((4,)),
    ]
    spec = pl.BlockSpec(memory_space=pltpu.VMEM)
    return pl.pallas_call(
        functools.partial(kernel, (nx, ny, nz), names),
        out_shape=jax.ShapeDtypeStruct(right_side.shape, f32),
        in_specs=[spec] * 3,
        out_specs=spec,
        scratch_shapes=scratch,
        compiler_params=pltpu.CompilerParams(
            collective_id=0, has_side_effects=True, vmem_limit_bytes=60 * 1024 * 1024),
    )(right_side, coefficients, first_guess)


def slab_kernel(sizes, mesh_counts, names, b_hbm, k_hbm, g_hbm, out_ref, *scratch):
    (stage, sb, rb, field, ub, bb, rr, fw, cells, ms, fs, es, tmp, so, ro, hx, hys, hyr, hzs, hz, ex,
     in_sem, send, recv, zsend, zrecv, gsend, grecv, osend, orecv, hsend, hrecv, esend, erecv) = scratch
    nx, ny, nz = sizes
    cx, cy, cz = mesh_counts
    group = cx * cy
    slab = nz // group
    pieces = LANES // slab
    rows_of = nx // pieces
    near = SWEEPS
    nears = (near, near, near // 2)
    span = LANES // cx
    gx, gy, gz = (lax.axis_index(n) for n in names)
    me = gx * cy + gy

    def slab_of(x, y, z):
        p = x * cy + y + lax.rem(x, 2) * (cy - 1 - 2 * y)
        return p + lax.rem(z, 2) * (group - 1 - 2 * p)

    def device_of(s, z):
        p = s + lax.rem(z, 2) * (group - 1 - 2 * s)
        x, t = p // cy, lax.rem(p, cy)
        return x, t + lax.rem(x, 2) * (cy - 1 - 2 * t)

    mine = slab_of(gx, gy, gz)
    chain = gz * group + mine
    has_prev, has_next = chain > 0, chain < cz * group - 1

    def neighbour(step):
        c = chain + step
        c = jnp.clip(c, 0, cz * group - 1)
        z, s = c // group, lax.rem(c, group)
        x, y = device_of(s, z)
        return {names[0]: x, names[1]: y, names[2]: z}

    prev_id, next_id = neighbour(-1), neighbour(1)
    place, counts = (gx, gy, gz), (cx, cy, cz)
    has_low = [q > 0 for q in place]
    has_high = [q < c - 1 for q, c in zip(place, counts)]

    loads = [pltpu.make_async_copy(k_hbm.at[j], stage.at[j], in_sem.at[j]) for j in range(4)]
    loads.append(pltpu.make_async_copy(g_hbm, stage.at[4], in_sem.at[4]))
    loads.append(pltpu.make_async_copy(b_hbm, stage.at[5], in_sem.at[5]))
    order = (2, 0, 1, 3)
    for f in order + (4, 5):
        loads[f].start()

    def peer(rel):
        return lax.rem(gx + rel // cy, cx), lax.rem(gy + rel % cy, cy)

    barrier = pltpu.get_barrier_semaphore()
    for rel in range(1, group):
        x, y = peer(rel)
        pl.semaphore_signal(barrier, inc=1, device_id={names[0]: x, names[1]: y}, device_id_type=MESH)

    @pl.when(has_low[2])
    def _():
        pl.semaphore_signal(barrier, inc=1, device_id={names[2]: gz - 1}, device_id_type=MESH)

    @pl.when(has_high[2])
    def _():
        pl.semaphore_signal(barrier, inc=1, device_id={names[2]: gz + 1}, device_id_type=MESH)

    def lane_of(shape):
        return iota(shape, len(shape) - 1)

    tile_lane = lane_of((ny, LANES))

    def regroup(values):
        values = list(values)
        step = pieces // 2
        while step:
            width = slab * step
            low = lax.rem(tile_lane // width, 2) == 0
            for i in range(pieces):
                if i & step == 0:
                    a, c = values[i], values[i + step]
                    values[i] = jnp.where(low, a, pltpu.roll(c, width, 1))
                    values[i + step] = jnp.where(low, pltpu.roll(a, LANES - width, 1), c)
            step //= 2
        return values

    def pack(f):
        for xi in range(rows_of):
            for t in range(nz // LANES):
                parts = regroup(
                    [stage[5 if f == 4 else f, q * rows_of + xi, :, LANES * t:LANES * (t + 1)] for q in range(pieces)])
                for q in range(pieces):
                    sb[f, t * pieces + q, xi] = parts[q]

    def spread_copies(f):
        copies = []
        for rel in range(1, group):
            x, y = peer(rel)
            copies.append(pltpu.make_async_remote_copy(
                src_ref=sb.at[f, slab_of(x, y, gz)], dst_ref=rb.at[f, :, me],
                send_sem=send.at[f, rel], recv_sem=recv.at[f, rel],
                device_id={names[0]: x, names[1]: y}, device_id_type=MESH))
        return copies

    def z_copies(ref, own_low, own, halo, ssem, rsem):
        up = pltpu.make_async_remote_copy(
            src_ref=ref.at[:, pl.ds(own_low + own - halo, halo)], dst_ref=ref.at[:, pl.ds(own_low - halo, halo)],
            send_sem=ssem.at[0], recv_sem=rsem.at[0], device_id=next_id, device_id_type=MESH)
        down = pltpu.make_async_remote_copy(
            src_ref=ref.at[:, pl.ds(own_low, halo)], dst_ref=ref.at[:, pl.ds(own_low + own, halo)],
            send_sem=ssem.at[1], recv_sem=rsem.at[1], device_id=prev_id, device_id_type=MESH)
        return up, down

    def z_start(copies):
        up, down = copies

        @pl.when(has_next)
        def _():
            up.start()

        @pl.when(has_prev)
        def _():
            down.start()

    def z_finish(copies):
        up, down = copies

        @pl.when(has_prev)
        def _():
            up.wait_recv()

        @pl.when(has_next)
        def _():
            down.wait_recv()

        @pl.when(has_next)
        def _():
            up.wait_send()

        @pl.when(has_prev)
        def _():
            down.wait_send()

    faces = []
    for a in range(2):
        for axis in range(3 if a == 0 else 2):
            v = 4 if a == 0 else axis
            for side in range(2):
                src = (stage.at[v, (0, nx - 1)[side]], hys.at[a, side], hzs.at[side])[axis]
                dst = (hx.at[a, 1 - side], hyr.at[a, 1 - side], hz.at[1 - side])[axis]
                faces.append((
                    pltpu.make_async_remote_copy(
                        src_ref=src, dst_ref=dst, send_sem=hsend.at[a, axis, side], recv_sem=hrecv.at[a, axis, side],
                        device_id={names[axis]: place[axis] + (-1, 1)[side]}, device_id_type=MESH),
                    (has_low, has_high)[side][axis], (has_high, has_low)[side][axis]))

    every = {}

    def send_out(f):
        every[f] = spread_copies(f)
        for c in every[f]:
            c.start()
        rb[f, :, me] = sb[f, mine]

    loads[2].wait()
    pack(2)
    pl.semaphore_wait(barrier, group - 1 + jnp.where(has_low[2], 1, 0) + jnp.where(has_high[2], 1, 0))
    send_out(2)
    loads[0].wait()
    pack(0)
    send_out(0)
    loads[1].wait()
    loads[4].wait()
    for a in range(2):
        for side in range(2):
            row = (0, ny - 1)[side]
            hys[a, side] = stage[4 if a == 0 else 1, :, row:row + 1, :]
    for side in range(2):
        edge = jnp.zeros((ny, LANES), jnp.float32)
        for a in range(2):
            for i in range(nx):
                v, to = 4 if a == 0 else 2, a * nx + i
                if side == 0:
                    rolled = pltpu.roll(stage[v, i, :, 0:LANES], to, 1) if to else stage[v, i, :, 0:LANES]
                else:
                    rolled = pltpu.roll(stage[v, i, :, nz - LANES:nz], to + 1, 1)
                edge = jnp.where(tile_lane == to, rolled, edge)
        hzs[side] = edge
    for c, goes, _ in faces:
        @pl.when(goes)
        def _():
            c.start()

    pack(1)
    send_out(1)
    loads[3].wait()
    pack(3)
    send_out(3)
    loads[5].wait()

    for side in range(2):
        absent = [jnp.logical_not((has_low, has_high)[side][axis]) for axis in range(3)]

        @pl.when(absent[0])
        def _():
            hx[:, side] = jnp.zeros((2, ny, nz), jnp.float32)

        @pl.when(absent[1])
        def _():
            hyr[:, side] = jnp.zeros((2, nx, 1, nz), jnp.float32)

        @pl.when(absent[2])
        def _():
            hz[side] = jnp.zeros((ny, LANES), jnp.float32)

    @pl.when(jnp.logical_not(has_prev))
    def _():
        field[:, :, 0:near] = jnp.zeros((4, nx, near, LANES), jnp.float32)
        for g in range(3):
            x = fs[g].shape[1]
            fs[g][:, :, 0:nears[g]] = jnp.zeros((CYCLES, x, nears[g], LANES), jnp.float32)
        ex[:, :, 0:nears[2]] = jnp.zeros((CYCLES, nx, nears[2], LANES), jnp.float32)

    @pl.when(jnp.logical_not(has_next))
    def _():
        field[:, :, slab + near:] = jnp.zeros((4, nx, near, LANES), jnp.float32)
        for g in range(3):
            x, rows = fs[g].shape[1:3]
            fs[g][:, :, rows - nears[g]:] = jnp.zeros((CYCLES, x, nears[g], LANES), jnp.float32)
        ex[:, :, slab // 2 + nears[2]:] = jnp.zeros((CYCLES, nx, nears[2], LANES), jnp.float32)

    tile_row = iota((ny, LANES), 0)
    count_t = nz // LANES

    def home_shifts(f, a, i, axis):
        tiles_of = [stage[f, i, :, LANES * t:LANES * (t + 1)] for t in range(count_t)]
        if axis == 0:
            low = stage[f, i - 1] if i > 0 else hx[a, 0]
            high = stage[f, i + 1] if i < nx - 1 else hx[a, 1]
            cut = lambda v: [v[:, LANES * t:LANES * (t + 1)] for t in range(count_t)]
            return list(zip(cut(low), cut(high)))
        if axis == 1:
            found = []
            for t in range(count_t):
                at = slice(LANES * t, LANES * (t + 1))
                found.append((
                    jnp.where(tile_row == 0, hyr[a, 0, i, :, at], pltpu.roll(tiles_of[t], 1, 0)),
                    jnp.where(tile_row == ny - 1, hyr[a, 1, i, :, at], pltpu.roll(tiles_of[t], ny - 1, 0))))
            return found
        to = a * nx + i
        ups = [pltpu.roll(hz[0], LANES - to, 1) if to else hz[0]] + [pltpu.roll(v, 1, 1) for v in tiles_of]
        downs = [pltpu.roll(v, LANES - 1, 1) for v in tiles_of] + [pltpu.roll(hz[1], LANES - 1 - to, 1)]
        return [
            (jnp.where(tile_lane == 0, ups[t], ups[t + 1]),
             jnp.where(tile_lane == LANES - 1, downs[t + 1], downs[t])) for t in range(count_t)]

    def arrive(f):
        for c in every[f]:
            c.wait_recv()
        for xi in range(rows_of):
            turned = rb[f, xi].reshape((LANES, LANES)).T
            for q in range(pieces):
                part = turned[q * slab:(q + 1) * slab]
                x = q * rows_of + xi
                if f < 4:
                    field[f, x, near:near + slab] = part
                else:
                    bb[x] = part

    halos = {}

    def take(f):
        arrive(f)
        halos[f] = z_copies(field.at[f], near, slab, near, zsend.at[f], zrecv.at[f])
        z_start(halos[f])

    take(2)
    for c, goes, comes in faces:
        @pl.when(comes)
        def _():
            c.wait_recv()
    for i in range(nx):
        around = [(home_shifts(4, 0, i, axis), home_shifts(axis, 1, i, axis)) for axis in range(3)]
        for t in range(count_t):
            at = slice(LANES * t, LANES * (t + 1))
            total = stage[3, i, :, at]
            pulled = stage[5, i, :, at]
            for axis in range(3):
                middle = stage[axis, i, :, at]
                for side in range(2):
                    w = 0.5 * (middle + around[axis][1][t][side])
                    total = total + w
                    pulled = pulled + w * around[axis][0][t][side]
            stage[5, i, :, at] = pulled - total * stage[4, i, :, at]

    pack(4)
    send_out(4)

    wide_rows = slab + 2 * near
    half = span // 2
    r, c = iota((2 * LANES, LANES), 0), iota((2 * LANES, LANES), 1)
    lane = lax.rem(r, LANES)
    y_mean = jnp.where(
        (r // LANES == lax.rem(c, span) // half) & (lane // span == c // span)
        & (lax.rem(lane, span) // 2 == lax.rem(c, half)), 0.5, 0.0).astype(jnp.bfloat16)
    r, c = iota((LANES, 2 * LANES), 0), iota((LANES, 2 * LANES), 1)
    lane = lax.rem(c, LANES)
    here = (c // LANES == lax.rem(r, span) // half) & (lane // span == r // span)
    fine_y = lax.rem(lane, span)
    main = fine_y // 2
    side = jnp.where(lax.rem(fine_y, 2) == 1, main + 1, main - 1)
    coarse_y = lax.rem(r, half)
    y_spread = jnp.where(
        here & (coarse_y == main), 0.75, jnp.where(here & (coarse_y == side), 0.25, 0.0)).astype(jnp.bfloat16)
    folds = nx // 2

    def fold_y(rows_low, rows_high):
        n = rows_low.shape[0] * rows_low.shape[1]
        both = jnp.concatenate([rows_low.reshape((n, LANES)), rows_high.reshape((n, LANES))], 1)
        return spread(both, y_mean).reshape(rows_low.shape)

    def coarsen(f, low, high):
        factors = [0.25 if f == d else 1.0 for d in range(3)]
        for i in range(nx // 2):
            cells[0][f, i, low:high] = (0.5 * factors[0]) * (field[f, 2 * i, low:high] + field[f, 2 * i + 1, low:high])
        cells[1][f, :, low:high] = fold_y(field[f, 0:folds, low:high], field[f, folds:nx, low:high]) * factors[1]
        n = (high - low) // 2
        for x in range(nx):
            cells[2][f, x, low // 2:high // 2] = (0.5 * factors[2]) * (
                field[f, x, pl.ds(low, n, stride=2)] + field[f, x, pl.ds(low + 1, n, stride=2)])

    def take_halo(f):
        z_finish(halos[f])
        coarsen(f, 0, near)
        coarsen(f, near + slab, wide_rows)

    coarsen(2, near, near + slab)
    for f in order[1:]:
        take(f)
        coarsen(f, near, near + slab)
    take_halo(2)

    def masks(shape, width):
        lanes = lane_of(shape)
        y = lax.rem(lanes, width)
        return y != 0, y != width - 1, lanes >= width, lanes < LANES - width

    def x_pair(get, i, count, width):
        below = get(i - 1) if i > 0 else pltpu.roll(get(count - 1), width, 1)
        above = get(i + 1) if i < count - 1 else pltpu.roll(get(0), LANES - width, 1)
        return below, above

    def weights(k, i, count, width, z_pair):
        y_low, y_high, x_low, x_high = masks(k(3, i).shape, width)
        k0, k1, k2 = k(0, i), k(1, i), k(2, i)
        below, above = x_pair(lambda p: k(0, p), i, count, width)
        if i == 0:
            below = jnp.where(x_low, below, 0.0)
        if i == count - 1:
            above = jnp.where(x_high, above, 0.0)
        around = [
            (k0, below, x_low if i == 0 else None), (k0, above, x_high if i == count - 1 else None),
            (k1, jnp.where(y_low, pltpu.roll(k1, 1, 1), 0.0), y_low),
            (k1, jnp.where(y_high, pltpu.roll(k1, LANES - 1, 1), 0.0), y_high),
        ]
        around += [(k2, other, None) for other in z_pair]
        total = k(3, i)
        found = []
        for middle, other, keep in around:
            w = 0.5 * (middle + other)
            total = total + w
            found.append(w if keep is None else jnp.where(keep, w, 0.0))
        return found, total

    widths = (span, half, span)
    for g in range(3):
        count, rows = cells[g].shape[1:3]
        at = slice(nears[g], rows - nears[g])
        for i in range(count):
            z_pair = [cells[g][2, i, at.start + step:at.stop + step] for step in (-1, 1)]
            _, total = weights(lambda j, p: cells[g][j, p, at], i, count, widths[g], z_pair)
            ms[g][6, i, at] = relaxation / total
    own = slice(near, near + slab)
    for i in range(nx):
        z_pair = (field[2, i, near - 1:near + slab - 1], field[2, i, near + 1:near + slab + 1])
        w, total = weights(lambda j, p: field[j, p, own], i, nx, span, z_pair)
        for j in range(6):
            fw[j, i] = w[j]
        fw[6, i] = total

    def restrict(cycle, left):
        moves = {}

        def send_first(g):
            rows = fs[g].shape[2]
            moves[g] = z_copies(
                fs[g].at[cycle], nears[g], rows - 2 * nears[g], nears[g], gsend.at[cycle, g], grecv.at[cycle, g])
            z_start(moves[g])

        low2, high2 = nears[2], nears[2] + slab // 2
        for x in range(nx):
            first = 0.5 * (left[x, pl.ds(0, slab // 2, stride=2)] + left[x, pl.ds(1, slab // 2, stride=2)])
            fs[2][cycle, x, low2:high2] = ms[2][6, x, low2:high2] * first
        send_first(2)
        for i in range(nx // 2):
            first = 0.5 * (left[2 * i] + left[2 * i + 1])
            fs[0][cycle, i, near:near + slab] = ms[0][6, i, near:near + slab] * first
        send_first(0)
        first = fold_y(left[0:folds], left[folds:nx])
        fs[1][cycle, :, near:near + slab] = ms[1][6, :, near:near + slab] * first
        send_first(1)
        return moves

    take_halo(0)
    take_halo(1)
    arrive(4)
    first_moves = restrict(0, bb)
    take_halo(3)
    for g in range(3):
        count, rows = cells[g].shape[1:3]
        for i in range(count):
            k2 = cells[g][2, i]
            z_pair = (pltpu.roll(k2, 1, 0), pltpu.roll(k2, rows - 1, 0))
            w, total = weights(lambda j, p: cells[g][j, p], i, count, widths[g], z_pair)
            inside = cells[g][3, i] > 0.0
            scale = jnp.where(inside, relaxation / jnp.where(inside, total, 1.0), 0.0)
            ms[g][6, i] = scale
            for j in range(6):
                ms[g][j, i] = w[j] * scale
    low2 = nears[2]
    pad = 8

    def plane(src, i, rows, shift=0):
        if len(src.shape) == 2:
            at = pad + i * rows + shift
            return src[at:at + rows]
        return pltpu.roll(src[i], -shift % rows, 0) if shift else src[i]

    for g in range(3):
        rows = es[g].shape[1]
        es[g][:, 0:pad] = jnp.zeros((2, pad, LANES), jnp.float32)
        es[g][:, rows - pad:] = jnp.zeros((2, pad, LANES), jnp.float32)

    def sweep(g, src, dst, inner=False):
        count, rows = fs[g].shape[1:3]
        m, f = ms[g], fs[g]
        below = pltpu.roll(plane(src, count - 1, rows), widths[g], 1)
        middle = plane(src, 0, rows)
        for i in range(count):
            if i < count - 1:
                above = follow = plane(src, i + 1, rows)
            else:
                above, follow = pltpu.roll(plane(src, 0, rows), LANES - widths[g], 1), None
            new = (1.0 - relaxation) * middle + f[cycle, i]
            new = new + m[0, i] * below
            new = new + m[1, i] * above
            new = new + m[2, i] * pltpu.roll(middle, 1, 1)
            new = new + m[3, i] * pltpu.roll(middle, LANES - 1, 1)
            new = new + m[4, i] * pltpu.roll(middle, 1, 0)
            new = new + m[5, i] * pltpu.roll(middle, rows - 1, 0)
            below, middle = middle, follow
            if inner:
                dst[i, nears[g]:rows - nears[g]] = new[nears[g]:rows - nears[g]]
            else:
                dst[pad + i * rows:pad + (i + 1) * rows] = new

    backs = []

    def give_back(xi):
        block = jnp.concatenate([ub[q * rows_of + xi, near:near + slab] for q in range(pieces)], 0)
        turned = block.T
        for j in range(group):
            so[j, xi] = turned[j * ny:(j + 1) * ny]
        copies = []
        for rel in range(1, group):
            x, y = peer(rel)
            copies.append(pltpu.make_async_remote_copy(
                src_ref=so.at[x * cy + y, xi], dst_ref=ro.at[mine, xi], send_sem=osend.at[rel, xi],
                recv_sem=orecv.at[rel, xi], device_id={names[0]: x, names[1]: y}, device_id_type=MESH))
        for c in copies:
            c.start()
        backs.append(copies)
        ro[mine, xi] = so[me, xi]

    for cycle in range(CYCLES):
        for i in range(nx if cycle else 0):
            u = ub[i, near:near + slab]
            below, above = x_pair(lambda p: ub[p, near:near + slab], i, nx, span)
            residual = bb[i] - fw[6, i] * u
            residual = residual + fw[0, i] * below
            residual = residual + fw[1, i] * above
            residual = residual + fw[2, i] * pltpu.roll(u, 1, 1)
            residual = residual + fw[3, i] * pltpu.roll(u, LANES - 1, 1)
            residual = residual + fw[4, i] * ub[i, near - 1:near + slab - 1]
            residual = residual + fw[5, i] * ub[i, near + 1:near + slab + 1]
            rr[i] = residual
        moves = first_moves if cycle == 0 else restrict(cycle, rr)
        z_finish(moves[2])
        src = fs[2].at[cycle]
        for repeat in range(nears[2] - 1):
            sweep(2, src, es[2].at[repeat % 2])
            src = es[2].at[repeat % 2]
        sweep(2, src, ex.at[cycle], True)
        middle_move = z_copies(ex.at[cycle], low2, slab // 2, low2, esend.at[cycle], erecv.at[cycle])
        z_start(middle_move)
        for g in range(2):
            z_finish(moves[g])
            sweep(g, fs[g].at[cycle], es[g].at[0])

        @pl.loop(0, SWEEPS - 2)
        def _(repeat):
            old = lax.rem(repeat, 2)
            for g in range(2):
                sweep(g, es[g].at[old], es[g].at[1 - old])

        last = (SWEEPS - 2) % 2
        z_finish(middle_move)
        src = ex.at[cycle]
        for repeat in range(SWEEPS - 1 - nears[2]):
            slot = (last + SWEEPS - nears[2] - repeat) % 2
            sweep(2, src, es[2].at[slot])
            src = es[2].at[slot]
        keep = wide_rows if cycle < CYCLES - 1 else slab
        low = 0 if cycle < CYCLES - 1 else near
        taken = slice(low, low + keep)
        lanes = lane_of((keep, LANES))
        e_of = [functools.partial(plane, es[g].at[last], rows=fs[g].shape[2]) for g in range(3)]
        e = jnp.concatenate([e_of[1](i)[taken] for i in range(folds)], 0)
        from_y = spread(e, y_spread)
        count = keep // 2
        for x in range(nx):
            middle, lower, upper = (e_of[2](x, shift=step)[low // 2:low // 2 + count] for step in (0, -1, 1))
            tmp[x, pl.ds(0, count, stride=2)] = 0.75 * middle + 0.25 * lower
            tmp[x, pl.ds(1, count, stride=2)] = 0.75 * middle + 0.25 * upper
        for x in range(nx) if cycle < CYCLES - 1 else [q * rows_of + xi for xi in range(rows_of) for q in range(pieces)]:
            i, odd = x // 2, x % 2
            middle = e_of[0](i)[taken]
            other = x_pair(lambda p: e_of[0](p)[taken], i, nx // 2, span)[odd]
            if x == 0:
                other = jnp.where(lanes >= span, other, 0.0)
            if x == nx - 1:
                other = jnp.where(lanes < LANES - span, other, 0.0)
            from_x = 0.75 * middle + 0.25 * other
            fold, xi = x // folds, x % folds
            mid_y = from_y[xi * keep:(xi + 1) * keep, LANES * fold:LANES * (fold + 1)]
            update = blending * ((from_x + mid_y) + tmp[x, 0:keep])
            ub[x, taken] = ub[x, taken] + update if cycle else update
            if cycle == CYCLES - 1 and x // rows_of == pieces - 1:
                give_back(x % rows_of)
        if cycle < CYCLES - 1:
            @pl.when(jnp.logical_not(has_prev))
            def _():
                ub[:, 0:near] = jnp.zeros((nx, near, LANES), jnp.float32)

            @pl.when(jnp.logical_not(has_next))
            def _():
                ub[:, slab + near:] = jnp.zeros((nx, near, LANES), jnp.float32)

    for xi in range(rows_of):
        for c in backs[xi]:
            c.wait_recv()
        for t in range(nz // LANES):
            parts = regroup([ro[t * pieces + q, xi] for q in range(pieces)])
            for q in range(pieces):
                x, at = q * rows_of + xi, slice(LANES * t, LANES * (t + 1))
                out_ref[x, :, at] = stage[4, x, :, at] + parts[q]
    for copies in list(every.values()) + backs:
        for c in copies:
            c.wait_send()
    for c, goes, _ in faces:
        @pl.when(goes)
        def _():
            c.wait_send()


def slab_fits(shape, counts):
    nx, ny, nz = shape
    cx, cy, _ = counts
    group = cx * cy
    if nz % group or ny * group != LANES or LANES % (2 * cx):
        return False
    slab = nz // group
    pieces = LANES // slab
    return (
        slab * pieces == LANES and pieces & (pieces - 1) == 0 and nx % (2 * pieces) == 0
        and slab % 16 == 0 and slab >= 2 * SWEEPS and nz % LANES == 0 and 2 * nx <= LANES)


def slab_body(names, counts, right_side, coefficients, first_guess):
    nx, ny, nz = right_side.shape
    f32 = jnp.float32
    vmem = lambda *shape: pltpu.VMEM(shape, f32)
    dma = pltpu.SemaphoreType.DMA
    group = counts[0] * counts[1]
    slab = nz // group
    rows_of = nx // (LANES // slab)
    near = SWEEPS
    wide = slab + 2 * near
    shapes = ((nx // 2, wide), (nx // 2, wide), (nx, slab // 2 + near))
    blocks = (group, rows_of, ny, LANES)
    scratch = [
        vmem(6, nx, ny, nz),
        vmem(5, *blocks),
        vmem(5, rows_of, group, ny, LANES),
        vmem(4, nx, wide, LANES),
        vmem(nx, wide, LANES),
        vmem(nx, slab, LANES),
        vmem(nx, slab, LANES),
        vmem(7, nx, slab, LANES),
        tuple(vmem(4, x, z, LANES) for x, z in shapes),
        tuple(vmem(7, x, z, LANES) for x, z in shapes),
        tuple(vmem(CYCLES, x, z, LANES) for x, z in shapes),
        tuple(vmem(2, x * z + 16, LANES) for x, z in shapes),
        vmem(nx, wide, LANES),
        vmem(*blocks),
        vmem(*blocks),
        vmem(2, 2, ny, nz), vmem(2, 2, nx, 1, nz), vmem(2, 2, nx, 1, nz), vmem(2, ny, LANES),
        vmem(2, ny, LANES), vmem(CYCLES, *shapes[2], LANES),
        dma((6,)), dma((5, group)), dma((5, group)), dma((4, 2)), dma((4, 2)),
        dma((CYCLES, 3, 2)), dma((CYCLES, 3, 2)), dma((group, rows_of)), dma((group, rows_of)),
        dma((2, 3, 2)), dma((2, 3, 2)), dma((CYCLES, 2)), dma((CYCLES, 2)),
    ]
    hbm = pl.BlockSpec(memory_space=pl.ANY)
    return pl.pallas_call(
        functools.partial(slab_kernel, (nx, ny, nz), counts, names),
        out_shape=jax.ShapeDtypeStruct(right_side.shape, f32),
        in_specs=[hbm] * 3,
        out_specs=pl.BlockSpec(memory_space=pltpu.VMEM),
        scratch_shapes=scratch,
        compiler_params=pltpu.CompilerParams(
            collective_id=0, has_side_effects=True, vmem_limit_bytes=60 * 1024 * 1024),
    )(right_side, coefficients, first_guess)


def solution(mesh):
    names = tuple(mesh.axis_names)
    counts = tuple(mesh.shape[n] for n in names)
    in_specs = (P(*names), P(None, *names), P(*names))

    def local(right_side, coefficients, first_guess):
        if slab_fits(right_side.shape, counts):
            return slab_body(names, counts, right_side, coefficients, first_guess)
        return body(names, right_side, coefficients, first_guess)

    return jax.shard_map(
        local, mesh=mesh, in_specs=in_specs, out_specs=P(*names), check_vma=False)
```

```python
import functools

import jax
import jax.numpy as jnp
from jax import lax
from jax.experimental import pallas as pl
from jax.experimental.pallas import tpu as pltpu
from jax.sharding import PartitionSpec as P

CYCLES = 2
SWEEPS = 8
REACH = 2 * (SWEEPS + 1)
STEP = 20
LANES = 128
CHUNK = 1

relaxation = 0.8
blending = 0.4
MESH = pl.DeviceIdType.MESH


def iota(shape, dim):
    return lax.broadcasted_iota(jnp.int32, shape, dim)


def spread(a, b):
    total = None
    for _ in range(3):
        part = a.astype(jnp.bfloat16)
        a = a - part.astype(jnp.float32)
        term = jnp.dot(part, b, preferred_element_type=jnp.float32)
        total = term if total is None else total + term
    return total


def kernel(sizes, names, b_ref, k_ref, g_ref, out_ref, *scratch):
    (fields, cells, tiles, es, yss, yrs, ms, fs, kxr, kys, kyr, zs, zr, us, ur,
     send, recv, ksend, krecv, zsend, zrecv) = scratch
    nx, ny, nz = sizes
    wide = nz + LANES
    shapes = ((nx // 2, ny, wide), (nx, ny // 2, wide), (nx, ny, nz // 2 + LANES), (nx, ny, wide))
    place = [lax.axis_index(n) for n in names]
    counts = [lax.axis_size(n) for n in names]
    has_low = [p > 0 for p in place]
    has_high = [p < c - 1 for p, c in zip(place, counts)]
    ways = []
    for axis in range(3):
        ways.append((axis, -1, has_low[axis], has_high[axis]))
        ways.append((axis, 1, has_high[axis], has_low[axis]))

    def target(way):
        axis, step = ways[way][:2]
        return {names[axis]: place[axis] + step}

    def copy(src, dst, ssem, rsem, way):
        return pltpu.make_async_remote_copy(
            src_ref=src, dst_ref=dst, send_sem=ssem, recv_sem=rsem,
            device_id=target(way), device_id_type=MESH,
        )

    def start(copies):
        for way, c in copies:
            @pl.when(ways[way][2])
            def _():
                c.start()

    def finish(copies):
        for way, c in copies:
            @pl.when(ways[way][3])
            def _():
                c.wait_recv()
        for way, c in copies:
            @pl.when(ways[way][2])
            def _():
                c.wait_send()

    def faces(g, slot, keep=(0, 1, 2, 3)):
        x = shapes[g][0]
        e, ys, yr = es[g], yss[g], yrs[g]
        ends = (
            (e.at[slot, 1], e.at[slot, x + 1]),
            (e.at[slot, x], e.at[slot, 0]),
            (ys.at[slot, 0], yr.at[slot, 1]),
            (ys.at[slot, 1], yr.at[slot, 0]),
        )
        return [
            (way, copy(*ends[way], send.at[g, way, slot], recv.at[g, way, slot], way)) for way in keep
        ]

    for g in range(4):
        x = shapes[g][0]
        for slot in range(2):
            zero = jnp.zeros(shapes[g][1:], jnp.float32)
            es[g][slot, 0] = zero
            es[g][slot, x + 1] = zero
        yrs[g][...] = jnp.zeros(yrs[g].shape, jnp.float32)
    kxr[...] = jnp.zeros(kxr.shape, jnp.float32)
    kyr[...] = jnp.zeros(kyr.shape, jnp.float32)
    zr[...] = jnp.zeros(zr.shape, jnp.float32)
    ur[...] = jnp.zeros(ur.shape, jnp.float32)

    barrier = pltpu.get_barrier_semaphore()
    for way in range(6):
        @pl.when(ways[way][2])
        def _():
            pl.semaphore_signal(barrier, inc=1, device_id=target(way), device_id_type=MESH)
    peers = sum(jnp.where(has, 1, 0) for has in has_low + has_high)
    pl.semaphore_wait(barrier, peers)

    lane = iota((nx, ny, LANES), 2)
    low = jnp.zeros((nx, ny, LANES), jnp.float32)
    high = low
    for j in range(6):
        if j < 4:
            first, last = k_ref[j, :, :, :LANES], k_ref[j, :, :, nz - LANES:]
        elif j == 4:
            first, last = g_ref[:, :, :LANES], g_ref[:, :, nz - LANES:]
        else:
            first, last = b_ref[:, :, :LANES], b_ref[:, :, nz - LANES:]
        here = (lane >= STEP * j) & (lane < STEP * j + REACH)
        low = jnp.where(here, pltpu.roll(first, STEP * j, 2) if j else first, low)
        high = jnp.where(here, pltpu.roll(last, (STEP * j + REACH) % LANES, 2), high)
    zs[0] = low
    zs[1] = high
    deep = [
        (4, copy(zs.at[0], zr.at[1], zsend.at[0], zrecv.at[0], 4)),
        (5, copy(zs.at[1], zr.at[0], zsend.at[1], zrecv.at[1], 5)),
    ]
    start(deep)
    for j in range(4):
        fields[j, :, :, :nz] = k_ref[j]
    fields[4, :, :, :nz] = b_ref[...]
    es[3][0, 1:nx + 1, :, :nz] = g_ref[...]
    finish(deep)
    above, below = zr[1], zr[0]

    def beside(j):
        up = pltpu.roll(above, (LANES - STEP * j) % LANES, 2) if j else above
        down = pltpu.roll(below, (2 * LANES - REACH - STEP * j) % LANES, 2)
        return jnp.where(lane < REACH, up, jnp.where(lane >= LANES - REACH, down, 0.0))

    for j in range(4):
        fields[j, :, :, nz:] = beside(j)
    es[3][0, 1:nx + 1, :, nz:] = beside(4)
    fields[4, :, :, nz:] = beside(5)

    def send_guess(slot):
        u = es[3][slot, 1:nx + 1]
        yss[3][slot, 0] = u[:, 0:1, :]
        yss[3][slot, 1] = u[:, ny - 1:ny, :]
        start(faces(3, slot))

    ky = fields[1]
    for row in range(2):
        kys[0, row] = ky[:, row:row + 1, :]
        kys[1, row] = ky[:, ny - 2 + row:ny - 1 + row, :]
    edges = [
        (0, copy(fields.at[0, pl.ds(0, 2)], kxr.at[1], ksend.at[0], krecv.at[0], 0)),
        (1, copy(fields.at[0, pl.ds(nx - 2, 2)], kxr.at[0], ksend.at[1], krecv.at[1], 1)),
        (2, copy(kys.at[0], kyr.at[1], ksend.at[2], krecv.at[2], 2)),
        (3, copy(kys.at[1], kyr.at[0], ksend.at[3], krecv.at[3], 3)),
    ]
    start(edges)
    send_guess(0)

    half = nz // 2
    r, c = iota((wide, half + LANES), 0), iota((wide, half + LANES), 1)
    home = jnp.where(
        r < nz, r // 2,
        jnp.where(r < nz + LANES // 2, half + (r - nz) // 2, half + LANES // 2 + (r - nz) // 2),
    )
    z_mean = jnp.where(home == c, 0.5, 0.0).astype(jnp.bfloat16)
    rows = nx * ny
    r, c = iota((half + LANES, nz), 0), iota((half + LANES, nz), 1)
    main = c // 2
    total = half + LANES
    side = jnp.where(c % 2 == 1, main + 1, jnp.where(main == 0, total - 1, main - 1))
    z_spread = (jnp.where(r == main, 0.75, 0.0) + jnp.where(r == side, 0.25, 0.0)).astype(jnp.bfloat16)

    count = wide // LANES
    even_rows, odd_rows = pl.ds(0, ny // 2, stride=2), pl.ds(1, ny // 2, stride=2)

    def put_tiles(planes, values):
        for t in range(values.shape[2] // LANES):
            tiles[t, planes] = values[:, :, LANES * t:LANES * (t + 1)]

    def get_tiles(planes, tiles_of=count):
        return jnp.concatenate([tiles[t, planes] for t in range(tiles_of)], 2)

    def y_mean(planes):
        return jnp.concatenate(
            [0.5 * (tiles[t, planes, even_rows] + tiles[t, planes, odd_rows]) for t in range(count)], 2)

    def chunks(x, step=CHUNK):
        return [slice(x0, x0 + step) for x0 in range(0, x, step)]

    def below_of(ref, planes, halo):
        if planes.start > 0:
            return ref[planes.start - 1:planes.stop - 1]
        return halo if planes.stop == 1 else jnp.concatenate([halo, ref[0:planes.stop - 1]], 0)

    def above_of(ref, planes, halo):
        if planes.stop < ref.shape[0]:
            return ref[planes.start + 1:planes.stop + 1]
        if planes.stop == planes.start + 1:
            return halo
        return jnp.concatenate([ref[planes.start + 1:planes.stop], halo], 0)

    def y_shift(values, halo_low, halo_high):
        y = values.shape[1]
        row = iota(values.shape, 1)
        lower = jnp.where(row == 0, halo_low, pltpu.roll(values, 1, 1))
        upper = jnp.where(row == y - 1, halo_high, pltpu.roll(values, y - 1, 1))
        return lower, upper

    def z_shift(values):
        return pltpu.roll(values, 1, 2), pltpu.roll(values, values.shape[2] - 1, 2)

    def face_weights(k, planes, near_x, near_y):
        k0, k1, k2 = k.at[0], k.at[1], k.at[2]
        m1, m2 = k1[planes], k2[planes]
        groups = (
            (k0[planes], (below_of(k0, planes, near_x[0]), above_of(k0, planes, near_x[1]))),
            (m1, y_shift(m1, near_y[0](planes), near_y[1](planes))),
            (m2, z_shift(m2)),
        )
        found = []
        total = k[3, planes]
        for middle, pair in groups:
            for other in pair:
                found.append(0.5 * (middle + other))
                total = total + found[-1]
        return found, total

    for j in range(4):
        for d in range(2):
            factor = 0.25 if j == d else 1.0
            if d == 0:
                for i in range(nx // 2):
                    cells[0][j, i] = (0.5 * factor) * (fields[j, 2 * i] + fields[j, 2 * i + 1])
            else:
                for planes in chunks(nx):
                    put_tiles(planes, fields[j, planes])
                for planes in chunks(nx):
                    cells[1][j, planes] = y_mean(planes) * factor
    for j in range(4):
        factor = 0.25 if j == 2 else 1.0
        for planes in chunks(nx, nx // 2):
            flat = fields[j, planes].reshape((rows // 2, wide))
            cells[2][j, planes] = (spread(flat, z_mean) * factor).reshape((nx // 2,) + shapes[2][1:])
    finish(edges)
    near_rows = [kxr[0, 1], kxr[1, 0]] + [kyr[0, 1].reshape((nx, wide)), kyr[1, 0].reshape((nx, wide))]
    edge = spread(jnp.concatenate(near_rows, 0), z_mean)
    edge_x = [edge[0:ny][None], edge[ny:2 * ny][None]]
    edge_y = [edge[2 * ny + nx * side:2 * ny + nx * (side + 1)].reshape((nx, 1, half + LANES)) for side in range(2)]
    put_tiles(slice(0, 2), jnp.stack([kxr[0, 1], kxr[1, 0]]))
    pair = y_mean(slice(0, 2))

    near_xs = (
        [0.125 * (kxr[side, 0:1] + kxr[side, 1:2]) for side in range(2)],
        [pair[0:1], pair[1:2]],
        edge_x,
    )

    def y_face(d, side):
        nearest = kyr.at[side, 1 - side]
        if d == 0:
            return lambda planes: jnp.concatenate(
                [0.5 * (nearest[2 * i:2 * i + 1] + nearest[2 * i + 1:2 * i + 2])
                 for i in range(planes.start, planes.stop)], 0)
        if d == 1:
            return lambda planes: 0.125 * (kyr[side, 0, planes] + kyr[side, 1, planes])
        if d == 2:
            return lambda planes: edge_y[side][planes]
        return lambda planes: nearest[planes]

    for d in range(3):
        for planes in chunks(shapes[d][0]):
            w, total_coarse = face_weights(
                cells[d], planes, near_xs[d], (y_face(d, 0), y_face(d, 1)))
            inside = cells[d][3, planes] > 0.0
            scale = jnp.where(inside, relaxation / jnp.where(inside, total_coarse, 1.0), 0.0)
            ms[d][6, planes] = scale
            for j in range(6):
                ms[d][j, planes] = w[j] * scale

    def sweep(g, slot, new_slot, keep=(0, 1, 2, 3)):
        e, yr, ys, m, f = es[g], yrs[g], yss[g], ms[g], fs[g]
        x, y, z = shapes[g]
        order = list(range(0, x, CHUNK))
        order = order[:1] + order[-1:] + order[1:-1]
        for x0 in order:
            planes = slice(x0, x0 + CHUNK)
            middle = e[slot, x0 + 1:x0 + 1 + CHUNK]
            y_low, y_high = y_shift(middle, yr[slot, 0, planes], yr[slot, 1, planes])
            z_low, z_high = z_shift(middle)
            new = (1.0 - relaxation) * middle + f[planes]
            new = new + m[0, planes] * e[slot, x0:x0 + CHUNK]
            new = new + m[1, planes] * e[slot, x0 + 2:x0 + 2 + CHUNK]
            new = new + m[2, planes] * y_low
            new = new + m[3, planes] * y_high
            new = new + m[4, planes] * z_low
            new = new + m[5, planes] * z_high
            e[new_slot, x0 + 1:x0 + 1 + CHUNK] = new
            ys[new_slot, 0, planes] = new[:, 0:1]
            ys[new_slot, 1, planes] = new[:, y - 1:y]
            if x0 == order[1] and 0 in keep:
                start(faces(g, new_slot, (0, 1)))
        if 2 in keep:
            start(faces(g, new_slot, (2, 3)))

    for cycle in range(CYCLES):
        slot = cycle % 2
        finish(faces(3, slot))
        u = es[3]
        for planes in chunks(nx):
            x0, x1 = planes.start, planes.stop
            middle = u[slot, x0 + 1:x1 + 1]
            y_low, y_high = y_shift(middle, yrs[3][slot, 0, planes], yrs[3][slot, 1, planes])
            z_low, z_high = z_shift(middle)
            w, total_fine = face_weights(
                fields, planes, (kxr[0, 1:2], kxr[1, 0:1]), (y_face(3, 0), y_face(3, 1)))
            residual = fields[4, planes] - total_fine * middle
            around = (u[slot, x0:x1], u[slot, x0 + 2:x1 + 2], y_low, y_high, z_low, z_high)
            for j in range(6):
                residual = residual + w[j] * around[j]
            put_tiles(planes, residual)
        for g in range(3):
            x, y, z = shapes[g]
            if g == 2:
                flat = get_tiles(slice(0, nx)).reshape((rows, wide))
                whole = spread(flat, z_mean).reshape(shapes[2])
            for planes in chunks(x):
                if g == 0:
                    pairs = [get_tiles(slice(2 * i, 2 * i + 2)) for i in range(planes.start, planes.stop)]
                    first = jnp.concatenate([0.5 * (p[0:1] + p[1:2]) for p in pairs], 0)
                elif g == 1:
                    first = y_mean(planes)
                else:
                    first = whole[planes]
                first = ms[g][6, planes] * first
                fs[g][planes] = first
                es[g][1, planes.start + 1:planes.stop + 1] = first
                yss[g][1, 0, planes] = first[:, 0:1]
                yss[g][1, 1, planes] = first[:, y - 1:y]
            start(faces(g, 1))

        @pl.loop(1, SWEEPS - 1)
        def _(repeat):
            old = lax.rem(repeat, 2)
            for g in range(3):
                finish(faces(g, old))
                sweep(g, old, 1 - old)

        last = SWEEPS % 2
        needed = ((0, 1), (2, 3), ())
        for g in range(3):
            finish(faces(g, 1 - last))
            sweep(g, 1 - last, last, needed[g])
        e = es[2][last, 1:nx + 1].reshape((rows, half + LANES))
        from_z = spread(e, z_spread).reshape((nx, ny, nz))
        finish(faces(1, last, needed[1]))
        for planes in chunks(nx):
            e = es[1][last, planes.start + 1:planes.stop + 1, :, :nz]
            y_low, y_high = y_shift(
                e, yrs[1][last, 0, planes, :, :nz], yrs[1][last, 1, planes, :, :nz])
            even = 0.75 * e + 0.25 * y_low
            odd = 0.75 * e + 0.25 * y_high
            for t in range(nz // LANES):
                tiles[t, planes, even_rows] = even[:, :, LANES * t:LANES * (t + 1)]
                tiles[t, planes, odd_rows] = odd[:, :, LANES * t:LANES * (t + 1)]
        finish(faces(0, last, needed[0]))
        for i in range(nx // 2):
            planes = slice(2 * i, 2 * i + 2)
            e = es[0][last, i:i + 3, :, :nz]
            even = 0.75 * e[1:2] + 0.25 * e[0:1]
            odd = 0.75 * e[1:2] + 0.25 * e[2:3]
            update = (jnp.concatenate([even, odd], 0) + get_tiles(planes, nz // LANES)) + from_z[planes]
            final = es[3][slot, 2 * i + 1:2 * i + 3, :, :nz] + blending * update
            if cycle == CYCLES - 1:
                out_ref[planes] = final
            else:
                es[3][1 - slot, 2 * i + 1:2 * i + 3, :, :nz] = final
        if cycle == CYCLES - 1:
            continue
        result = es[3].at[1 - slot, 1:nx + 1]
        per = LANES // STEP
        plane_lane = iota((ny, LANES), 1)
        groups = us.shape[1]
        for q in range(groups):
            low = jnp.zeros((ny, LANES), jnp.float32)
            high = low
            for p in range(min(per, nx - q * per)):
                here = (plane_lane >= STEP * p) & (plane_lane < STEP * p + REACH)
                first = result[q * per + p, :, :LANES]
                low = jnp.where(here, pltpu.roll(first, STEP * p, 1) if p else first, low)
                high = jnp.where(
                    here, pltpu.roll(result[q * per + p, :, nz - LANES:nz], (STEP * p + REACH) % LANES, 1), high)
            us[0, q] = low
            us[1, q] = high
        again = [
            (4, copy(us.at[0], ur.at[1], zsend.at[2], zrecv.at[2], 4)),
            (5, copy(us.at[1], ur.at[0], zsend.at[3], zrecv.at[3], 5)),
        ]
        start(again)
        finish(again)
        for i in range(nx):
            q, p = i // per, i % per
            up = pltpu.roll(ur[1, q], (LANES - STEP * p) % LANES, 1) if p else ur[1, q]
            down = pltpu.roll(ur[0, q], (2 * LANES - REACH - STEP * p) % LANES, 1)
            es[3][1 - slot, i + 1, :, nz:] = jnp.where(
                plane_lane < REACH, up, jnp.where(plane_lane >= LANES - REACH, down, 0.0))
        send_guess(1 - slot)


def body(names, right_side, coefficients, first_guess):
    nx, ny, nz = right_side.shape
    wide = nz + LANES
    shapes = ((nx // 2, ny, wide), (nx, ny // 2, wide), (nx, ny, nz // 2 + LANES), (nx, ny, wide))
    f32 = jnp.float32
    vmem = lambda *shape: pltpu.VMEM(shape, f32)
    dma = pltpu.SemaphoreType.DMA
    groups = -(-nx // (LANES // STEP))
    scratch = [
        vmem(5, nx, ny, wide),
        tuple(vmem(4, x, y, z) for x, y, z in shapes[:3]),
        vmem(wide // LANES, nx, ny, LANES),
        tuple(vmem(2, x + 2, y, z) for x, y, z in shapes),
        tuple(vmem(2, 2, x, 1, z) for x, y, z in shapes),
        tuple(vmem(2, 2, x, 1, z) for x, y, z in shapes),
        tuple(vmem(7, x, y, z) for x, y, z in shapes[:3]),
        tuple(vmem(x, y, z) for x, y, z in shapes[:3]),
        vmem(2, 2, ny, wide),
        vmem(2, 2, nx, 1, wide),
        vmem(2, 2, nx, 1, wide),
        vmem(2, nx, ny, LANES),
        vmem(2, nx, ny, LANES),
        vmem(2, groups, ny, LANES),
        vmem(2, groups, ny, LANES),
        dma((4, 4, 2)), dma((4, 4, 2)), dma((4,)), dma((4,)), dma((4,)), dma((4,)),
    ]
    spec = pl.BlockSpec(memory_space=pltpu.VMEM)
    return pl.pallas_call(
        functools.partial(kernel, (nx, ny, nz), names),
        out_shape=jax.ShapeDtypeStruct(right_side.shape, f32),
        in_specs=[spec] * 3,
        out_specs=spec,
        scratch_shapes=scratch,
        compiler_params=pltpu.CompilerParams(
            collective_id=0, has_side_effects=True, vmem_limit_bytes=60 * 1024 * 1024),
    )(right_side, coefficients, first_guess)


def slab_kernel(sizes, mesh_counts, names, b_hbm, k_hbm, g_hbm, out_ref, *scratch):
    (stage, sb, rb, field, ub, bb, rr, fw, cells, ms, fs, es, tmp, so, ro, hx, hys, hyr, hzs, hz, ex,
     in_sem, send, recv, zsend, zrecv, gsend, grecv, osend, orecv, hsend, hrecv, esend, erecv) = scratch
    nx, ny, nz = sizes
    cx, cy, cz = mesh_counts
    group = cx * cy
    slab = nz // group
    pieces = LANES // slab
    rows_of = nx // pieces
    near = SWEEPS
    nears = (near, near, near // 2)
    span = LANES // cx
    gx, gy, gz = (lax.axis_index(n) for n in names)
    me = gx * cy + gy

    def slab_of(x, y, z):
        p = x * cy + y + lax.rem(x, 2) * (cy - 1 - 2 * y)
        return p + lax.rem(z, 2) * (group - 1 - 2 * p)

    def device_of(s, z):
        p = s + lax.rem(z, 2) * (group - 1 - 2 * s)
        x, t = p // cy, lax.rem(p, cy)
        return x, t + lax.rem(x, 2) * (cy - 1 - 2 * t)

    mine = slab_of(gx, gy, gz)
    chain = gz * group + mine
    has_prev, has_next = chain > 0, chain < cz * group - 1

    def neighbour(step):
        c = chain + step
        c = jnp.clip(c, 0, cz * group - 1)
        z, s = c // group, lax.rem(c, group)
        x, y = device_of(s, z)
        return {names[0]: x, names[1]: y, names[2]: z}

    prev_id, next_id = neighbour(-1), neighbour(1)
    place, counts = (gx, gy, gz), (cx, cy, cz)
    has_low = [q > 0 for q in place]
    has_high = [q < c - 1 for q, c in zip(place, counts)]

    loads = [pltpu.make_async_copy(k_hbm.at[j], stage.at[j], in_sem.at[j]) for j in range(4)]
    loads.append(pltpu.make_async_copy(g_hbm, stage.at[4], in_sem.at[4]))
    loads.append(pltpu.make_async_copy(b_hbm, stage.at[5], in_sem.at[5]))
    order = (2, 0, 1, 3)
    for f in order + (4, 5):
        loads[f].start()

    def peer(rel):
        return lax.rem(gx + rel // cy, cx), lax.rem(gy + rel % cy, cy)

    barrier = pltpu.get_barrier_semaphore()
    for rel in range(1, group):
        x, y = peer(rel)
        pl.semaphore_signal(barrier, inc=1, device_id={names[0]: x, names[1]: y}, device_id_type=MESH)

    @pl.when(has_low[2])
    def _():
        pl.semaphore_signal(barrier, inc=1, device_id={names[2]: gz - 1}, device_id_type=MESH)

    @pl.when(has_high[2])
    def _():
        pl.semaphore_signal(barrier, inc=1, device_id={names[2]: gz + 1}, device_id_type=MESH)

    def lane_of(shape):
        return iota(shape, len(shape) - 1)

    tile_lane = lane_of((ny, LANES))

    def regroup(values):
        values = list(values)
        step = pieces // 2
        while step:
            width = slab * step
            low = lax.rem(tile_lane // width, 2) == 0
            for i in range(pieces):
                if i & step == 0:
                    a, c = values[i], values[i + step]
                    values[i] = jnp.where(low, a, pltpu.roll(c, width, 1))
                    values[i + step] = jnp.where(low, pltpu.roll(a, LANES - width, 1), c)
            step //= 2
        return values

    def pack(f):
        for xi in range(rows_of):
            for t in range(nz // LANES):
                parts = regroup(
                    [stage[5 if f == 4 else f, q * rows_of + xi, :, LANES * t:LANES * (t + 1)] for q in range(pieces)])
                for q in range(pieces):
                    sb[f, t * pieces + q, xi] = parts[q]

    def spread_copies(f):
        copies = []
        for rel in range(1, group):
            x, y = peer(rel)
            copies.append(pltpu.make_async_remote_copy(
                src_ref=sb.at[f, slab_of(x, y, gz)], dst_ref=rb.at[f, me],
                send_sem=send.at[f, rel], recv_sem=recv.at[f, rel],
                device_id={names[0]: x, names[1]: y}, device_id_type=MESH))
        return copies

    def z_copies(ref, own_low, own, halo, ssem, rsem):
        up = pltpu.make_async_remote_copy(
            src_ref=ref.at[:, pl.ds(own_low + own - halo, halo)], dst_ref=ref.at[:, pl.ds(own_low - halo, halo)],
            send_sem=ssem.at[0], recv_sem=rsem.at[0], device_id=next_id, device_id_type=MESH)
        down = pltpu.make_async_remote_copy(
            src_ref=ref.at[:, pl.ds(own_low, halo)], dst_ref=ref.at[:, pl.ds(own_low + own, halo)],
            send_sem=ssem.at[1], recv_sem=rsem.at[1], device_id=prev_id, device_id_type=MESH)
        return up, down

    def z_start(copies):
        up, down = copies

        @pl.when(has_next)
        def _():
            up.start()

        @pl.when(has_prev)
        def _():
            down.start()

    def z_finish(copies):
        up, down = copies

        @pl.when(has_prev)
        def _():
            up.wait_recv()

        @pl.when(has_next)
        def _():
            down.wait_recv()

        @pl.when(has_next)
        def _():
            up.wait_send()

        @pl.when(has_prev)
        def _():
            down.wait_send()

    faces = []
    for a in range(2):
        for axis in range(3 if a == 0 else 2):
            v = 4 if a == 0 else axis
            for side in range(2):
                src = (stage.at[v, (0, nx - 1)[side]], hys.at[a, side], hzs.at[side])[axis]
                dst = (hx.at[a, 1 - side], hyr.at[a, 1 - side], hz.at[1 - side])[axis]
                faces.append((
                    pltpu.make_async_remote_copy(
                        src_ref=src, dst_ref=dst, send_sem=hsend.at[a, axis, side], recv_sem=hrecv.at[a, axis, side],
                        device_id={names[axis]: place[axis] + (-1, 1)[side]}, device_id_type=MESH),
                    (has_low, has_high)[side][axis], (has_high, has_low)[side][axis]))

    every = {}

    def send_out(f):
        every[f] = spread_copies(f)
        for c in every[f]:
            c.start()
        rb[f, me] = sb[f, mine]

    loads[2].wait()
    pack(2)
    pl.semaphore_wait(barrier, group - 1 + jnp.where(has_low[2], 1, 0) + jnp.where(has_high[2], 1, 0))
    send_out(2)
    loads[0].wait()
    pack(0)
    send_out(0)
    loads[1].wait()
    loads[4].wait()
    for a in range(2):
        for side in range(2):
            row = (0, ny - 1)[side]
            hys[a, side] = stage[4 if a == 0 else 1, :, row:row + 1, :]
    for side in range(2):
        edge = jnp.zeros((ny, LANES), jnp.float32)
        for a in range(2):
            for i in range(nx):
                v, to = 4 if a == 0 else 2, a * nx + i
                if side == 0:
                    rolled = pltpu.roll(stage[v, i, :, 0:LANES], to, 1) if to else stage[v, i, :, 0:LANES]
                else:
                    rolled = pltpu.roll(stage[v, i, :, nz - LANES:nz], to + 1, 1)
                edge = jnp.where(tile_lane == to, rolled, edge)
        hzs[side] = edge
    for c, goes, _ in faces:
        @pl.when(goes)
        def _():
            c.start()

    pack(1)
    send_out(1)
    loads[3].wait()
    pack(3)
    send_out(3)
    loads[5].wait()

    for side in range(2):
        absent = [jnp.logical_not((has_low, has_high)[side][axis]) for axis in range(3)]

        @pl.when(absent[0])
        def _():
            hx[:, side] = jnp.zeros((2, ny, nz), jnp.float32)

        @pl.when(absent[1])
        def _():
            hyr[:, side] = jnp.zeros((2, nx, 1, nz), jnp.float32)

        @pl.when(absent[2])
        def _():
            hz[side] = jnp.zeros((ny, LANES), jnp.float32)

    @pl.when(jnp.logical_not(has_prev))
    def _():
        field[:, :, 0:near] = jnp.zeros((4, nx, near, LANES), jnp.float32)
        for g in range(3):
            x = fs[g].shape[1]
            fs[g][:, :, 0:nears[g]] = jnp.zeros((CYCLES, x, nears[g], LANES), jnp.float32)
        ex[:, :, 0:nears[2]] = jnp.zeros((CYCLES, nx, nears[2], LANES), jnp.float32)

    @pl.when(jnp.logical_not(has_next))
    def _():
        field[:, :, slab + near:] = jnp.zeros((4, nx, near, LANES), jnp.float32)
        for g in range(3):
            x, rows = fs[g].shape[1:3]
            fs[g][:, :, rows - nears[g]:] = jnp.zeros((CYCLES, x, nears[g], LANES), jnp.float32)
        ex[:, :, slab // 2 + nears[2]:] = jnp.zeros((CYCLES, nx, nears[2], LANES), jnp.float32)

    tile_row = iota((ny, LANES), 0)
    count_t = nz // LANES

    def home_shifts(f, a, i, axis):
        tiles_of = [stage[f, i, :, LANES * t:LANES * (t + 1)] for t in range(count_t)]
        if axis == 0:
            low = stage[f, i - 1] if i > 0 else hx[a, 0]
            high = stage[f, i + 1] if i < nx - 1 else hx[a, 1]
            cut = lambda v: [v[:, LANES * t:LANES * (t + 1)] for t in range(count_t)]
            return list(zip(cut(low), cut(high)))
        if axis == 1:
            found = []
            for t in range(count_t):
                at = slice(LANES * t, LANES * (t + 1))
                found.append((
                    jnp.where(tile_row == 0, hyr[a, 0, i, :, at], pltpu.roll(tiles_of[t], 1, 0)),
                    jnp.where(tile_row == ny - 1, hyr[a, 1, i, :, at], pltpu.roll(tiles_of[t], ny - 1, 0))))
            return found
        to = a * nx + i
        ups = [pltpu.roll(hz[0], LANES - to, 1) if to else hz[0]] + [pltpu.roll(v, 1, 1) for v in tiles_of]
        downs = [pltpu.roll(v, LANES - 1, 1) for v in tiles_of] + [pltpu.roll(hz[1], LANES - 1 - to, 1)]
        return [
            (jnp.where(tile_lane == 0, ups[t], ups[t + 1]),
             jnp.where(tile_lane == LANES - 1, downs[t + 1], downs[t])) for t in range(count_t)]

    def arrive(f):
        for c in every[f]:
            c.wait_recv()
        for xi in range(rows_of):
            turned = jnp.concatenate([rb[f, j, xi] for j in range(group)], 0).T
            for q in range(pieces):
                part = turned[q * slab:(q + 1) * slab]
                x = q * rows_of + xi
                if f < 4:
                    field[f, x, near:near + slab] = part
                else:
                    bb[x] = part

    halos = {}

    def take(f):
        arrive(f)
        halos[f] = z_copies(field.at[f], near, slab, near, zsend.at[f], zrecv.at[f])
        z_start(halos[f])

    take(2)
    for c, goes, comes in faces:
        @pl.when(comes)
        def _():
            c.wait_recv()
    for i in range(nx):
        around = [(home_shifts(4, 0, i, axis), home_shifts(axis, 1, i, axis)) for axis in range(3)]
        for t in range(count_t):
            at = slice(LANES * t, LANES * (t + 1))
            total = stage[3, i, :, at]
            pulled = stage[5, i, :, at]
            for axis in range(3):
                middle = stage[axis, i, :, at]
                for side in range(2):
                    w = 0.5 * (middle + around[axis][1][t][side])
                    total = total + w
                    pulled = pulled + w * around[axis][0][t][side]
            stage[5, i, :, at] = pulled - total * stage[4, i, :, at]

    pack(4)
    send_out(4)

    wide_rows = slab + 2 * near
    half = span // 2
    r, c = iota((2 * LANES, LANES), 0), iota((2 * LANES, LANES), 1)
    lane = lax.rem(r, LANES)
    y_mean = jnp.where(
        (r // LANES == lax.rem(c, span) // half) & (lane // span == c // span)
        & (lax.rem(lane, span) // 2 == lax.rem(c, half)), 0.5, 0.0).astype(jnp.bfloat16)
    r, c = iota((LANES, 2 * LANES), 0), iota((LANES, 2 * LANES), 1)
    lane = lax.rem(c, LANES)
    here = (c // LANES == lax.rem(r, span) // half) & (lane // span == r // span)
    fine_y = lax.rem(lane, span)
    main = fine_y // 2
    side = jnp.where(lax.rem(fine_y, 2) == 1, main + 1, main - 1)
    coarse_y = lax.rem(r, half)
    y_spread = jnp.where(
        here & (coarse_y == main), 0.75, jnp.where(here & (coarse_y == side), 0.25, 0.0)).astype(jnp.bfloat16)
    folds = nx // 2

    def fold_y(rows_low, rows_high):
        n = rows_low.shape[0] * rows_low.shape[1]
        both = jnp.concatenate([rows_low.reshape((n, LANES)), rows_high.reshape((n, LANES))], 1)
        return spread(both, y_mean).reshape(rows_low.shape)

    def coarsen(f, low, high):
        factors = [0.25 if f == d else 1.0 for d in range(3)]
        for i in range(nx // 2):
            cells[0][f, i, low:high] = (0.5 * factors[0]) * (field[f, 2 * i, low:high] + field[f, 2 * i + 1, low:high])
        cells[1][f, :, low:high] = fold_y(field[f, 0:folds, low:high], field[f, folds:nx, low:high]) * factors[1]
        n = (high - low) // 2
        for x in range(nx):
            cells[2][f, x, low // 2:high // 2] = (0.5 * factors[2]) * (
                field[f, x, pl.ds(low, n, stride=2)] + field[f, x, pl.ds(low + 1, n, stride=2)])

    def take_halo(f):
        z_finish(halos[f])
        coarsen(f, 0, near)
        coarsen(f, near + slab, wide_rows)

    coarsen(2, near, near + slab)
    for f in order[1:]:
        take(f)
        coarsen(f, near, near + slab)
    take_halo(2)

    def masks(shape, width):
        lanes = lane_of(shape)
        y = lax.rem(lanes, width)
        return y != 0, y != width - 1, lanes >= width, lanes < LANES - width

    def x_pair(get, i, count, width):
        below = get(i - 1) if i > 0 else pltpu.roll(get(count - 1), width, 1)
        above = get(i + 1) if i < count - 1 else pltpu.roll(get(0), LANES - width, 1)
        return below, above

    def weights(k, i, count, width, z_pair):
        y_low, y_high, x_low, x_high = masks(k(3, i).shape, width)
        k0, k1, k2 = k(0, i), k(1, i), k(2, i)
        below, above = x_pair(lambda p: k(0, p), i, count, width)
        if i == 0:
            below = jnp.where(x_low, below, 0.0)
        if i == count - 1:
            above = jnp.where(x_high, above, 0.0)
        around = [
            (k0, below, x_low if i == 0 else None), (k0, above, x_high if i == count - 1 else None),
            (k1, jnp.where(y_low, pltpu.roll(k1, 1, 1), 0.0), y_low),
            (k1, jnp.where(y_high, pltpu.roll(k1, LANES - 1, 1), 0.0), y_high),
        ]
        around += [(k2, other, None) for other in z_pair]
        total = k(3, i)
        found = []
        for middle, other, keep in around:
            w = 0.5 * (middle + other)
            total = total + w
            found.append(w if keep is None else jnp.where(keep, w, 0.0))
        return found, total

    widths = (span, half, span)
    for g in range(3):
        count, rows = cells[g].shape[1:3]
        at = slice(nears[g], rows - nears[g])
        for i in range(count):
            z_pair = [cells[g][2, i, at.start + step:at.stop + step] for step in (-1, 1)]
            _, total = weights(lambda j, p: cells[g][j, p, at], i, count, widths[g], z_pair)
            ms[g][6, i, at] = relaxation / total
    own = slice(near, near + slab)
    for i in range(nx):
        z_pair = (field[2, i, near - 1:near + slab - 1], field[2, i, near + 1:near + slab + 1])
        w, total = weights(lambda j, p: field[j, p, own], i, nx, span, z_pair)
        for j in range(6):
            fw[j, i] = w[j]
        fw[6, i] = total

    def restrict(cycle, left):
        moves = {}

        def send_first(g):
            rows = fs[g].shape[2]
            moves[g] = z_copies(
                fs[g].at[cycle], nears[g], rows - 2 * nears[g], nears[g], gsend.at[cycle, g], grecv.at[cycle, g])
            z_start(moves[g])

        low2, high2 = nears[2], nears[2] + slab // 2
        for x in range(nx):
            first = 0.5 * (left[x, pl.ds(0, slab // 2, stride=2)] + left[x, pl.ds(1, slab // 2, stride=2)])
            fs[2][cycle, x, low2:high2] = ms[2][6, x, low2:high2] * first
        send_first(2)
        for i in range(nx // 2):
            first = 0.5 * (left[2 * i] + left[2 * i + 1])
            fs[0][cycle, i, near:near + slab] = ms[0][6, i, near:near + slab] * first
        send_first(0)
        first = fold_y(left[0:folds], left[folds:nx])
        fs[1][cycle, :, near:near + slab] = ms[1][6, :, near:near + slab] * first
        send_first(1)
        return moves

    take_halo(0)
    take_halo(1)
    arrive(4)
    first_moves = restrict(0, bb)
    take_halo(3)
    for g in range(3):
        count, rows = cells[g].shape[1:3]
        for i in range(count):
            k2 = cells[g][2, i]
            z_pair = (pltpu.roll(k2, 1, 0), pltpu.roll(k2, rows - 1, 0))
            w, total = weights(lambda j, p: cells[g][j, p], i, count, widths[g], z_pair)
            inside = cells[g][3, i] > 0.0
            scale = jnp.where(inside, relaxation / jnp.where(inside, total, 1.0), 0.0)
            ms[g][6, i] = scale
            for j in range(6):
                ms[g][j, i] = w[j] * scale
    low2 = nears[2]
    pad = 8

    def plane(src, i, rows, shift=0):
        if len(src.shape) == 2:
            at = pad + i * rows + shift
            return src[at:at + rows]
        return pltpu.roll(src[i], -shift % rows, 0) if shift else src[i]

    for g in range(3):
        rows = es[g].shape[1]
        es[g][:, 0:pad] = jnp.zeros((2, pad, LANES), jnp.float32)
        es[g][:, rows - pad:] = jnp.zeros((2, pad, LANES), jnp.float32)

    def sweep(g, src, dst, inner=False):
        count, rows = fs[g].shape[1:3]
        m, f = ms[g], fs[g]
        below = pltpu.roll(plane(src, count - 1, rows), widths[g], 1)
        middle = plane(src, 0, rows)
        for i in range(count):
            if i < count - 1:
                above = follow = plane(src, i + 1, rows)
            else:
                above, follow = pltpu.roll(plane(src, 0, rows), LANES - widths[g], 1), None
            new = (1.0 - relaxation) * middle + f[cycle, i]
            new = new + m[0, i] * below
            new = new + m[1, i] * above
            new = new + m[2, i] * pltpu.roll(middle, 1, 1)
            new = new + m[3, i] * pltpu.roll(middle, LANES - 1, 1)
            new = new + m[4, i] * pltpu.roll(middle, 1, 0)
            new = new + m[5, i] * pltpu.roll(middle, rows - 1, 0)
            below, middle = middle, follow
            if inner:
                dst[i, nears[g]:rows - nears[g]] = new[nears[g]:rows - nears[g]]
            else:
                dst[pad + i * rows:pad + (i + 1) * rows] = new

    backs = []

    def give_back(xi):
        block = jnp.concatenate([ub[q * rows_of + xi, near:near + slab] for q in range(pieces)], 0)
        turned = block.T
        for j in range(group):
            so[j, xi] = turned[j * ny:(j + 1) * ny]
        copies = []
        for rel in range(1, group):
            x, y = peer(rel)
            copies.append(pltpu.make_async_remote_copy(
                src_ref=so.at[x * cy + y, xi], dst_ref=ro.at[mine, xi], send_sem=osend.at[rel, xi],
                recv_sem=orecv.at[rel, xi], device_id={names[0]: x, names[1]: y}, device_id_type=MESH))
        for c in copies:
            c.start()
        backs.append(copies)
        ro[mine, xi] = so[me, xi]

    for cycle in range(CYCLES):
        for i in range(nx if cycle else 0):
            u = ub[i, near:near + slab]
            below, above = x_pair(lambda p: ub[p, near:near + slab], i, nx, span)
            residual = bb[i] - fw[6, i] * u
            residual = residual + fw[0, i] * below
            residual = residual + fw[1, i] * above
            residual = residual + fw[2, i] * pltpu.roll(u, 1, 1)
            residual = residual + fw[3, i] * pltpu.roll(u, LANES - 1, 1)
            residual = residual + fw[4, i] * ub[i, near - 1:near + slab - 1]
            residual = residual + fw[5, i] * ub[i, near + 1:near + slab + 1]
            rr[i] = residual
        moves = first_moves if cycle == 0 else restrict(cycle, rr)
        z_finish(moves[2])
        src = fs[2].at[cycle]
        for repeat in range(nears[2] - 1):
            sweep(2, src, es[2].at[repeat % 2])
            src = es[2].at[repeat % 2]
        sweep(2, src, ex.at[cycle], True)
        middle_move = z_copies(ex.at[cycle], low2, slab // 2, low2, esend.at[cycle], erecv.at[cycle])
        z_start(middle_move)
        for g in range(2):
            z_finish(moves[g])
            sweep(g, fs[g].at[cycle], es[g].at[0])

        @pl.loop(0, SWEEPS - 2)
        def _(repeat):
            old = lax.rem(repeat, 2)
            for g in range(2):
                sweep(g, es[g].at[old], es[g].at[1 - old])

        last = (SWEEPS - 2) % 2
        z_finish(middle_move)
        src = ex.at[cycle]
        for repeat in range(SWEEPS - 1 - nears[2]):
            slot = (last + SWEEPS - nears[2] - repeat) % 2
            sweep(2, src, es[2].at[slot])
            src = es[2].at[slot]
        keep = wide_rows if cycle < CYCLES - 1 else slab
        low = 0 if cycle < CYCLES - 1 else near
        taken = slice(low, low + keep)
        lanes = lane_of((keep, LANES))
        e_of = [functools.partial(plane, es[g].at[last], rows=fs[g].shape[2]) for g in range(3)]
        e = jnp.concatenate([e_of[1](i)[taken] for i in range(folds)], 0)
        from_y = spread(e, y_spread)
        count = keep // 2
        for x in range(nx):
            middle, lower, upper = (e_of[2](x, shift=step)[low // 2:low // 2 + count] for step in (0, -1, 1))
            tmp[x, pl.ds(0, count, stride=2)] = 0.75 * middle + 0.25 * lower
            tmp[x, pl.ds(1, count, stride=2)] = 0.75 * middle + 0.25 * upper
        for x in range(nx) if cycle < CYCLES - 1 else [q * rows_of + xi for xi in range(rows_of) for q in range(pieces)]:
            i, odd = x // 2, x % 2
            middle = e_of[0](i)[taken]
            other = x_pair(lambda p: e_of[0](p)[taken], i, nx // 2, span)[odd]
            if x == 0:
                other = jnp.where(lanes >= span, other, 0.0)
            if x == nx - 1:
                other = jnp.where(lanes < LANES - span, other, 0.0)
            from_x = 0.75 * middle + 0.25 * other
            fold, xi = x // folds, x % folds
            mid_y = from_y[xi * keep:(xi + 1) * keep, LANES * fold:LANES * (fold + 1)]
            update = blending * ((from_x + mid_y) + tmp[x, 0:keep])
            ub[x, taken] = ub[x, taken] + update if cycle else update
            if cycle == CYCLES - 1 and x // rows_of == pieces - 1:
                give_back(x % rows_of)
        if cycle < CYCLES - 1:
            @pl.when(jnp.logical_not(has_prev))
            def _():
                ub[:, 0:near] = jnp.zeros((nx, near, LANES), jnp.float32)

            @pl.when(jnp.logical_not(has_next))
            def _():
                ub[:, slab + near:] = jnp.zeros((nx, near, LANES), jnp.float32)

    for xi in range(rows_of):
        for c in backs[xi]:
            c.wait_recv()
        for t in range(nz // LANES):
            parts = regroup([ro[t * pieces + q, xi] for q in range(pieces)])
            for q in range(pieces):
                x, at = q * rows_of + xi, slice(LANES * t, LANES * (t + 1))
                out_ref[x, :, at] = stage[4, x, :, at] + parts[q]
    for copies in list(every.values()) + backs:
        for c in copies:
            c.wait_send()
    for c, goes, _ in faces:
        @pl.when(goes)
        def _():
            c.wait_send()


def slab_fits(shape, counts):
    nx, ny, nz = shape
    cx, cy, _ = counts
    group = cx * cy
    if nz % group or ny * group != LANES or LANES % (2 * cx):
        return False
    slab = nz // group
    pieces = LANES // slab
    return (
        slab * pieces == LANES and pieces & (pieces - 1) == 0 and nx % (2 * pieces) == 0
        and slab % 16 == 0 and slab >= 2 * SWEEPS and nz % LANES == 0 and 2 * nx <= LANES)


def slab_body(names, counts, right_side, coefficients, first_guess):
    nx, ny, nz = right_side.shape
    f32 = jnp.float32
    vmem = lambda *shape: pltpu.VMEM(shape, f32)
    dma = pltpu.SemaphoreType.DMA
    group = counts[0] * counts[1]
    slab = nz // group
    rows_of = nx // (LANES // slab)
    near = SWEEPS
    wide = slab + 2 * near
    shapes = ((nx // 2, wide), (nx // 2, wide), (nx, slab // 2 + near))
    blocks = (group, rows_of, ny, LANES)
    scratch = [
        vmem(6, nx, ny, nz),
        vmem(5, *blocks),
        vmem(5, *blocks),
        vmem(4, nx, wide, LANES),
        vmem(nx, wide, LANES),
        vmem(nx, slab, LANES),
        vmem(nx, slab, LANES),
        vmem(7, nx, slab, LANES),
        tuple(vmem(4, x, z, LANES) for x, z in shapes),
        tuple(vmem(7, x, z, LANES) for x, z in shapes),
        tuple(vmem(CYCLES, x, z, LANES) for x, z in shapes),
        tuple(vmem(2, x * z + 16, LANES) for x, z in shapes),
        vmem(nx, wide, LANES),
        vmem(*blocks),
        vmem(*blocks),
        vmem(2, 2, ny, nz), vmem(2, 2, nx, 1, nz), vmem(2, 2, nx, 1, nz), vmem(2, ny, LANES),
        vmem(2, ny, LANES), vmem(CYCLES, *shapes[2], LANES),
        dma((6,)), dma((5, group)), dma((5, group)), dma((4, 2)), dma((4, 2)),
        dma((CYCLES, 3, 2)), dma((CYCLES, 3, 2)), dma((group, rows_of)), dma((group, rows_of)),
        dma((2, 3, 2)), dma((2, 3, 2)), dma((CYCLES, 2)), dma((CYCLES, 2)),
    ]
    hbm = pl.BlockSpec(memory_space=pl.ANY)
    return pl.pallas_call(
        functools.partial(slab_kernel, (nx, ny, nz), counts, names),
        out_shape=jax.ShapeDtypeStruct(right_side.shape, f32),
        in_specs=[hbm] * 3,
        out_specs=pl.BlockSpec(memory_space=pltpu.VMEM),
        scratch_shapes=scratch,
        compiler_params=pltpu.CompilerParams(
            collective_id=0, has_side_effects=True, vmem_limit_bytes=60 * 1024 * 1024),
    )(right_side, coefficients, first_guess)


def solution(mesh):
    names = tuple(mesh.axis_names)
    counts = tuple(mesh.shape[n] for n in names)
    in_specs = (P(*names), P(None, *names), P(*names))

    def local(right_side, coefficients, first_guess):
        if slab_fits(right_side.shape, counts):
            return slab_body(names, counts, right_side, coefficients, first_guess)
        return body(names, right_side, coefficients, first_guess)

    return jax.shard_map(
        local, mesh=mesh, in_specs=in_specs, out_specs=P(*names), check_vma=False)
```
